32 devices in a mesh: dp: 4 (over x, core), expert: 8 (over z, y).
Axes of the slice: x: 2, y: 2, z: 4, core: 2. Of those that a mesh axis runs over, the one named last changes fastest.
Arguments:
- hidden: bfloat16 [2048, 8, 1536], P(('dp', 'expert')), may hold values from -6 to 6
- routes: int32 [2048, 8], P(('dp', 'expert')), may hold values from 0 to 15, all different within a row; in each aligned block of 64 rows (0 to 63, 64 to 127, ...) at most 48 rows name the same one
- gate_scores: int32 [2048, 8], P(('dp', 'expert')), may hold values from 1 to 64
- down_weight: bfloat16 [16, 1536, 4096], P('expert', None, 'dp'), may hold values from -0.15625 to 0.15625
Outputs:
- output: bfloat16 [2048, 4096], P(('dp', 'expert'))
- gram: float32 [16, 1536, 1536], P('expert', 'dp')
The draws below stay inside these ranges and needn't reach their ends.
Inputs may be any that keep to these rules, and one draw needn't show every extreme that they name: `routes`: each token names 8 different experts. Among the 64 tokens of one device no expert is named more than 48 times, and on some devices one expert is named exactly 48 times. Every expert is named by some token.
All inputs are finite; a program needn't handle non-finite values.
Results may differ from the reference program's by a relative error of at most 0.005.
Values may be sent and summed in bfloat16 or wider, within the bound.
A program may use at most 128 MiB of HBM per device.

```python
import math
import jax
import jax.numpy as jnp
import numpy as np
from jax import lax

D = 4096
FF = 1536
TOPK = 8
TOK_DEV = 64
EXPERTS = 16
CAP = 48
TOKENS = 2048
N_DP = 4
N_EXPERT = 8


def touch_ends(entries, stream_key, low, largest):
    index_at = [jax.random.randint(jax.random.fold_in(stream_key, axis), (), 0, length) for axis, length in enumerate(entries.shape)]
    longest = entries.shape.index(max(entries.shape))
    next_to = index_at[:longest] + [(index_at[longest] + 1) % entries.shape[longest]] + index_at[longest + 1:]
    return entries.at[tuple(index_at)].set(low).at[tuple(next_to)].set(largest)


def level_of(rng, dims, cuts, low, largest):
    def one(dim, blocks):
        steps = jax.random.uniform(jax.random.fold_in(jax.random.fold_in(rng, 6), dim), (blocks,), jnp.float32, low / len(cuts), largest / len(cuts))
        return jnp.repeat(jnp.exp(steps), dims[dim] // blocks).reshape((-1,) + (1,) * (len(dims) - dim - 1))

    loudness = one(*cuts[0])
    for cut in cuts[1:]:
        loudness = loudness * one(*cut)
    return loudness


def shared_out(rng, own, number, rows, amount, top, reach, slope):
    ranking = jax.random.permutation(rng, amount)
    crowded, common = shares(amount, rows * top, reach, slope, True), shares(amount, rows * top, reach, slope, False)
    places = jnp.arange(amount)

    def named(tallies, rotation):
        used = int((tallies > 0).sum())
        fixed = max(1, used // 4)
        passed = fixed + (places - fixed + rotation * (used - fixed)) % max(1, amount - fixed)
        return jnp.zeros((amount,), jnp.int32).at[ranking[jnp.where(places < fixed, places, passed)]].set(jnp.asarray(tallies, jnp.int32))

    tallies = jnp.where(number % 4 == 0, named(crowded, number // 4), named(common, number - number // 4 - 1))
    mixed = jax.random.permutation(jax.random.fold_in(own, 3), amount)
    giver, receiver = mixed[0:amount // 2 * 2:2], mixed[1:amount // 2 * 2:2]
    room = jnp.minimum(tallies[giver] - 1, reach - tallies[receiver]) // 2
    room = jnp.where((giver == ranking[0]) | (receiver == ranking[0]) | (tallies[receiver] == 0), 0, jnp.maximum(room, 0))
    passed = jax.random.randint(jax.random.fold_in(own, 4), (amount // 2,), 0, 1 << 20) % (room + 1)
    tallies = tallies.at[giver].add(-passed).at[receiver].add(passed)
    members = jnp.searchsorted(jnp.cumsum(tallies), jnp.arange(rows * top), side="right").astype(jnp.int32)
    grid = members.reshape(top, rows).T
    grid = grid[jax.random.permutation(jax.random.fold_in(own, 1), rows)]
    rotation = jax.random.randint(jax.random.fold_in(own, 2), (rows, 1), 0, top)
    return jnp.take_along_axis(grid, (jnp.arange(top)[None, :] + rotation) % top, axis=1)


def shares(count, total, reach, slope, full):
    weights = [(1 << 20) // math.isqrt(standing ** slope) + 1 for standing in range(1, count + 1)]
    largest = reach if full else min(reach, max(-(-total // count), total * weights[0] // sum(weights)))
    least = 1 if total - largest >= count - 1 else 0
    given, rest = [largest] + [least] * (count - 1), total - largest - least * (count - 1)
    while rest > 0:
        movable = [i for i in range(1, count) if given[i] < largest] or [i for i in range(1, count) if given[i] < reach]
        pool, remaining = sum([weights[i] for i in movable]), rest
        for i in movable:
            addition = min(reach - given[i], max(1, remaining * weights[i] // pool), rest)
            given[i] = given[i] + addition
            rest = rest - addition
    return np.array(given)


def gaussian(stream_key, shape, deviation, limit, pieces=(), held_as=jnp.bfloat16):
    values = jax.random.normal(stream_key, shape, jnp.float32) * deviation
    if len(pieces) > 0:
        values = level_of(stream_key, shape, pieces, -0.22, 0.18) * values
    return jnp.clip(values, min=-limit, max=limit).astype(held_as)


def setup_inputs(seed: int = 0) -> dict:
    streams_of = jax.random.split(jax.random.key(seed), 5)
    hidden = gaussian(streams_of[0], (TOKENS, TOPK, FF), 1.0, 6.0, ((0, 32),))
    routes_keys = jax.random.split(jax.random.fold_in(streams_of[1], 1), TOKENS // TOK_DEV)
    routes_turns = jax.random.permutation(jax.random.fold_in(streams_of[1], 3), TOKENS // TOK_DEV)
    routes = jax.vmap(lambda own, number: shared_out(jax.random.fold_in(streams_of[1], 2), own, number, TOK_DEV, EXPERTS, TOPK, CAP, 2))(routes_keys, routes_turns).reshape((TOKENS, TOPK))
    gate_scores = touch_ends(jax.random.randint(streams_of[2], (TOKENS, TOPK), 1, 65), jax.random.fold_in(streams_of[2], 1), 1, 64).astype(jnp.int32)
    down_weight = gaussian(streams_of[3], (EXPERTS, FF, D), FF ** -0.5, 0.15625, ((0, 8), (2, 4)))
    return {"hidden": hidden, "routes": routes, "gate_scores": gate_scores, "down_weight": down_weight}


def reference(hidden, routes, gate_scores, down_weight):
    experts = down_weight.shape[0]
    model_width = down_weight.shape[2]
    tokens = hidden.shape[0]
    top_count = hidden.shape[1]
    hidden_width = hidden.shape[2]
    pair_total = tokens * top_count
    flat_routes = routes.reshape(pair_total).astype(jnp.int32)
    pair_rows = hidden.reshape(pair_total, hidden_width)
    sort_order = jnp.argsort(flat_routes, stable=True).astype(jnp.int32)
    counts = jnp.zeros((experts,), jnp.int32).at[flat_routes].add(1)
    starts = (jnp.cumsum(counts) - counts).astype(jnp.int32)
    span_rows = N_DP * N_EXPERT * CAP
    padded_rows = jnp.concatenate([pair_rows[sort_order], jnp.zeros((span_rows, hidden_width), pair_rows.dtype)], axis=0)
    owner_token = jnp.concatenate([(sort_order // top_count).astype(jnp.int32), jnp.full((span_rows,), tokens, jnp.int32)])
    scores = gate_scores.astype(jnp.float32)
    weight = scores / jnp.sum(scores, axis=1, keepdims=True)
    padded_weight = jnp.concatenate([weight.reshape(pair_total)[sort_order], jnp.zeros((span_rows,), jnp.float32)])

    def per_expert(accumulated, expert):
        first_row = starts[expert]
        segment = lax.dynamic_slice_in_dim(padded_rows, first_row, span_rows, 0)
        live_rows = jnp.arange(span_rows, dtype=jnp.int32) < counts[expert]
        segment = jnp.where(live_rows[:, None], segment, jnp.zeros_like(segment))
        gram_block = jnp.dot(segment.T, segment, preferred_element_type=jnp.float32) / counts[expert].astype(jnp.float32)
        contrib = jnp.dot(segment, down_weight[expert], preferred_element_type=jnp.float32).astype(jnp.bfloat16)
        pair_weights = lax.dynamic_slice_in_dim(padded_weight, first_row, span_rows, 0)
        target = lax.dynamic_slice_in_dim(owner_token, first_row, span_rows, 0)
        target = jnp.where(live_rows, target, tokens)
        accumulated = accumulated.at[target].add(contrib.astype(jnp.float32) * pair_weights[:, None], mode="drop")
        return accumulated, gram_block

    accumulated, grams = lax.scan(per_expert, jnp.zeros((tokens, model_width), jnp.float32), jnp.arange(experts, dtype=jnp.int32))
    return accumulated.astype(jnp.bfloat16), grams
```

```python
import functools

import jax
import jax.numpy as jnp
from jax import lax
from jax.experimental import pallas as pl
from jax.experimental.pallas import tpu as pltpu
from jax.sharding import PartitionSpec as P

MESH = pl.DeviceIdType.MESH
META = 128
TILE = 256
VMEM_BUDGET = 58 * 2**20
VMEM_LIMIT = 63 * 2**20


def fused_kernel(
    nd, ne, tokens, cap, width,
    og, w_hbm, o_ref, g_ref, c_ref,
    buf, w, sendy, recvy, keep, sendz, recvz, fin, osc, chi, clo,
    wsem, lsem, asend, xsend, csend, recv, ysend, yrecv, zsend, zrecv, osend, orecv,
):
    po = w.shape[0]
    nz = ne // 2
    nx = nd // 2
    rows = nd * cap
    group = nd * tokens
    cols = w.shape[2]
    d = lax.axis_index("dp")
    e = lax.axis_index("expert")
    x, c = lax.div(d, 2), lax.rem(d, 2)
    z, y = lax.div(e, 2), lax.rem(e, 2)
    other = d + 1 - 2 * c
    pair = e + 1 - 2 * y

    load_w = pltpu.make_async_copy(w_hbm, w, wsem)
    load_w.start()

    def slot_of(dd, ee):
        return buf.at[:, pl.ds(pl.multiple_of((ee * nd + dd) * cap, cap), cap), :]

    own = pltpu.make_async_copy(
        og.at[pl.ds(e * po, po)], slot_of(d, e), lsem
    )
    own.start()

    barrier = pltpu.get_barrier_semaphore()
    for k in range(1, ne):
        pl.semaphore_signal(
            barrier, inc=1, device_id=(d, lax.rem(e + k, ne)), device_id_type=MESH
        )
    for k in range(1, nd):
        pl.semaphore_signal(
            barrier, inc=1, device_id=(lax.rem(d + k, nd), e), device_id_type=MESH
        )
    pl.semaphore_wait(barrier, ne - 1 + nd - 1)

    def remote(src, dst, ss, rs, dd, ee):
        return pltpu.make_async_remote_copy(
            src_ref=src, dst_ref=dst, send_sem=ss, recv_sem=rs,
            device_id=(dd, ee), device_id_type=MESH,
        )

    def first(i):
        kz, ky = (i // 2 + 1) % nz, i % 2
        target = lax.rem(z + kz, nz) * 2 + lax.rem(y + ky, 2)
        return remote(
            og.at[pl.ds(target * po, po)], slot_of(d, e), asend.at[i],
            recv.at[e * nd + d], d, target,
        )

    for i in range(ne):
        if i != ne - 2:
            first(i).start()
    own.wait()
    c_ref[...] = jnp.zeros_like(c_ref)

    def source_of(i):
        kz = lax.rem(lax.div(i, 2) + 1, nz)
        zi = lax.rem(z - kz + nz, nz)
        return zi, zi * 2 + lax.rem(y + lax.rem(i, 2), 2)

    def arrived(dd, ee):
        here = slot_of(dd, ee)
        remote(here, here, asend.at[0], recv.at[ee * nd + dd], d, e).wait_recv()

    def to_x(i, j, ee):
        here = slot_of(d, ee)
        return remote(
            here, here, xsend.at[i, j], recv.at[ee * nd + d],
            lax.rem(x + j + 1, nx) * 2 + c, e,
        )

    def to_core(i, j, ee):
        dd = lax.rem(x + j, nx) * 2 + c
        here = slot_of(dd, ee)
        return remote(here, here, csend.at[i, j], recv.at[ee * nd + dd], other, e)

    def to_pair(zi):
        return remote(sendy.at[zi], recvy.at[zi], ysend.at[zi], yrecv.at[zi], d, pair)

    def to_line(zi):
        return remote(
            sendz.at[zi], recvz.at[z], zsend.at[zi], zrecv.at[z], d, zi * 2 + y
        )

    def from_pair(zi):
        remote(sendy.at[zi], recvy.at[zi], ysend.at[zi], yrecv.at[zi], d, e).wait_recv()

    def work(i):
        zi, ee = source_of(i)
        mine = lax.rem(i, 2) == 0
        span = pl.ds(pl.multiple_of(ee * rows, rows), rows)
        row = lax.broadcasted_iota(jnp.int32, (rows, 1), 0)
        base = jnp.zeros((rows, 1), jnp.int32)
        for k in range(1, nd):
            base = base + jnp.where(row >= k * cap, tokens, 0)
        col = lax.broadcasted_iota(jnp.int32, (rows, group), 1)
        for q in range(po):
            meta = buf[q, span, width:width + META].astype(jnp.float32)
            hit = col == meta[:, 0:1].astype(jnp.int32) + base
            chi[q] = jnp.where(hit, meta[:, 1:2], 0.0).astype(jnp.bfloat16)
            clo[q] = jnp.where(hit, meta[:, 2:3], 0.0).astype(jnp.bfloat16)
            c_ref[q] = c_ref[q] + jnp.sum(meta[:, 3:4], axis=0, keepdims=True)

        @pl.loop(0, cols // TILE)
        def _(t):
            cs = pl.ds(pl.multiple_of(t * TILE, TILE), TILE)
            acc = jnp.zeros((group, TILE), jnp.float32)
            for q in range(po):
                h = jnp.dot(
                    buf[q, span, 0:width], w[q, :, cs], preferred_element_type=jnp.float32
                ).astype(jnp.bfloat16)
                for part in (chi, clo):
                    acc = acc + lax.dot_general(
                        part[q], h, (((0,), (0,)), ((), ())),
                        preferred_element_type=jnp.float32,
                    )

            @pl.when(mine)
            def _():
                keep[zi, :, cs] = acc

            @pl.when(jnp.logical_not(mine))
            def _():
                sendy[zi, :, cs] = acc.astype(jnp.bfloat16)

        @pl.when(jnp.logical_not(mine))
        def _():
            to_pair(zi).start()

            @pl.when(i >= 3)
            def _():
                zp, _ = source_of(i - 2)
                from_pair(zp)
                sendz[zp] = (keep[zp] + recvy[zp].astype(jnp.float32)).astype(jnp.bfloat16)
                to_line(zp).start()

    load_w.wait()

    def step(i, carry):
        @pl.when(i < ne)
        def _():
            _, ee = source_of(i)

            @pl.when(i != ne - 2)
            def _():
                arrived(d, ee)

            for j in range(nx - 1):
                to_x(i, j, ee).start()
            to_core(i, 0, ee).start()

        @pl.when(jnp.logical_and(i >= 1, i < ne + 1))
        def _():
            _, ee = source_of(i - 1)
            for j in range(1, nx):
                arrived(lax.rem(x + j, nx) * 2 + c, ee)
                to_core(i - 1, j, ee).start()

        @pl.when(i >= 2)
        def _():
            _, ee = source_of(i - 2)
            for j in range(nx):
                arrived(lax.rem(x + j, nx) * 2 + 1 - c, ee)
            work(i - 2)

        return carry

    lax.fori_loop(0, ne + 2, step, 0)

    block = g_ref.shape[1]
    for q in range(po):
        @pl.loop(0, width // TILE)
        def _(t):
            cs = pl.ds(pl.multiple_of(t * TILE, TILE), TILE)
            g_ref[q, :, cs] = lax.dot_general(
                buf[q, :, pl.ds(pl.multiple_of(d * block, block), block)],
                buf[q, :, cs],
                (((0,), (0,)), ((), ())),
                preferred_element_type=jnp.float32,
            )

    from_pair(z)
    for k in range(1, nz):
        zk = lax.rem(z + k, nz)
        remote(sendz.at[zk], recvz.at[zk], zsend.at[zk], zrecv.at[zk], d, e).wait_recv()

    @pl.loop(0, nd)
    def _(k):
        rs = pl.ds(pl.multiple_of(k * tokens, tokens), tokens)
        total = keep[z, rs, :] + recvy[z, rs, :].astype(jnp.float32)
        for j in range(1, nz):
            total = total + recvz[lax.rem(z + j, nz), rs, :].astype(jnp.float32)
        fin[k] = total.astype(jnp.bfloat16)

    def to_token(k):
        dd = lax.rem(d + k, nd)
        return remote(fin.at[dd], osc.at[d], osend.at[k], orecv.at[d], dd, e)

    for k in range(1, nd):
        to_token(k).start()
    o_ref[:, pl.ds(pl.multiple_of(d * cols, cols), cols)] = fin[d]
    for k in range(1, nd):
        dd = lax.rem(d + k, nd)
        remote(fin.at[dd], osc.at[dd], osend.at[k], orecv.at[dd], d, e).wait_recv()
        o_ref[:, pl.ds(pl.multiple_of(dd * cols, cols), cols)] = osc[dd]

    for i in range(ne):
        if i != ne - 2:
            first(i).wait_send()

    def drain(i, carry):
        _, ee = source_of(i)
        for j in range(nx - 1):
            to_x(i, j, ee).wait_send()
        for j in range(nx):
            to_core(i, j, ee).wait_send()
        return carry

    lax.fori_loop(0, ne, drain, 0)
    for k in range(nz):
        to_pair(k).wait_send()
    for k in range(1, nz):
        to_line(lax.rem(z + k, nz)).wait_send()
    for k in range(1, nd):
        to_token(k).wait_send()


def earlier(onehot):
    pairs = jnp.arange(onehot.shape[0], dtype=jnp.int32)
    above = (pairs[None, :] < pairs[:, None]).astype(jnp.bfloat16)
    return jnp.dot(
        above, onehot.astype(jnp.bfloat16), preferred_element_type=jnp.float32
    ).astype(jnp.int32)


def positions(routes, experts):
    flat_routes = routes.reshape(-1)
    onehot = (flat_routes[:, None] == jnp.arange(experts, dtype=jnp.int32)[None, :]).astype(
        jnp.int32
    )
    before = earlier(onehot)
    return flat_routes, onehot, jnp.sum(before * onehot, axis=1)


def fused(hidden, routes, gate_scores, down_weight):
    tokens, top_count, width = hidden.shape
    ne, nd = lax.axis_size("expert"), lax.axis_size("dp")
    po, _, cols = down_weight.shape
    experts = ne * po
    pairs = tokens * top_count
    cap = 3 * pairs // (2 * experts)
    flat_routes, _, position = positions(routes, experts)
    slot_index = flat_routes * cap + position
    scores = gate_scores.astype(jnp.float32)
    weight = (scores / jnp.sum(scores, axis=1, keepdims=True)).reshape(pairs)
    hi = weight.astype(jnp.bfloat16)
    lo = (weight - hi.astype(jnp.float32)).astype(jnp.bfloat16)
    token = (jnp.arange(pairs, dtype=jnp.int32) // top_count).astype(jnp.bfloat16)
    meta = jnp.stack([token, hi, lo, jnp.ones_like(hi)], axis=1)
    meta = jnp.pad(meta, ((0, 0), (0, META - 4)))
    pick = (
        jnp.arange(experts * cap, dtype=jnp.int32)[:, None] == slot_index[None, :]
    ).astype(jnp.bfloat16)
    packed = jnp.concatenate([hidden.reshape(pairs, width), meta], axis=1)
    outgoing = jnp.dot(pick, packed, preferred_element_type=jnp.float32).astype(jnp.bfloat16)
    outgoing = outgoing.reshape(experts, cap, width + META)

    nz, nx, group = ne // 2, nd // 2, nd * tokens
    bf, f32 = jnp.bfloat16, jnp.float32
    dma = pltpu.SemaphoreType.DMA
    any_space = pl.BlockSpec(memory_space=pl.ANY)
    vmem = pl.BlockSpec(memory_space=pltpu.VMEM)
    out, gram, count = pl.pallas_call(
        functools.partial(fused_kernel, nd, ne, tokens, cap, width),
        out_shape=(
            jax.ShapeDtypeStruct((tokens, nd * cols), bf),
            jax.ShapeDtypeStruct((po, width // nd, width), f32),
            jax.ShapeDtypeStruct((po, 8, 128), f32),
        ),
        in_specs=[vmem, any_space],
        out_specs=(vmem, vmem, vmem),
        scratch_shapes=[
            pltpu.VMEM((po, ne * nd * cap, width + META), bf),
            pltpu.VMEM((po, width, cols), bf),
            pltpu.VMEM((nz, group, cols), bf),
            pltpu.VMEM((nz, group, cols), bf),
            pltpu.VMEM((nz, group, cols), f32),
            pltpu.VMEM((nz, group, cols), bf),
            pltpu.VMEM((nz, group, cols), bf),
            pltpu.VMEM((nd, tokens, cols), bf),
            pltpu.VMEM((nd, tokens, cols), bf),
            pltpu.VMEM((po, nd * cap, group), bf),
            pltpu.VMEM((po, nd * cap, group), bf),
            dma, dma,
            dma((ne,)), dma((ne, max(nx - 1, 1))), dma((ne, nx)), dma((ne * nd,)),
            dma((nz,)), dma((nz,)), dma((nz,)), dma((nz,)), dma((nd,)), dma((nd,)),
        ],
        compiler_params=pltpu.CompilerParams(
            collective_id=0, has_side_effects=True, vmem_limit_bytes=VMEM_LIMIT
        ),
    )(outgoing, down_weight)
    return out, gram / count[:, :1, :1]


def plain(hidden, routes, gate_scores, down_weight):
    tokens = hidden.shape[0]
    top_count = hidden.shape[1]
    hidden_width = hidden.shape[2]
    n_owner = lax.axis_size("expert")
    n_group = lax.axis_size("dp")
    per_owner = down_weight.shape[0]
    experts = n_owner * per_owner
    pair_total = tokens * top_count
    capacity = 3 * tokens * top_count // (2 * experts)
    flat_routes = routes.reshape(pair_total)
    onehot = (flat_routes[:, None] == jnp.arange(experts, dtype=jnp.int32)[None, :]).astype(
        jnp.int32
    )
    before = earlier(onehot)
    position = jnp.sum(before * onehot, axis=1)
    slot_index = flat_routes * capacity + position
    local_counts = jnp.sum(onehot, axis=0).astype(jnp.float32)
    totals = lax.psum(local_counts, ("dp", "expert"))
    pair_rows = hidden.reshape(pair_total, hidden_width)
    outgoing = (
        jnp.zeros((experts * capacity, hidden_width), jnp.bfloat16).at[slot_index].set(pair_rows)
    )
    outgoing = outgoing.reshape(n_owner, per_owner, capacity, hidden_width)
    arrived = lax.all_to_all(outgoing, "expert", split_axis=0, concat_axis=0, tiled=True)
    everyone = lax.all_gather(arrived, "dp", axis=0, tiled=True)
    own_counts = lax.dynamic_slice_in_dim(
        totals, lax.axis_index("expert") * per_owner, per_owner, 0
    )
    block_width = hidden_width // n_group
    my_columns = lax.dynamic_slice_in_dim(
        everyone, lax.axis_index("dp") * block_width, block_width, 3
    )
    gram_rows = jnp.einsum(
        "sxcf,sxcg->xfg", my_columns, everyone, preferred_element_type=jnp.float32
    )
    results = jnp.einsum(
        "sxcf,xfd->sxcd", everyone, down_weight, preferred_element_type=jnp.float32
    ).astype(jnp.bfloat16)
    returned = lax.all_to_all(
        lax.all_to_all(results, "dp", split_axis=0, concat_axis=3, tiled=True),
        "expert",
        split_axis=0,
        concat_axis=0,
        tiled=True,
    )
    gram = gram_rows / own_counts[:, None, None]
    model_width = returned.shape[3]
    pair_results = returned.reshape(experts * capacity, model_width)[slot_index]
    scores = gate_scores.astype(jnp.float32)
    weight = scores / jnp.sum(scores, axis=1, keepdims=True)
    combined = jnp.sum(
        pair_results.reshape(tokens, top_count, model_width).astype(jnp.float32)
        * weight[:, :, None],
        axis=1,
    )
    return (combined.astype(jnp.bfloat16), gram)


def fits(hidden, down_weight, nd, ne):
    tokens, top_count, width = hidden.shape
    po, _, cols = down_weight.shape
    cap = 3 * tokens * top_count // (2 * ne * po)
    group = nd * tokens
    if cap % 16 or tokens % 16 or nd % 2 or ne % 2 or ne < 4 or tokens > 256:
        return False
    if width % TILE or cols % TILE or (width // nd) % 128:
        return False
    need = (
        2 * po * ne * cap * (nd + 1) * (width + META)
        + 2 * po * width * cols
        + (ne // 2) * group * cols * 12
        + 4 * po * (width // nd) * width
        + 6 * group * cols
        + 4 * po * nd * cap * group
    )
    return need <= VMEM_BUDGET


def local(hidden, routes, gate_scores, down_weight):
    if fits(hidden, down_weight, lax.axis_size("dp"), lax.axis_size("expert")):
        return fused(hidden, routes, gate_scores, down_weight)
    return plain(hidden, routes, gate_scores, down_weight)


def solution(mesh):
    placed = (
        P(("dp", "expert"), None, None),
        P(("dp", "expert"), None),
        P(("dp", "expert"), None),
        P("expert", None, "dp"),
    )
    return jax.shard_map(
        local,
        mesh=mesh,
        in_specs=placed,
        out_specs=(P(("dp", "expert"), None), P("expert", "dp", None)),
        check_vma=False,
    )
```

```python
import functools

import jax
import jax.numpy as jnp
from jax import lax
from jax.experimental import pallas as pl
from jax.experimental.pallas import tpu as pltpu
from jax.sharding import PartitionSpec as P

MESH = pl.DeviceIdType.MESH
META = 128
TILE = 256
VMEM_BUDGET = 58 * 2**20
VMEM_LIMIT = 63 * 2**20


def fused_kernel(
    nd, ne, tokens, cap, width,
    og, w_hbm, o_ref, g_ref, c_ref,
    buf, w, sendy, recvy, keep, sendz, recvz, fin, osc, chi, clo,
    wsem, lsem, asend, xsend, csend, recv, ysend, yrecv, zsend, zrecv, osend, orecv,
):
    po = w.shape[0]
    nz = ne // 2
    nx = nd // 2
    rows = nd * cap
    group = nd * tokens
    cols = w.shape[2]
    d = lax.axis_index("dp")
    e = lax.axis_index("expert")
    x, c = lax.div(d, 2), lax.rem(d, 2)
    z, y = lax.div(e, 2), lax.rem(e, 2)
    other = d + 1 - 2 * c
    pair = e + 1 - 2 * y

    load_w = pltpu.make_async_copy(w_hbm, w, wsem)
    load_w.start()

    def slot_of(dd, ee):
        return buf.at[:, pl.ds(pl.multiple_of((ee * nd + dd) * cap, cap), cap), :]

    own = pltpu.make_async_copy(
        og.at[pl.ds(e * po, po)], slot_of(d, e), lsem
    )
    own.start()

    barrier = pltpu.get_barrier_semaphore()
    for k in range(1, ne):
        pl.semaphore_signal(
            barrier, inc=1, device_id=(d, lax.rem(e + k, ne)), device_id_type=MESH
        )
    for k in range(1, nd):
        pl.semaphore_signal(
            barrier, inc=1, device_id=(lax.rem(d + k, nd), e), device_id_type=MESH
        )
    pl.semaphore_wait(barrier, ne - 1 + nd - 1)

    def remote(src, dst, ss, rs, dd, ee):
        return pltpu.make_async_remote_copy(
            src_ref=src, dst_ref=dst, send_sem=ss, recv_sem=rs,
            device_id=(dd, ee), device_id_type=MESH,
        )

    def first(i):
        kz, ky = (i // 2 + 1) % nz, i % 2
        target = lax.rem(z + kz, nz) * 2 + lax.rem(y + ky, 2)
        return remote(
            og.at[pl.ds(target * po, po)], slot_of(d, e), asend.at[i],
            recv.at[e * nd + d], d, target,
        )

    for i in range(ne):
        if i != ne - 2:
            first(i).start()
    own.wait()
    c_ref[...] = jnp.zeros_like(c_ref)

    def source_of(i):
        kz = lax.rem(lax.div(i, 2) + 1, nz)
        zi = lax.rem(z - kz + nz, nz)
        return zi, zi * 2 + lax.rem(y + lax.rem(i, 2), 2)

    def arrived(dd, ee):
        here = slot_of(dd, ee)
        remote(here, here, asend.at[0], recv.at[ee * nd + dd], d, e).wait_recv()

    def to_x(i, j, ee):
        here = slot_of(d, ee)
        return remote(
            here, here, xsend.at[i, j], recv.at[ee * nd + d],
            lax.rem(x + j + 1, nx) * 2 + c, e,
        )

    def to_core(i, j, ee):
        dd = lax.rem(x + j, nx) * 2 + c
        here = slot_of(dd, ee)
        return remote(here, here, csend.at[i, j], recv.at[ee * nd + dd], other, e)

    def to_pair(zi):
        return remote(sendy.at[zi], recvy.at[zi], ysend.at[zi], yrecv.at[zi], d, pair)

    def to_line(zi):
        return remote(
            sendz.at[zi], recvz.at[z], zsend.at[zi], zrecv.at[z], d, zi * 2 + y
        )

    def from_pair(zi):
        remote(sendy.at[zi], recvy.at[zi], ysend.at[zi], yrecv.at[zi], d, e).wait_recv()

    def work(i):
        zi, ee = source_of(i)
        mine = lax.rem(i, 2) == 0
        span = pl.ds(pl.multiple_of(ee * rows, rows), rows)
        row = lax.broadcasted_iota(jnp.int32, (rows, 1), 0)
        base = jnp.zeros((rows, 1), jnp.int32)
        for k in range(1, nd):
            base = base + jnp.where(row >= k * cap, tokens, 0)
        col = lax.broadcasted_iota(jnp.int32, (rows, group), 1)
        for q in range(po):
            meta = buf[q, span, width:width + META].astype(jnp.float32)
            hit = col == meta[:, 0:1].astype(jnp.int32) + base
            chi[q] = jnp.where(hit, meta[:, 1:2], 0.0).astype(jnp.bfloat16)
            clo[q] = jnp.where(hit, meta[:, 2:3], 0.0).astype(jnp.bfloat16)
            c_ref[q] = c_ref[q] + jnp.sum(meta[:, 3:4], axis=0, keepdims=True)

        acc = jnp.zeros((group, cols), jnp.float32)
        for q in range(po):
            h = jnp.dot(
                buf[q, span, 0:width], w[q], preferred_element_type=jnp.float32
            ).astype(jnp.bfloat16)
            for part in (chi, clo):
                acc = acc + lax.dot_general(
                    part[q], h, (((0,), (0,)), ((), ())),
                    preferred_element_type=jnp.float32,
                )

        @pl.when(mine)
        def _():
            keep[zi] = acc

        @pl.when(jnp.logical_not(mine))
        def _():
            sendy[zi] = acc.astype(jnp.bfloat16)

        @pl.when(jnp.logical_not(mine))
        def _():
            to_pair(zi).start()

            @pl.when(i >= 3)
            def _():
                zp, _ = source_of(i - 2)
                from_pair(zp)
                sendz[zp] = (keep[zp] + recvy[zp].astype(jnp.float32)).astype(jnp.bfloat16)
                to_line(zp).start()

    load_w.wait()

    def step(i, carry):
        @pl.when(i < ne)
        def _():
            _, ee = source_of(i)

            @pl.when(i != ne - 2)
            def _():
                arrived(d, ee)

            for j in range(nx - 1):
                to_x(i, j, ee).start()
            to_core(i, 0, ee).start()

        @pl.when(jnp.logical_and(i >= 1, i < ne + 1))
        def _():
            _, ee = source_of(i - 1)
            for j in range(1, nx):
                arrived(lax.rem(x + j, nx) * 2 + c, ee)
                to_core(i - 1, j, ee).start()

        @pl.when(i >= 2)
        def _():
            _, ee = source_of(i - 2)
            for j in range(nx):
                arrived(lax.rem(x + j, nx) * 2 + 1 - c, ee)
            work(i - 2)

        return carry

    lax.fori_loop(0, ne + 2, step, 0)

    block = g_ref.shape[1]
    wide = width // 2 if width % (2 * TILE) == 0 else TILE
    for q in range(po):
        @pl.loop(0, width // wide)
        def _(t):
            cs = pl.ds(pl.multiple_of(t * wide, wide), wide)
            g_ref[q, :, cs] = lax.dot_general(
                buf[q, :, pl.ds(pl.multiple_of(d * block, block), block)],
                buf[q, :, cs],
                (((0,), (0,)), ((), ())),
                preferred_element_type=jnp.float32,
            )

    from_pair(z)
    for k in range(1, nz):
        zk = lax.rem(z + k, nz)
        remote(sendz.at[zk], recvz.at[zk], zsend.at[zk], zrecv.at[zk], d, e).wait_recv()

    @pl.loop(0, nd)
    def _(k):
        rs = pl.ds(pl.multiple_of(k * tokens, tokens), tokens)
        total = keep[z, rs, :] + recvy[z, rs, :].astype(jnp.float32)
        for j in range(1, nz):
            total = total + recvz[lax.rem(z + j, nz), rs, :].astype(jnp.float32)
        fin[k] = total.astype(jnp.bfloat16)

    def to_token(k):
        dd = lax.rem(d + k, nd)
        return remote(fin.at[dd], osc.at[d], osend.at[k], orecv.at[d], dd, e)

    for k in range(1, nd):
        to_token(k).start()
    o_ref[:, pl.ds(pl.multiple_of(d * cols, cols), cols)] = fin[d]
    for k in range(1, nd):
        dd = lax.rem(d + k, nd)
        remote(fin.at[dd], osc.at[dd], osend.at[k], orecv.at[dd], d, e).wait_recv()
        o_ref[:, pl.ds(pl.multiple_of(dd * cols, cols), cols)] = osc[dd]

    for i in range(ne):
        if i != ne - 2:
            first(i).wait_send()

    def drain(i, carry):
        _, ee = source_of(i)
        for j in range(nx - 1):
            to_x(i, j, ee).wait_send()
        for j in range(nx):
            to_core(i, j, ee).wait_send()
        return carry

    lax.fori_loop(0, ne, drain, 0)
    for k in range(nz):
        to_pair(k).wait_send()
    for k in range(1, nz):
        to_line(lax.rem(z + k, nz)).wait_send()
    for k in range(1, nd):
        to_token(k).wait_send()


def earlier(onehot):
    pairs = jnp.arange(onehot.shape[0], dtype=jnp.int32)
    above = (pairs[None, :] < pairs[:, None]).astype(jnp.bfloat16)
    return jnp.dot(
        above, onehot.astype(jnp.bfloat16), preferred_element_type=jnp.float32
    ).astype(jnp.int32)


def positions(routes, experts):
    flat_routes = routes.reshape(-1)
    onehot = (flat_routes[:, None] == jnp.arange(experts, dtype=jnp.int32)[None, :]).astype(
        jnp.int32
    )
    before = earlier(onehot)
    return flat_routes, onehot, jnp.sum(before * onehot, axis=1)


def fused(hidden, routes, gate_scores, down_weight):
    tokens, top_count, width = hidden.shape
    ne, nd = lax.axis_size("expert"), lax.axis_size("dp")
    po, _, cols = down_weight.shape
    experts = ne * po
    pairs = tokens * top_count
    cap = 3 * pairs // (2 * experts)
    flat_routes, _, position = positions(routes, experts)
    slot_index = flat_routes * cap + position
    scores = gate_scores.astype(jnp.float32)
    weight = (scores / jnp.sum(scores, axis=1, keepdims=True)).reshape(pairs)
    hi = weight.astype(jnp.bfloat16)
    lo = (weight - hi.astype(jnp.float32)).astype(jnp.bfloat16)
    token = (jnp.arange(pairs, dtype=jnp.int32) // top_count).astype(jnp.bfloat16)
    meta = jnp.stack([token, hi, lo, jnp.ones_like(hi)], axis=1)
    meta = jnp.pad(meta, ((0, 0), (0, META - 4)))
    pick = (
        jnp.arange(experts * cap, dtype=jnp.int32)[:, None] == slot_index[None, :]
    ).astype(jnp.bfloat16)
    packed = jnp.concatenate([hidden.reshape(pairs, width), meta], axis=1)
    outgoing = jnp.dot(pick, packed, preferred_element_type=jnp.float32).astype(jnp.bfloat16)
    outgoing = outgoing.reshape(experts, cap, width + META)

    nz, nx, group = ne // 2, nd // 2, nd * tokens
    bf, f32 = jnp.bfloat16, jnp.float32
    dma = pltpu.SemaphoreType.DMA
    any_space = pl.BlockSpec(memory_space=pl.ANY)
    vmem = pl.BlockSpec(memory_space=pltpu.VMEM)
    out, gram, count = pl.pallas_call(
        functools.partial(fused_kernel, nd, ne, tokens, cap, width),
        out_shape=(
            jax.ShapeDtypeStruct((tokens, nd * cols), bf),
            jax.ShapeDtypeStruct((po, width // nd, width), f32),
            jax.ShapeDtypeStruct((po, 8, 128), f32),
        ),
        in_specs=[vmem, any_space],
        out_specs=(vmem, vmem, vmem),
        scratch_shapes=[
            pltpu.VMEM((po, ne * nd * cap, width + META), bf),
            pltpu.VMEM((po, width, cols), bf),
            pltpu.VMEM((nz, group, cols), bf),
            pltpu.VMEM((nz, group, cols), bf),
            pltpu.VMEM((nz, group, cols), f32),
            pltpu.VMEM((nz, group, cols), bf),
            pltpu.VMEM((nz, group, cols), bf),
            pltpu.VMEM((nd, tokens, cols), bf),
            pltpu.VMEM((nd, tokens, cols), bf),
            pltpu.VMEM((po, nd * cap, group), bf),
            pltpu.VMEM((po, nd * cap, group), bf),
            dma, dma,
            dma((ne,)), dma((ne, max(nx - 1, 1))), dma((ne, nx)), dma((ne * nd,)),
            dma((nz,)), dma((nz,)), dma((nz,)), dma((nz,)), dma((nd,)), dma((nd,)),
        ],
        compiler_params=pltpu.CompilerParams(
            collective_id=0, has_side_effects=True, vmem_limit_bytes=VMEM_LIMIT
        ),
    )(outgoing, down_weight)
    return out, gram / count[:, :1, :1]


def plain(hidden, routes, gate_scores, down_weight):
    tokens = hidden.shape[0]
    top_count = hidden.shape[1]
    hidden_width = hidden.shape[2]
    n_owner = lax.axis_size("expert")
    n_group = lax.axis_size("dp")
    per_owner = down_weight.shape[0]
    experts = n_owner * per_owner
    pair_total = tokens * top_count
    capacity = 3 * tokens * top_count // (2 * experts)
    flat_routes = routes.reshape(pair_total)
    onehot = (flat_routes[:, None] == jnp.arange(experts, dtype=jnp.int32)[None, :]).astype(
        jnp.int32
    )
    before = earlier(onehot)
    position = jnp.sum(before * onehot, axis=1)
    slot_index = flat_routes * capacity + position
    local_counts = jnp.sum(onehot, axis=0).astype(jnp.float32)
    totals = lax.psum(local_counts, ("dp", "expert"))
    pair_rows = hidden.reshape(pair_total, hidden_width)
    outgoing = (
        jnp.zeros((experts * capacity, hidden_width), jnp.bfloat16).at[slot_index].set(pair_rows)
    )
    outgoing = outgoing.reshape(n_owner, per_owner, capacity, hidden_width)
    arrived = lax.all_to_all(outgoing, "expert", split_axis=0, concat_axis=0, tiled=True)
    everyone = lax.all_gather(arrived, "dp", axis=0, tiled=True)
    own_counts = lax.dynamic_slice_in_dim(
        totals, lax.axis_index("expert") * per_owner, per_owner, 0
    )
    block_width = hidden_width // n_group
    my_columns = lax.dynamic_slice_in_dim(
        everyone, lax.axis_index("dp") * block_width, block_width, 3
    )
    gram_rows = jnp.einsum(
        "sxcf,sxcg->xfg", my_columns, everyone, preferred_element_type=jnp.float32
    )
    results = jnp.einsum(
        "sxcf,xfd->sxcd", everyone, down_weight, preferred_element_type=jnp.float32
    ).astype(jnp.bfloat16)
    returned = lax.all_to_all(
        lax.all_to_all(results, "dp", split_axis=0, concat_axis=3, tiled=True),
        "expert",
        split_axis=0,
        concat_axis=0,
        tiled=True,
    )
    gram = gram_rows / own_counts[:, None, None]
    model_width = returned.shape[3]
    pair_results = returned.reshape(experts * capacity, model_width)[slot_index]
    scores = gate_scores.astype(jnp.float32)
    weight = scores / jnp.sum(scores, axis=1, keepdims=True)
    combined = jnp.sum(
        pair_results.reshape(tokens, top_count, model_width).astype(jnp.float32)
        * weight[:, :, None],
        axis=1,
    )
    return (combined.astype(jnp.bfloat16), gram)


def fits(hidden, down_weight, nd, ne):
    tokens, top_count, width = hidden.shape
    po, _, cols = down_weight.shape
    cap = 3 * tokens * top_count // (2 * ne * po)
    group = nd * tokens
    if cap % 16 or tokens % 16 or nd % 2 or ne % 2 or ne < 4 or tokens > 256:
        return False
    if width % TILE or cols % TILE or (width // nd) % 128:
        return False
    need = (
        2 * po * ne * cap * (nd + 1) * (width + META)
        + 2 * po * width * cols
        + (ne // 2) * group * cols * 12
        + 4 * po * (width // nd) * width
        + 6 * group * cols
        + 4 * po * nd * cap * group
    )
    return need <= VMEM_BUDGET


def local(hidden, routes, gate_scores, down_weight):
    if fits(hidden, down_weight, lax.axis_size("dp"), lax.axis_size("expert")):
        return fused(hidden, routes, gate_scores, down_weight)
    return plain(hidden, routes, gate_scores, down_weight)


def solution(mesh):
    placed = (
        P(("dp", "expert"), None, None),
        P(("dp", "expert"), None),
        P(("dp", "expert"), None),
        P("expert", None, "dp"),
    )
    return jax.shard_map(
        local,
        mesh=mesh,
        in_specs=placed,
        out_specs=(P(("dp", "expert"), None), P("expert", "dp", None)),
        check_vma=False,
    )
```

```python
import functools

import jax
import jax.numpy as jnp
from jax import lax
from jax.experimental import pallas as pl
from jax.experimental.pallas import tpu as pltpu
from jax.sharding import PartitionSpec as P

MESH = pl.DeviceIdType.MESH
META = 128
PIECES = 4
VMEM_BUDGET = 58 * 2**20
VMEM_LIMIT = 63 * 2**20


def fused_kernel(
    nd, ne, top, cap, np_,
    hid, rt, gt, w_hbm, o_ref, g_hbm, c_ref,
    buf, mbuf, og, mog, slot, meta, w, sendy, recvy, keep, sendz, recvz, fin, g,
    wsem, gsem, lsem, mlsem, asend, msend, xsend, mxsend, csend, mcsend, recv, mrecv,
    ysend, yrecv, zsend, zrecv, osend, orecv,
):
    f32, bf = jnp.float32, jnp.bfloat16
    po, width, cols = w.shape
    pairs = hid.shape[0]
    tokens = pairs // top
    nz = ne // 2
    rows = nd * cap
    chunk = po * cap
    group = nd * tokens
    pc = cols // np_
    experts = ne * po
    d = lax.axis_index("dp")
    e = lax.axis_index("expert")
    x, c = lax.div(d, 2), lax.rem(d, 2)
    z, y = lax.div(e, 2), lax.rem(e, 2)
    other = d + 1 - 2 * c
    across = lax.rem(d + 2, nd)
    pair = e + 1 - 2 * y
    inner = jnp.logical_and(z > 0, z < nz - 1)
    outer = jnp.logical_not(inner)

    load_w = pltpu.make_async_copy(w_hbm, w, wsem)
    load_w.start()

    barrier = pltpu.get_barrier_semaphore()
    for k in range(1, ne):
        pl.semaphore_signal(
            barrier, inc=1, device_id=(d, lax.rem(e + k, ne)), device_id_type=MESH
        )
    for k in range(1, nd):
        pl.semaphore_signal(
            barrier, inc=1, device_id=(lax.rem(d + k, nd), e), device_id_type=MESH
        )

    def remote(src, dst, ss, rs, dd, ee):
        return pltpu.make_async_remote_copy(
            src_ref=src, dst_ref=dst, send_sem=ss, recv_sem=rs,
            device_id=(dd, ee), device_id_type=MESH,
        )

    def slot_of(dd, ee):
        return buf.at[:, pl.ds(pl.multiple_of((ee * nd + dd) * cap, cap), cap), :]

    def meta_of(dd, ee):
        return mbuf.at[ee * nd + dd]

    shift = top.bit_length() - 1
    route = rt[...]
    set_ = jnp.where(
        lax.broadcasted_iota(jnp.int32, (experts, pairs), 0) == route, 1.0, 0.0
    )
    down = lax.broadcasted_iota(jnp.int32, (pairs, pairs), 0)
    along = lax.broadcasted_iota(jnp.int32, (pairs, pairs), 1)
    before = jnp.dot(
        set_.astype(bf), jnp.where(down < along, 1.0, 0.0).astype(bf),
        preferred_element_type=f32,
    )
    position = jnp.sum(before * set_, axis=0, keepdims=True).astype(jnp.int32)
    slot[...] = jnp.broadcast_to(route * cap + position, slot.shape)
    together = jnp.right_shift(down, shift) == jnp.right_shift(along, shift)
    score = jnp.broadcast_to(gt[...].astype(f32), (16, pairs))
    weight = score / jnp.dot(
        score.astype(bf), jnp.where(together, 1.0, 0.0).astype(bf), preferred_element_type=f32
    )
    high = weight.astype(bf).astype(f32)
    kind = lax.broadcasted_iota(jnp.int32, (16, pairs), 0)
    token = jnp.right_shift(lax.broadcasted_iota(jnp.int32, (16, pairs), 1), shift)
    meta[...] = jnp.where(
        kind == 0, token.astype(f32),
        jnp.where(kind == 1, high, jnp.where(kind == 2, weight - high, jnp.where(kind == 3, 1.0, 0.0))),
    ).astype(bf)

    def pack(zt):
        first = zt * 2 * chunk
        pick = jnp.where(
            lax.broadcasted_iota(jnp.int32, (2 * chunk, pairs), 0) + first == slot[0:1], 1.0, 0.0
        ).astype(bf)
        block = jnp.dot(pick, hid[...], preferred_element_type=f32).astype(bf)
        og[pl.ds(zt * 2 * po, 2 * po)] = block.reshape(2 * po, cap, width)
        for k in range(2):
            pick = jnp.where(
                lax.broadcasted_iota(jnp.int32, (META, pairs), 0) + (first + k * chunk)
                == slot[0:1],
                1.0, 0.0,
            ).astype(bf)
            mog[zt * 2 + k] = lax.dot_general(
                meta[...], pick, (((1,), (1,)), ((), ())), preferred_element_type=f32
            ).astype(bf)

    def first_leg(target):
        return (
            remote(og.at[pl.ds(target * po, po)], slot_of(d, e), asend.at[target],
                   recv.at[e * nd + d], d, target),
            remote(mog.at[target], meta_of(d, e), msend.at[target],
                   mrecv.at[e * nd + d], d, target),
        )

    def to_x(ee):
        here, there = slot_of(d, ee), meta_of(d, ee)
        return (
            remote(here, here, xsend.at[ee], recv.at[ee * nd + d], across, e),
            remote(there, there, mxsend.at[ee], mrecv.at[ee * nd + d], across, e),
        )

    def to_core(j, ee):
        dd = d if j == 0 else across
        here, there = slot_of(dd, ee), meta_of(dd, ee)
        return (
            remote(here, here, csend.at[j, ee], recv.at[ee * nd + dd], other, e),
            remote(there, there, mcsend.at[j, ee], mrecv.at[ee * nd + dd], other, e),
        )

    def start(copies):
        for copy in copies:
            copy.start()

    def arrived(dd, ee):
        here, there = slot_of(dd, ee), meta_of(dd, ee)
        remote(here, here, asend.at[0], recv.at[ee * nd + dd], d, e).wait_recv()
        remote(there, there, msend.at[0], mrecv.at[ee * nd + dd], d, e).wait_recv()

    def send_to(zt):
        start(first_leg(zt * 2 + 1 - y))
        start(first_leg(zt * 2 + y))

    target_1 = (nz - 1) * (1 - lax.rem(z, 2))
    target_2 = lax.rem(z + 2, nz)
    target_3 = 1 + lax.rem(z, 2)

    def source(s):
        return jnp.where(
            s == 0, z,
            jnp.where(
                s == 1, (nz - 1) * (1 - lax.div(z, 2)),
                jnp.where(s == 2, z + 1 - 2 * lax.rem(z, 2), 2 - lax.div(z, 2)),
            ),
        )

    pack(target_1)
    pl.semaphore_wait(barrier, ne - 1 + nd - 1)

    @pl.when(outer)
    def _():
        send_to(target_1)

    pack(z)
    own = pltpu.make_async_copy(og.at[pl.ds(e * po, po)], slot_of(d, e), lsem)
    own_meta = pltpu.make_async_copy(mog.at[e], meta_of(d, e), mlsem)
    own.start()
    own_meta.start()
    start(first_leg(pair))
    own.wait()
    own_meta.wait()
    start(to_x(e))
    start(to_core(0, e))
    pack(target_2)

    @pl.when(outer)
    def _():
        send_to(target_2)

    pack(target_3)

    @pl.when(outer)
    def _():
        send_to(target_3)

    load_w.wait()

    def to_pair(zi, p):
        return remote(
            sendy.at[zi, p], recvy.at[zi, p], ysend.at[zi, p], yrecv.at[zi, p], d, pair
        )

    def from_pair(zi, p):
        remote(
            sendy.at[zi, p], recvy.at[zi, p], ysend.at[zi, p], yrecv.at[zi, p], d, e
        ).wait_recv()

    def partial_sums(ee):
        span = pl.ds(pl.multiple_of(ee * rows, rows), rows)
        told = [mbuf[ee * nd + k].astype(f32).T for k in range(nd)]
        row = lax.broadcasted_iota(jnp.int32, (rows, 1), 0)
        base = jnp.zeros((rows, 1), jnp.int32)
        for k in range(1, nd):
            base = base + jnp.where(row >= k * cap, tokens, 0)
        col = lax.broadcasted_iota(jnp.int32, (rows, group), 1)
        acc = jnp.zeros((group, cols), f32)
        for q in range(po):
            mine = jnp.concatenate([m[q * cap:(q + 1) * cap] for m in told], axis=0)
            hit = col == mine[:, 0:1].astype(jnp.int32) + base
            h = jnp.dot(buf[q, span, :], w[q], preferred_element_type=f32).astype(bf)
            for k in (1, 2):
                acc = acc + lax.dot_general(
                    jnp.where(hit, mine[:, k:k + 1], 0.0).astype(bf), h,
                    (((0,), (0,)), ((), ())), preferred_element_type=f32,
                )
        return acc

    def add_on(s):
        zs = source(s)
        up = zs > z
        follow = jnp.where(up, z + 1, z - 1)
        place = jnp.where(jnp.logical_and(jnp.logical_not(up), follow == zs), nz, zs)
        beyond = jnp.where(up, z > 0, z < nz - 1)
        for p in range(np_):
            cs = pl.ds(p * pc, pc)
            from_pair(zs, p)

            @pl.when(beyond)
            def _():
                remote(
                    sendz.at[zs, p], recvz.at[zs, p], zsend.at[zs, p], zrecv.at[zs, p], d, e
                ).wait_recv()
                sendz[zs, p] = (
                    keep[zs, :, cs] + recvy[zs, p].astype(f32) + recvz[zs, p].astype(f32)
                ).astype(bf)

            @pl.when(jnp.logical_not(beyond))
            def _():
                sendz[zs, p] = (keep[zs, :, cs] + recvy[zs, p].astype(f32)).astype(bf)

            remote(
                sendz.at[zs, p], recvz.at[place, p], zsend.at[zs, p], zrecv.at[place, p],
                d, follow * 2 + y,
            ).start()

    def stage(s, carry):
        zs = source(s)
        far, near = zs * 2 + 1 - y, zs * 2 + y
        arrived(d, far)
        start(to_x(far))
        start(to_core(0, far))

        @pl.when(jnp.logical_and(inner, s == 0))
        def _():
            send_to(target_1)

        @pl.when(jnp.logical_and(inner, s == 1))
        def _():
            send_to(target_2)
            send_to(target_3)

        @pl.when(s > 0)
        def _():
            arrived(d, near)
            start(to_x(near))
            start(to_core(0, near))

        arrived(across, far)
        start(to_core(1, far))
        arrived(other, far)
        arrived(other + across - d, far)
        acc = partial_sums(far)
        for p in range(np_):
            sendy[zs, p] = acc[:, p * pc:(p + 1) * pc].astype(bf)
            to_pair(zs, p).start()
        arrived(across, near)
        start(to_core(1, near))
        arrived(other, near)
        arrived(other + across - d, near)
        keep[zs] = partial_sums(near)

        @pl.when(s >= 2)
        def _():
            add_on(s - 1)

        return carry

    lax.fori_loop(0, nz, stage, 0)

    block = width // nd
    wide = width // 2
    for q in range(po):
        @pl.loop(0, width // wide)
        def _(t):
            cs = pl.ds(pl.multiple_of(t * wide, wide), wide)
            g[q, :, cs] = lax.dot_general(
                buf[q, :, pl.ds(pl.multiple_of(d * block, block), block)],
                buf[q, :, cs],
                (((0,), (0,)), ((), ())),
                preferred_element_type=f32,
            )
    out_g = pltpu.make_async_copy(g, g_hbm, gsem)
    out_g.start()
    told = jnp.sum(mbuf[...].astype(f32), axis=0)[3:4]
    lane = lax.broadcasted_iota(jnp.int32, (1, META), 1)
    for q in range(po):
        here = jnp.logical_and(lane >= q * cap, lane < (q + 1) * cap)
        c_ref[q] = jnp.broadcast_to(
            jnp.sum(jnp.where(here, told, 0.0), axis=1, keepdims=True), c_ref.shape[1:]
        )

    add_on(nz - 1)

    def to_token(p, k):
        dd = lax.rem(d + k, nd)
        return remote(
            fin.at[p, dd], o_ref.at[:, pl.ds(pl.multiple_of(d * cols + p * pc, pc), pc)],
            osend.at[p, k], orecv.at[p, d], dd, e,
        )

    for p in range(np_):
        cs = pl.ds(p * pc, pc)
        from_pair(z, p)
        keep[z, :, cs] = keep[z, :, cs] + recvy[z, p].astype(f32)
        for there, place in ((z > 0, z), (z < nz - 1, nz)):
            @pl.when(there)
            def _():
                remote(
                    sendz.at[0, p], recvz.at[place, p], zsend.at[0, p], zrecv.at[place, p], d, e
                ).wait_recv()
                keep[z, :, cs] = keep[z, :, cs] + recvz[place, p].astype(f32)
        fin[p] = keep[z, :, cs].astype(bf).reshape(nd, tokens, pc)
        for k in range(1, nd):
            to_token(p, k).start()
        o_ref[:, pl.ds(pl.multiple_of(d * cols + p * pc, pc), pc)] = fin[p, d]

    for p in range(np_):
        for k in range(1, nd):
            dd = lax.rem(d + k, nd)
            remote(
                fin.at[p, dd], o_ref.at[:, pl.ds(pl.multiple_of(dd * cols + p * pc, pc), pc)],
                osend.at[p, k], orecv.at[p, dd], d, e,
            ).wait_recv()

    out_g.wait()

    def drain(k, carry):
        @pl.when(k != e)
        def _():
            for copy in first_leg(k):
                copy.wait_send()

        for copies in (to_x(k), to_core(0, k), to_core(1, k)):
            for copy in copies:
                copy.wait_send()
        return carry

    lax.fori_loop(0, ne, drain, 0)

    def drain_z(k, carry):
        for p in range(np_):
            to_pair(k, p).wait_send()

            @pl.when(k != z)
            def _():
                remote(
                    sendz.at[k, p], recvz.at[k, p], zsend.at[k, p], zrecv.at[k, p], d, e
                ).wait_send()

        return carry

    lax.fori_loop(0, nz, drain_z, 0)
    for p in range(np_):
        for k in range(1, nd):
            to_token(p, k).wait_send()


def fused(hidden, routes, gate_scores, down_weight):
    tokens, top, width = hidden.shape
    ne, nd = lax.axis_size("expert"), lax.axis_size("dp")
    po, _, cols = down_weight.shape
    pairs = tokens * top
    cap = 3 * pairs // (2 * ne * po)
    nz, group = ne // 2, nd * tokens
    pc = cols // PIECES
    bf, f32 = jnp.bfloat16, jnp.float32
    dma = pltpu.SemaphoreType.DMA
    any_space = pl.BlockSpec(memory_space=pl.ANY)
    vmem = pl.BlockSpec(memory_space=pltpu.VMEM)
    out, gram, count = pl.pallas_call(
        functools.partial(fused_kernel, nd, ne, top, cap, PIECES),
        out_shape=(
            jax.ShapeDtypeStruct((tokens, nd * cols), bf),
            jax.ShapeDtypeStruct((po, width // nd, width), f32),
            jax.ShapeDtypeStruct((po, 8, 128), f32),
        ),
        in_specs=[vmem, vmem, vmem, any_space],
        out_specs=(vmem, any_space, vmem),
        scratch_shapes=[
            pltpu.VMEM((po, ne * nd * cap, width), bf),
            pltpu.VMEM((ne * nd, 16, META), bf),
            pltpu.VMEM((ne * po, cap, width), bf),
            pltpu.VMEM((ne, 16, META), bf),
            pltpu.VMEM((8, pairs), jnp.int32),
            pltpu.VMEM((16, pairs), bf),
            pltpu.VMEM((po, width, cols), bf),
            pltpu.VMEM((nz, PIECES, group, pc), bf),
            pltpu.VMEM((nz, PIECES, group, pc), bf),
            pltpu.VMEM((nz, group, cols), f32),
            pltpu.VMEM((nz, PIECES, group, pc), bf),
            pltpu.VMEM((nz + 1, PIECES, group, pc), bf),
            pltpu.VMEM((PIECES, nd, tokens, pc), bf),
            pltpu.VMEM((po, width // nd, width), f32),
            dma, dma, dma, dma,
            dma((ne,)), dma((ne,)), dma((ne,)), dma((ne,)), dma((2, ne)), dma((2, ne)),
            dma((ne * nd,)), dma((ne * nd,)),
            dma((nz, PIECES)), dma((nz, PIECES)), dma((nz, PIECES)), dma((nz + 1, PIECES)),
            dma((PIECES, nd)), dma((PIECES, nd)),
        ],
        compiler_params=pltpu.CompilerParams(
            collective_id=0, has_side_effects=True, vmem_limit_bytes=VMEM_LIMIT
        ),
    )(
        hidden.reshape(pairs, width), routes.reshape(1, pairs),
        gate_scores.reshape(1, pairs), down_weight,
    )
    return out, gram / count[:, :1, :1]


def earlier(onehot):
    pairs = jnp.arange(onehot.shape[0], dtype=jnp.int32)
    above = (pairs[None, :] < pairs[:, None]).astype(jnp.bfloat16)
    return jnp.dot(
        above, onehot.astype(jnp.bfloat16), preferred_element_type=jnp.float32
    ).astype(jnp.int32)


def plain(hidden, routes, gate_scores, down_weight):
    tokens = hidden.shape[0]
    top_count = hidden.shape[1]
    hidden_width = hidden.shape[2]
    n_owner = lax.axis_size("expert")
    n_group = lax.axis_size("dp")
    per_owner = down_weight.shape[0]
    experts = n_owner * per_owner
    pair_total = tokens * top_count
    capacity = 3 * tokens * top_count // (2 * experts)
    flat_routes = routes.reshape(pair_total)
    onehot = (flat_routes[:, None] == jnp.arange(experts, dtype=jnp.int32)[None, :]).astype(
        jnp.int32
    )
    before = earlier(onehot)
    position = jnp.sum(before * onehot, axis=1)
    slot_index = flat_routes * capacity + position
    local_counts = jnp.sum(onehot, axis=0).astype(jnp.float32)
    totals = lax.psum(local_counts, ("dp", "expert"))
    pair_rows = hidden.reshape(pair_total, hidden_width)
    outgoing = (
        jnp.zeros((experts * capacity, hidden_width), jnp.bfloat16).at[slot_index].set(pair_rows)
    )
    outgoing = outgoing.reshape(n_owner, per_owner, capacity, hidden_width)
    arrived = lax.all_to_all(outgoing, "expert", split_axis=0, concat_axis=0, tiled=True)
    everyone = lax.all_gather(arrived, "dp", axis=0, tiled=True)
    own_counts = lax.dynamic_slice_in_dim(
        totals, lax.axis_index("expert") * per_owner, per_owner, 0
    )
    block_width = hidden_width // n_group
    my_columns = lax.dynamic_slice_in_dim(
        everyone, lax.axis_index("dp") * block_width, block_width, 3
    )
    gram_rows = jnp.einsum(
        "sxcf,sxcg->xfg", my_columns, everyone, preferred_element_type=jnp.float32
    )
    results = jnp.einsum(
        "sxcf,xfd->sxcd", everyone, down_weight, preferred_element_type=jnp.float32
    ).astype(jnp.bfloat16)
    returned = lax.all_to_all(
        lax.all_to_all(results, "dp", split_axis=0, concat_axis=3, tiled=True),
        "expert",
        split_axis=0,
        concat_axis=0,
        tiled=True,
    )
    gram = gram_rows / own_counts[:, None, None]
    model_width = returned.shape[3]
    pair_results = returned.reshape(experts * capacity, model_width)[slot_index]
    scores = gate_scores.astype(jnp.float32)
    weight = scores / jnp.sum(scores, axis=1, keepdims=True)
    combined = jnp.sum(
        pair_results.reshape(tokens, top_count, model_width).astype(jnp.float32)
        * weight[:, :, None],
        axis=1,
    )
    return (combined.astype(jnp.bfloat16), gram)


def fits(hidden, down_weight, nd, ne):
    tokens, top, width = hidden.shape
    po, _, cols = down_weight.shape
    pairs = tokens * top
    cap = 3 * pairs // (2 * ne * po)
    nz, group = ne // 2, nd * tokens
    if nd != 4 or ne != 8 or cap % 16 or po * cap > META or tokens % 16 or tokens > 256:
        return False
    if top & (top - 1) or cols % (PIECES * 128) or width % 256 or (width // nd) % 128:
        return False
    need = (
        2 * po * ne * cap * (nd + 1) * width
        + 2 * po * width * cols
        + nz * group * cols * 12
        + 2 * group * cols * 2
        + 4 * po * (width // nd) * width
        + 4 * pairs * width
        + 8 * group * cols
    )
    return need <= VMEM_BUDGET


def local(hidden, routes, gate_scores, down_weight):
    if fits(hidden, down_weight, lax.axis_size("dp"), lax.axis_size("expert")):
        return fused(hidden, routes, gate_scores, down_weight)
    return plain(hidden, routes, gate_scores, down_weight)


def solution(mesh):
    placed = (
        P(("dp", "expert"), None, None),
        P(("dp", "expert"), None),
        P(("dp", "expert"), None),
        P("expert", None, "dp"),
    )
    return jax.shard_map(
        local,
        mesh=mesh,
        in_specs=placed,
        out_specs=(P(("dp", "expert"), None), P("expert", "dp", None)),
        check_vma=False,
    )
```

```python
import functools

import jax
import jax.numpy as jnp
from jax import lax
from jax.experimental import pallas as pl
from jax.experimental.pallas import tpu as pltpu
from jax.sharding import PartitionSpec as P

MESH = pl.DeviceIdType.MESH
META = 128
PIECES = 4
VMEM_BUDGET = 46 * 2**20
VMEM_LIMIT = 52 * 2**20


def fused_kernel(
    nd, ne, top, cap, np_,
    hid_hbm, rt, gt, w_hbm, o_ref, g, c_ref,
    hid, buf, mbuf, og, mog, slot, meta, w, sendy, recvy, keep, sendz, recvz, fin,
    hsem, wsem, lsem, mlsem, asend, msend, xsend, mxsend, csend, mcsend, recv, mrecv,
    ysend, yrecv, zsend, zrecv, osend, orecv,
):
    f32, bf = jnp.float32, jnp.bfloat16
    po, width, cols = w.shape
    pairs = hid.shape[0]
    tokens = pairs // top
    nz = ne // 2
    rows = nd * cap
    chunk = po * cap
    group = nd * tokens
    pc = cols // np_
    experts = ne * po
    d = lax.axis_index("dp")
    e = lax.axis_index("expert")
    x, c = lax.div(d, 2), lax.rem(d, 2)
    z, y = lax.div(e, 2), lax.rem(e, 2)
    other = d + 1 - 2 * c
    across = lax.rem(d + 2, nd)
    pair = e + 1 - 2 * y
    inner = jnp.logical_and(z > 0, z < nz - 1)
    outer = jnp.logical_not(inner)

    load_h = pltpu.make_async_copy(hid_hbm, hid, hsem)
    load_h.start()
    load_w = pltpu.make_async_copy(w_hbm, w, wsem)
    load_w.start()

    barrier = pltpu.get_barrier_semaphore()
    for k in range(1, ne):
        pl.semaphore_signal(
            barrier, inc=1, device_id=(d, lax.rem(e + k, ne)), device_id_type=MESH
        )
    for k in range(1, nd):
        pl.semaphore_signal(
            barrier, inc=1, device_id=(lax.rem(d + k, nd), e), device_id_type=MESH
        )

    def remote(src, dst, ss, rs, dd, ee):
        return pltpu.make_async_remote_copy(
            src_ref=src, dst_ref=dst, send_sem=ss, recv_sem=rs,
            device_id=(dd, ee), device_id_type=MESH,
        )

    def slot_of(dd, ee):
        return buf.at[:, pl.ds(pl.multiple_of((ee * nd + dd) * cap, cap), cap), :]

    def meta_of(dd, ee):
        return mbuf.at[ee * nd + dd]

    shift = top.bit_length() - 1
    told = jnp.concatenate([rt[...], gt[...]], axis=0).astype(f32).astype(bf)
    spread = jnp.dot(
        told,
        jnp.where(
            lax.broadcasted_iota(jnp.int32, (tokens, pairs), 0)
            == jnp.right_shift(lax.broadcasted_iota(jnp.int32, (tokens, pairs), 1), shift),
            1.0, 0.0,
        ).astype(bf),
        preferred_element_type=f32,
    )
    choice = lax.broadcasted_iota(jnp.int32, (top, pairs), 0) == jnp.bitwise_and(
        lax.broadcasted_iota(jnp.int32, (top, pairs), 1), top - 1
    )
    route = jnp.sum(jnp.where(choice, spread[:top], 0.0), axis=0, keepdims=True).astype(jnp.int32)
    score = jnp.sum(jnp.where(choice, spread[top:], 0.0), axis=0, keepdims=True)
    weight = score / jnp.sum(spread[top:], axis=0, keepdims=True)
    high = weight.astype(bf).astype(f32)
    set_ = jnp.where(
        lax.broadcasted_iota(jnp.int32, (experts, pairs), 0) == route, 1.0, 0.0
    )
    before = jnp.dot(
        set_.astype(bf),
        jnp.where(
            lax.broadcasted_iota(jnp.int32, (pairs, pairs), 0)
            < lax.broadcasted_iota(jnp.int32, (pairs, pairs), 1),
            1.0, 0.0,
        ).astype(bf),
        preferred_element_type=f32,
    )
    position = jnp.sum(before * set_, axis=0, keepdims=True).astype(jnp.int32)
    slot[...] = jnp.broadcast_to(route * cap + position, slot.shape)
    kind = lax.broadcasted_iota(jnp.int32, (16, pairs), 0)
    token = jnp.right_shift(lax.broadcasted_iota(jnp.int32, (16, pairs), 1), shift)
    meta[...] = jnp.where(
        kind == 0, token.astype(f32),
        jnp.where(kind == 1, high, jnp.where(kind == 2, weight - high, jnp.where(kind == 3, 1.0, 0.0))),
    ).astype(bf)
    load_h.wait()

    def pack(zt):
        first = zt * 2 * chunk
        pick = jnp.where(
            lax.broadcasted_iota(jnp.int32, (2 * chunk, pairs), 0) + first == slot[0:1], 1.0, 0.0
        ).astype(bf)
        block = jnp.dot(pick, hid[...], preferred_element_type=f32).astype(bf)
        og[pl.ds(zt * 2 * po, 2 * po)] = block.reshape(2 * po, cap, width)
        for k in range(2):
            pick = jnp.where(
                lax.broadcasted_iota(jnp.int32, (META, pairs), 0) + (first + k * chunk)
                == slot[0:1],
                1.0, 0.0,
            ).astype(bf)
            mog[zt * 2 + k] = lax.dot_general(
                meta[...], pick, (((1,), (1,)), ((), ())), preferred_element_type=f32
            ).astype(bf)

    def first_leg(target):
        return (
            remote(og.at[pl.ds(target * po, po)], slot_of(d, e), asend.at[target],
                   recv.at[e * nd + d], d, target),
            remote(mog.at[target], meta_of(d, e), msend.at[target],
                   mrecv.at[e * nd + d], d, target),
        )

    def to_x(ee):
        here, there = slot_of(d, ee), meta_of(d, ee)
        return (
            remote(here, here, xsend.at[ee], recv.at[ee * nd + d], across, e),
            remote(there, there, mxsend.at[ee], mrecv.at[ee * nd + d], across, e),
        )

    def to_core(j, ee):
        dd = d if j == 0 else across
        here, there = slot_of(dd, ee), meta_of(dd, ee)
        return (
            remote(here, here, csend.at[j, ee], recv.at[ee * nd + dd], other, e),
            remote(there, there, mcsend.at[j, ee], mrecv.at[ee * nd + dd], other, e),
        )

    def start(copies):
        for copy in copies:
            copy.start()

    def arrived(dd, ee):
        here, there = slot_of(dd, ee), meta_of(dd, ee)
        remote(here, here, asend.at[0], recv.at[ee * nd + dd], d, e).wait_recv()
        remote(there, there, msend.at[0], mrecv.at[ee * nd + dd], d, e).wait_recv()

    def send_to(zt):
        start(first_leg(zt * 2 + 1 - y))
        start(first_leg(zt * 2 + y))

    target_1 = (nz - 1) * (1 - lax.rem(z, 2))
    target_2 = lax.rem(z + 2, nz)
    target_3 = 1 + lax.rem(z, 2)

    def source(s):
        return jnp.where(
            s == 0, z,
            jnp.where(
                s == 1, (nz - 1) * (1 - lax.div(z, 2)),
                jnp.where(s == 2, z + 1 - 2 * lax.rem(z, 2), 2 - lax.div(z, 2)),
            ),
        )

    pack(target_1)
    pl.semaphore_wait(barrier, ne - 1 + nd - 1)

    @pl.when(outer)
    def _():
        send_to(target_1)

    pack(z)
    own = pltpu.make_async_copy(og.at[pl.ds(e * po, po)], slot_of(d, e), lsem)
    own_meta = pltpu.make_async_copy(mog.at[e], meta_of(d, e), mlsem)
    own.start()
    own_meta.start()
    start(first_leg(pair))
    own.wait()
    own_meta.wait()
    start(to_x(e))
    start(to_core(0, e))
    pack(target_2)

    @pl.when(outer)
    def _():
        send_to(target_2)

    pack(target_3)

    @pl.when(outer)
    def _():
        send_to(target_3)

    load_w.wait()

    def to_pair(zi, p):
        return remote(
            sendy.at[zi, p], recvy.at[zi, p], ysend.at[zi, p], yrecv.at[zi, p], d, pair
        )

    def from_pair(zi, p):
        remote(
            sendy.at[zi, p], recvy.at[zi, p], ysend.at[zi, p], yrecv.at[zi, p], d, e
        ).wait_recv()

    def partial_sums(ee):
        span = pl.ds(pl.multiple_of(ee * rows, rows), rows)
        told = [mbuf[ee * nd + k].astype(f32).T for k in range(nd)]
        row = lax.broadcasted_iota(jnp.int32, (rows, 1), 0)
        base = jnp.zeros((rows, 1), jnp.int32)
        for k in range(1, nd):
            base = base + jnp.where(row >= k * cap, tokens, 0)
        col = lax.broadcasted_iota(jnp.int32, (rows, group), 1)
        acc = jnp.zeros((group, cols), f32)
        for q in range(po):
            mine = jnp.concatenate([m[q * cap:(q + 1) * cap] for m in told], axis=0)
            hit = col == mine[:, 0:1].astype(jnp.int32) + base
            h = jnp.dot(buf[q, span, :], w[q], preferred_element_type=f32).astype(bf)
            for k in (1, 2):
                acc = acc + lax.dot_general(
                    jnp.where(hit, mine[:, k:k + 1], 0.0).astype(bf), h,
                    (((0,), (0,)), ((), ())), preferred_element_type=f32,
                )
        return acc

    def add_on(s):
        zs = source(s)
        up = zs > z
        follow = jnp.where(up, z + 1, z - 1)
        place = jnp.where(jnp.logical_and(jnp.logical_not(up), follow == zs), nz, zs)
        beyond = jnp.where(up, z > 0, z < nz - 1)
        for p in range(np_):
            cs = pl.ds(p * pc, pc)
            from_pair(zs, p)

            @pl.when(beyond)
            def _():
                remote(
                    sendz.at[zs, p], recvz.at[zs, p], zsend.at[zs, p], zrecv.at[zs, p], d, e
                ).wait_recv()
                sendz[zs, p] = (
                    keep[zs, :, cs] + recvy[zs, p].astype(f32) + recvz[zs, p].astype(f32)
                ).astype(bf)

            @pl.when(jnp.logical_not(beyond))
            def _():
                sendz[zs, p] = (keep[zs, :, cs] + recvy[zs, p].astype(f32)).astype(bf)

            remote(
                sendz.at[zs, p], recvz.at[place, p], zsend.at[zs, p], zrecv.at[place, p],
                d, follow * 2 + y,
            ).start()

    def owner(n):
        ys = jnp.where(n == 0, y, jnp.where(n == 1, 1 - y, jnp.where(lax.rem(n, 2) == 0, 1 - y, y)))
        return source(lax.div(n, 2)), ys

    def step(n, carry):
        @pl.when(n < ne)
        def _():
            zs, ys = owner(n)
            arrived(d, zs * 2 + ys)
            start(to_x(zs * 2 + ys))
            start(to_core(0, zs * 2 + ys))

        @pl.when(jnp.logical_and(inner, n == 1))
        def _():
            send_to(target_1)

        @pl.when(jnp.logical_and(inner, n == 2))
        def _():
            send_to(target_2)
            send_to(target_3)

        zs, ys = owner(n - 1)
        ee = zs * 2 + ys
        arrived(across, ee)
        start(to_core(1, ee))
        arrived(other, ee)
        arrived(other + across - d, ee)
        acc = partial_sums(ee)

        @pl.when(ys == y)
        def _():
            keep[zs] = acc

        @pl.when(ys != y)
        def _():
            for p in range(np_):
                sendy[zs, p] = acc[:, p * pc:(p + 1) * pc].astype(bf)
                to_pair(zs, p).start()

        @pl.when(jnp.logical_and(n >= 5, lax.rem(n, 2) == 1))
        def _():
            add_on(lax.div(n - 3, 2))

        return carry

    lax.fori_loop(1, ne + 1, step, 0)

    block = width // nd
    wide = width // 2
    for q in range(po):
        @pl.loop(0, width // wide)
        def _(t):
            cs = pl.ds(pl.multiple_of(t * wide, wide), wide)
            g[q, :, cs] = lax.dot_general(
                buf[q, :, pl.ds(pl.multiple_of(d * block, block), block)],
                buf[q, :, cs],
                (((0,), (0,)), ((), ())),
                preferred_element_type=f32,
            )
    told = jnp.sum(mbuf[...].astype(f32), axis=0)[3:4]
    lane = lax.broadcasted_iota(jnp.int32, (1, META), 1)
    for q in range(po):
        here = jnp.logical_and(lane >= q * cap, lane < (q + 1) * cap)
        c_ref[q] = jnp.broadcast_to(
            jnp.sum(jnp.where(here, told, 0.0), axis=1, keepdims=True), c_ref.shape[1:]
        )

    add_on(nz - 1)

    def to_token(p, k):
        dd = lax.rem(d + k, nd)
        return remote(
            fin.at[p, dd], o_ref.at[:, pl.ds(pl.multiple_of(d * cols + p * pc, pc), pc)],
            osend.at[p, k], orecv.at[p, d], dd, e,
        )

    for p in range(np_):
        cs = pl.ds(p * pc, pc)
        from_pair(z, p)
        keep[z, :, cs] = keep[z, :, cs] + recvy[z, p].astype(f32)
        for there, place in ((z > 0, z), (z < nz - 1, nz)):
            @pl.when(there)
            def _():
                remote(
                    sendz.at[0, p], recvz.at[place, p], zsend.at[0, p], zrecv.at[place, p], d, e
                ).wait_recv()
                keep[z, :, cs] = keep[z, :, cs] + recvz[place, p].astype(f32)
        fin[p] = keep[z, :, cs].astype(bf).reshape(nd, tokens, pc)
        for k in range(1, nd):
            to_token(p, k).start()
        o_ref[:, pl.ds(pl.multiple_of(d * cols + p * pc, pc), pc)] = fin[p, d]

    for p in range(np_):
        for k in range(1, nd):
            dd = lax.rem(d + k, nd)
            remote(
                fin.at[p, dd], o_ref.at[:, pl.ds(pl.multiple_of(dd * cols + p * pc, pc), pc)],
                osend.at[p, k], orecv.at[p, dd], d, e,
            ).wait_recv()

    def drain(k, carry):
        @pl.when(k != e)
        def _():
            for copy in first_leg(k):
                copy.wait_send()

        for copies in (to_x(k), to_core(0, k), to_core(1, k)):
            for copy in copies:
                copy.wait_send()
        return carry

    lax.fori_loop(0, ne, drain, 0)

    def drain_z(k, carry):
        for p in range(np_):
            to_pair(k, p).wait_send()

            @pl.when(k != z)
            def _():
                remote(
                    sendz.at[k, p], recvz.at[k, p], zsend.at[k, p], zrecv.at[k, p], d, e
                ).wait_send()

        return carry

    lax.fori_loop(0, nz, drain_z, 0)
    for p in range(np_):
        for k in range(1, nd):
            to_token(p, k).wait_send()


def finish_kernel(steps, c_ref, out_ref, gram_ref, out_done, gram_done, work, osem, gsem):
    copy = pltpu.make_async_copy(out_ref, out_done, osem)
    copy.start()
    po, block, _ = gram_ref.shape
    size = block // steps
    scale = [1.0 / c_ref[q, 0:1, 0:1] for q in range(po)]
    sent = []
    for i in range(steps):
        span = pl.ds(i * size, size)
        for q in range(po):
            work[q, span] = gram_ref[q, span] * scale[q]
        sent.append(pltpu.make_async_copy(work.at[:, span], gram_done.at[:, span], gsem.at[i]))
        sent[i].start()
    copy.wait()
    for one in sent:
        one.wait()


def finish(out, gram, count):
    steps = 6
    any_space = pl.BlockSpec(memory_space=pl.ANY)
    vmem = pl.BlockSpec(memory_space=pltpu.VMEM)
    dma = pltpu.SemaphoreType.DMA
    return pl.pallas_call(
        functools.partial(finish_kernel, steps),
        out_shape=(
            jax.ShapeDtypeStruct(out.shape, out.dtype),
            jax.ShapeDtypeStruct(gram.shape, gram.dtype),
        ),
        in_specs=[vmem, vmem, vmem],
        out_specs=(any_space, any_space),
        scratch_shapes=[pltpu.VMEM(gram.shape, gram.dtype), dma, dma((steps,))],
        compiler_params=pltpu.CompilerParams(vmem_limit_bytes=40 * 2**20),
    )(count, out, gram)


def fused(hidden, routes, gate_scores, down_weight):
    tokens, top, width = hidden.shape
    ne, nd = lax.axis_size("expert"), lax.axis_size("dp")
    po, _, cols = down_weight.shape
    pairs = tokens * top
    cap = 3 * pairs // (2 * ne * po)
    nz, group = ne // 2, nd * tokens
    pc = cols // PIECES
    bf, f32 = jnp.bfloat16, jnp.float32
    dma = pltpu.SemaphoreType.DMA
    any_space = pl.BlockSpec(memory_space=pl.ANY)
    vmem = pl.BlockSpec(memory_space=pltpu.VMEM)
    out, gram, count = pl.pallas_call(
        functools.partial(fused_kernel, nd, ne, top, cap, PIECES),
        out_shape=(
            pltpu.VMEM((tokens, nd * cols), bf),
            pltpu.VMEM((po, width // nd, width), f32),
            pltpu.VMEM((po, 8, 128), f32),
        ),
        in_specs=[any_space, vmem, vmem, any_space],
        out_specs=(vmem, vmem, vmem),
        scratch_shapes=[
            pltpu.VMEM((pairs, width), bf),
            pltpu.VMEM((po, ne * nd * cap, width), bf),
            pltpu.VMEM((ne * nd, 16, META), bf),
            pltpu.VMEM((ne * po, cap, width), bf),
            pltpu.VMEM((ne, 16, META), bf),
            pltpu.VMEM((8, pairs), jnp.int32),
            pltpu.VMEM((16, pairs), bf),
            pltpu.VMEM((po, width, cols), bf),
            pltpu.VMEM((nz, PIECES, group, pc), bf),
            pltpu.VMEM((nz, PIECES, group, pc), bf),
            pltpu.VMEM((nz, group, cols), f32),
            pltpu.VMEM((nz, PIECES, group, pc), bf),
            pltpu.VMEM((nz + 1, PIECES, group, pc), bf),
            pltpu.VMEM((PIECES, nd, tokens, pc), bf),
            dma, dma, dma, dma,
            dma((ne,)), dma((ne,)), dma((ne,)), dma((ne,)), dma((2, ne)), dma((2, ne)),
            dma((ne * nd,)), dma((ne * nd,)),
            dma((nz, PIECES)), dma((nz, PIECES)), dma((nz, PIECES)), dma((nz + 1, PIECES)),
            dma((PIECES, nd)), dma((PIECES, nd)),
        ],
        compiler_params=pltpu.CompilerParams(
            collective_id=0, has_side_effects=True, vmem_limit_bytes=VMEM_LIMIT
        ),
    )(
        hidden.reshape(pairs, width), routes.T, gate_scores.T, down_weight,
    )
    return finish(out, gram, count)


def earlier(onehot):
    pairs = jnp.arange(onehot.shape[0], dtype=jnp.int32)
    above = (pairs[None, :] < pairs[:, None]).astype(jnp.bfloat16)
    return jnp.dot(
        above, onehot.astype(jnp.bfloat16), preferred_element_type=jnp.float32
    ).astype(jnp.int32)


def plain(hidden, routes, gate_scores, down_weight):
    tokens = hidden.shape[0]
    top_count = hidden.shape[1]
    hidden_width = hidden.shape[2]
    n_owner = lax.axis_size("expert")
    n_group = lax.axis_size("dp")
    per_owner = down_weight.shape[0]
    experts = n_owner * per_owner
    pair_total = tokens * top_count
    capacity = 3 * tokens * top_count // (2 * experts)
    flat_routes = routes.reshape(pair_total)
    onehot = (flat_routes[:, None] == jnp.arange(experts, dtype=jnp.int32)[None, :]).astype(
        jnp.int32
    )
    before = earlier(onehot)
    position = jnp.sum(before * onehot, axis=1)
    slot_index = flat_routes * capacity + position
    local_counts = jnp.sum(onehot, axis=0).astype(jnp.float32)
    totals = lax.psum(local_counts, ("dp", "expert"))
    pair_rows = hidden.reshape(pair_total, hidden_width)
    outgoing = (
        jnp.zeros((experts * capacity, hidden_width), jnp.bfloat16).at[slot_index].set(pair_rows)
    )
    outgoing = outgoing.reshape(n_owner, per_owner, capacity, hidden_width)
    arrived = lax.all_to_all(outgoing, "expert", split_axis=0, concat_axis=0, tiled=True)
    everyone = lax.all_gather(arrived, "dp", axis=0, tiled=True)
    own_counts = lax.dynamic_slice_in_dim(
        totals, lax.axis_index("expert") * per_owner, per_owner, 0
    )
    block_width = hidden_width // n_group
    my_columns = lax.dynamic_slice_in_dim(
        everyone, lax.axis_index("dp") * block_width, block_width, 3
    )
    gram_rows = jnp.einsum(
        "sxcf,sxcg->xfg", my_columns, everyone, preferred_element_type=jnp.float32
    )
    results = jnp.einsum(
        "sxcf,xfd->sxcd", everyone, down_weight, preferred_element_type=jnp.float32
    ).astype(jnp.bfloat16)
    returned = lax.all_to_all(
        lax.all_to_all(results, "dp", split_axis=0, concat_axis=3, tiled=True),
        "expert",
        split_axis=0,
        concat_axis=0,
        tiled=True,
    )
    gram = gram_rows / own_counts[:, None, None]
    model_width = returned.shape[3]
    pair_results = returned.reshape(experts * capacity, model_width)[slot_index]
    scores = gate_scores.astype(jnp.float32)
    weight = scores / jnp.sum(scores, axis=1, keepdims=True)
    combined = jnp.sum(
        pair_results.reshape(tokens, top_count, model_width).astype(jnp.float32)
        * weight[:, :, None],
        axis=1,
    )
    return (combined.astype(jnp.bfloat16), gram)


def fits(hidden, down_weight, nd, ne):
    tokens, top, width = hidden.shape
    po, _, cols = down_weight.shape
    pairs = tokens * top
    cap = 3 * pairs // (2 * ne * po)
    nz, group = ne // 2, nd * tokens
    if nd != 4 or ne != 8 or cap % 16 or po * cap > META or tokens % 16 or tokens > 256:
        return False
    if top & (top - 1) or cols % (PIECES * 128) or width % 256 or (width // nd) % 384 or top != 8:
        return False
    need = (
        2 * po * ne * cap * (nd + 1) * width
        + 2 * po * width * cols
        + nz * group * cols * 12
        + 2 * group * cols * 2
        + 4 * po * (width // nd) * width
        + 6 * pairs * width
        + 8 * group * cols
    )
    return need <= VMEM_BUDGET


def local(hidden, routes, gate_scores, down_weight):
    if fits(hidden, down_weight, lax.axis_size("dp"), lax.axis_size("expert")):
        return fused(hidden, routes, gate_scores, down_weight)
    return plain(hidden, routes, gate_scores, down_weight)


def solution(mesh):
    placed = (
        P(("dp", "expert"), None, None),
        P(("dp", "expert"), None),
        P(("dp", "expert"), None),
        P("expert", None, "dp"),
    )
    return jax.shard_map(
        local,
        mesh=mesh,
        in_specs=placed,
        out_specs=(P(("dp", "expert"), None), P("expert", "dp", None)),
        check_vma=False,
    )
```

```python
import functools

import jax
import jax.numpy as jnp
from jax import lax
from jax.experimental import pallas as pl
from jax.experimental.pallas import tpu as pltpu
from jax.sharding import PartitionSpec as P

MESH = pl.DeviceIdType.MESH
META = 128
PIECES = 4
GATE = 3
SWAP = 4
AT = (4, 6, 5, 6)
LATE = False
VMEM_BUDGET = 46 * 2**20
VMEM_LIMIT = 52 * 2**20


def fused_kernel(
    nd, ne, top, cap, np_,
    hid_hbm, rt, gt, w_hbm, o_ref, g, c_ref,
    hid, buf, mbuf, og, mog, held, mheld, slot, meta, w, sendy, recvy, keep, sendz, recvz, fin,
    hsem, wsem, lsem, mlsem, asend, msend, hsend, mhsend, hrecv, mhrecv, xsend, mxsend, csend, mcsend, recv, mrecv,
    ysend, yrecv, zsend, zrecv, osend, orecv,
):
    f32, bf = jnp.float32, jnp.bfloat16
    po, width, cols = w.shape
    pairs = hid.shape[0]
    tokens = pairs // top
    nz = ne // 2
    rows = nd * cap
    chunk = po * cap
    group = nd * tokens
    pc = cols // np_
    experts = ne * po
    d = lax.axis_index("dp")
    e = lax.axis_index("expert")
    x, c = lax.div(d, 2), lax.rem(d, 2)
    z, y = lax.div(e, 2), lax.rem(e, 2)
    other = d + 1 - 2 * c
    across = lax.rem(d + 2, nd)
    pair = e + 1 - 2 * y
    inner = jnp.logical_and(z > 0, z < nz - 1)
    outer = jnp.logical_not(inner)

    load_h = pltpu.make_async_copy(hid_hbm, hid, hsem)
    load_h.start()
    load_w = pltpu.make_async_copy(w_hbm, w, wsem)
    load_w.start()

    barrier = pltpu.get_barrier_semaphore()
    for k in range(1, nz):
        pl.semaphore_signal(
            barrier, inc=1, device_id=(d, lax.rem(e + 2 * k, ne)), device_id_type=MESH
        )
    pl.semaphore_signal(barrier, inc=1, device_id=(d, pair), device_id_type=MESH)
    for k in range(1, nd):
        pl.semaphore_signal(
            barrier, inc=1, device_id=(lax.rem(d + k, nd), e), device_id_type=MESH
        )

    def remote(src, dst, ss, rs, dd, ee):
        return pltpu.make_async_remote_copy(
            src_ref=src, dst_ref=dst, send_sem=ss, recv_sem=rs,
            device_id=(dd, ee), device_id_type=MESH,
        )

    def slot_of(dd, ee):
        return buf.at[:, pl.ds(pl.multiple_of((ee * nd + dd) * cap, cap), cap), :]

    def meta_of(dd, ee):
        return mbuf.at[ee * nd + dd]

    shift = top.bit_length() - 1
    told = jnp.concatenate([rt[...], gt[...]], axis=0).astype(f32).astype(bf)
    spread = jnp.dot(
        told,
        jnp.where(
            lax.broadcasted_iota(jnp.int32, (tokens, pairs), 0)
            == jnp.right_shift(lax.broadcasted_iota(jnp.int32, (tokens, pairs), 1), shift),
            1.0, 0.0,
        ).astype(bf),
        preferred_element_type=f32,
    )
    choice = lax.broadcasted_iota(jnp.int32, (top, pairs), 0) == jnp.bitwise_and(
        lax.broadcasted_iota(jnp.int32, (top, pairs), 1), top - 1
    )
    route = jnp.sum(jnp.where(choice, spread[:top], 0.0), axis=0, keepdims=True).astype(jnp.int32)
    score = jnp.sum(jnp.where(choice, spread[top:], 0.0), axis=0, keepdims=True)
    weight = score / jnp.sum(spread[top:], axis=0, keepdims=True)
    high = weight.astype(bf).astype(f32)
    set_ = jnp.where(
        lax.broadcasted_iota(jnp.int32, (experts, pairs), 0) == route, 1.0, 0.0
    )
    before = jnp.dot(
        set_.astype(bf),
        jnp.where(
            lax.broadcasted_iota(jnp.int32, (pairs, pairs), 0)
            < lax.broadcasted_iota(jnp.int32, (pairs, pairs), 1),
            1.0, 0.0,
        ).astype(bf),
        preferred_element_type=f32,
    )
    position = jnp.sum(before * set_, axis=0, keepdims=True).astype(jnp.int32)
    slot[...] = jnp.broadcast_to(route * cap + position, slot.shape)
    kind = lax.broadcasted_iota(jnp.int32, (16, pairs), 0)
    token = jnp.right_shift(lax.broadcasted_iota(jnp.int32, (16, pairs), 1), shift)
    meta[...] = jnp.where(
        kind == 0, token.astype(f32),
        jnp.where(kind == 1, high, jnp.where(kind == 2, weight - high, jnp.where(kind == 3, 1.0, 0.0))),
    ).astype(bf)
    load_h.wait()

    def pack(zt):
        first = zt * 2 * chunk
        pick = jnp.where(
            lax.broadcasted_iota(jnp.int32, (2 * chunk, pairs), 0) + first == slot[0:1], 1.0, 0.0
        ).astype(bf)
        block = jnp.dot(pick, hid[...], preferred_element_type=f32).astype(bf)
        og[pl.ds(zt * 2 * po, 2 * po)] = block.reshape(2 * po, cap, width)
        for k in range(2):
            pick = jnp.where(
                lax.broadcasted_iota(jnp.int32, (META, pairs), 0) + (first + k * chunk)
                == slot[0:1],
                1.0, 0.0,
            ).astype(bf)
            mog[zt * 2 + k] = lax.dot_general(
                meta[...], pick, (((1,), (1,)), ((), ())), preferred_element_type=f32
            ).astype(bf)

    def first_leg(target):
        return (
            remote(og.at[pl.ds(target * po, po)], slot_of(d, e), asend.at[target],
                   recv.at[e * nd + d], d, target),
            remote(mog.at[target], meta_of(d, e), msend.at[target],
                   mrecv.at[e * nd + d], d, target),
        )

    def to_x(ee):
        here, there = slot_of(d, ee), meta_of(d, ee)
        return (
            remote(here, here, xsend.at[ee], recv.at[ee * nd + d], across, e),
            remote(there, there, mxsend.at[ee], mrecv.at[ee * nd + d], across, e),
        )

    def to_core(j, ee):
        dd = d if j == 0 else across
        here, there = slot_of(dd, ee), meta_of(dd, ee)
        return (
            remote(here, here, csend.at[j, ee], recv.at[ee * nd + dd], other, e),
            remote(there, there, mcsend.at[j, ee], mrecv.at[ee * nd + dd], other, e),
        )

    def start(copies):
        for copy in copies:
            copy.start()

    def arrived(dd, ee):
        here, there = slot_of(dd, ee), meta_of(dd, ee)
        remote(here, here, asend.at[0], recv.at[ee * nd + dd], d, e).wait_recv()
        remote(there, there, msend.at[0], mrecv.at[ee * nd + dd], d, e).wait_recv()

    def near(k):
        start(first_leg(target[k] * 2 + y))

    def far(k):
        there = target[k] * 2 + 1 - y
        start((
            remote(og.at[pl.ds(there * po, po)], held.at[k], asend.at[there], hrecv.at[k], d, pair),
            remote(mog.at[there], mheld.at[k], msend.at[there], mhrecv.at[k], d, pair),
        ))

    def second_leg(k):
        there = target[k] * 2 + y
        return (
            remote(held.at[k], slot_of(d, pair), hsend.at[k], recv.at[pair * nd + d], d, there),
            remote(mheld.at[k], meta_of(d, pair), mhsend.at[k], mrecv.at[pair * nd + d], d, there),
        )

    def relay(k):
        remote(held.at[k], held.at[k], hsend.at[k], hrecv.at[k], d, e).wait_recv()
        remote(mheld.at[k], mheld.at[k], mhsend.at[k], mhrecv.at[k], d, e).wait_recv()
        start(second_leg(k))

    target = ((nz - 1) * (1 - lax.rem(z, 2)), lax.rem(z + 2, nz), 1 + lax.rem(z, 2))

    def source(s):
        return jnp.where(
            s == 0, z,
            jnp.where(
                s == 1, (nz - 1) * (1 - lax.div(z, 2)),
                jnp.where(s == 2, z + 1 - 2 * lax.rem(z, 2), 2 - lax.div(z, 2)),
            ),
        )

    pack(target[0])
    pl.semaphore_wait(barrier, nz + nd - 1)
    far(0)

    @pl.when(outer)
    def _():
        near(0)

    pack(z)
    own = pltpu.make_async_copy(og.at[pl.ds(e * po, po)], slot_of(d, e), lsem)
    own_meta = pltpu.make_async_copy(mog.at[e], meta_of(d, e), mlsem)
    own.start()
    own_meta.start()
    start(first_leg(pair))
    own.wait()
    own_meta.wait()
    start(to_x(e))
    start(to_core(0, e))
    pack(target[1])
    far(1)
    pack(target[2])
    far(2)

    @pl.when(outer)
    def _():
        relay(0)
        near(1)

    load_w.wait()

    def to_pair(zi, p):
        return remote(
            sendy.at[zi, p], recvy.at[zi, p], ysend.at[zi, p], yrecv.at[zi, p], d, pair
        )

    def from_pair(zi, p):
        remote(
            sendy.at[zi, p], recvy.at[zi, p], ysend.at[zi, p], yrecv.at[zi, p], d, e
        ).wait_recv()

    def partial_sums(ee):
        span = pl.ds(pl.multiple_of(ee * rows, rows), rows)
        told = [mbuf[ee * nd + k].astype(f32).T for k in range(nd)]
        row = lax.broadcasted_iota(jnp.int32, (rows, 1), 0)
        base = jnp.zeros((rows, 1), jnp.int32)
        for k in range(1, nd):
            base = base + jnp.where(row >= k * cap, tokens, 0)
        col = lax.broadcasted_iota(jnp.int32, (rows, group), 1)
        acc = jnp.zeros((group, cols), f32)
        for q in range(po):
            mine = jnp.concatenate([m[q * cap:(q + 1) * cap] for m in told], axis=0)
            hit = col == mine[:, 0:1].astype(jnp.int32) + base
            h = jnp.dot(buf[q, span, :], w[q], preferred_element_type=f32).astype(bf)
            for k in (1, 2):
                acc = acc + lax.dot_general(
                    jnp.where(hit, mine[:, k:k + 1], 0.0).astype(bf), h,
                    (((0,), (0,)), ((), ())), preferred_element_type=f32,
                )
        return acc

    def add_on(s, pieces):
        zs = source(s)
        up = zs > z
        follow = jnp.where(up, z + 1, z - 1)
        place = jnp.where(jnp.logical_and(jnp.logical_not(up), follow == zs), nz, zs)
        beyond = jnp.where(up, z > 0, z < nz - 1)
        for p in pieces:
            cs = pl.ds(p * pc, pc)
            from_pair(zs, p)

            @pl.when(beyond)
            def _():
                remote(
                    sendz.at[zs, p], recvz.at[zs, p], zsend.at[zs, p], zrecv.at[zs, p], d, e
                ).wait_recv()
                sendz[zs, p] = (
                    keep[zs, :, cs] + recvy[zs, p].astype(f32) + recvz[zs, p].astype(f32)
                ).astype(bf)

            @pl.when(jnp.logical_not(beyond))
            def _():
                sendz[zs, p] = (keep[zs, :, cs] + recvy[zs, p].astype(f32)).astype(bf)

            remote(
                sendz.at[zs, p], recvz.at[place, p], zsend.at[zs, p], zrecv.at[place, p],
                d, follow * 2 + y,
            ).start()

    every = tuple(range(np_))

    def owner(n):
        turn = jnp.where(inner, n, jnp.where(n == 0, 0, jnp.where(n == ne - 1, 1, n + 1)))
        ys = jnp.where(
            turn == 0, y, jnp.where(
                turn == 1, 1 - y, jnp.where(
                    lax.rem(turn + jnp.where(turn < SWAP, 1, 0), 2) == 0, 1 - y, y
                ),
            ),
        )
        return source(lax.div(turn, 2)), ys

    def step(n, carry):
        @pl.when(n < ne)
        def _():
            zs, ys = owner(n)
            arrived(d, zs * 2 + ys)
            start(to_x(zs * 2 + ys))
            start(to_core(0, zs * 2 + ys))

        @pl.when(jnp.logical_and(inner, n == 1))
        def _():
            relay(0)
            near(0)

        @pl.when(jnp.logical_and(inner, n == GATE))
        def _():
            relay(1)
            near(1)

        @pl.when(jnp.logical_and(inner, n == GATE + 1))
        def _():
            relay(2)
            near(2)

        @pl.when(jnp.logical_and(outer, n == 3))
        def _():
            relay(1)

        @pl.when(jnp.logical_and(outer, n == 4))
        def _():
            relay(2)
            near(2)

        zs, ys = owner(n - 1)
        ee = zs * 2 + ys
        arrived(across, ee)
        start(to_core(1, ee))
        arrived(other, ee)
        arrived(other + across - d, ee)
        acc = partial_sums(ee)

        @pl.when(ys == y)
        def _():
            keep[zs] = acc

        @pl.when(ys != y)
        def _():
            for p in range(np_):
                sendy[zs, p] = acc[:, p * pc:(p + 1) * pc].astype(bf)
                to_pair(zs, p).start()

        done = n - 1

        @pl.when(jnp.logical_and(outer, done == AT[0]))
        def _():
            add_on(1, every)

        @pl.when(jnp.logical_and(outer, done == AT[1]))
        def _():
            add_on(2, every)

        @pl.when(jnp.logical_and(inner, done == AT[2]))
        def _():
            add_on(1, every[:np_ // 2])

        @pl.when(jnp.logical_and(inner, done == AT[3]))
        def _():
            add_on(1, every[np_ // 2:])

        return carry

    lax.fori_loop(1, ne + 1, step, 0)

    @pl.when(outer)
    def _():
        add_on(3, every)

    @pl.when(inner)
    def _():
        if not LATE:
            add_on(2, every)

    block = width // nd
    wide = width // 2
    for q in range(po):
        @pl.loop(0, width // wide)
        def _(t):
            cs = pl.ds(pl.multiple_of(t * wide, wide), wide)
            g[q, :, cs] = lax.dot_general(
                buf[q, :, pl.ds(pl.multiple_of(d * block, block), block)],
                buf[q, :, cs],
                (((0,), (0,)), ((), ())),
                preferred_element_type=f32,
            )
    told = jnp.sum(mbuf[...].astype(f32), axis=0)[3:4]
    lane = lax.broadcasted_iota(jnp.int32, (1, META), 1)
    for q in range(po):
        here = jnp.logical_and(lane >= q * cap, lane < (q + 1) * cap)
        c_ref[q] = jnp.broadcast_to(
            jnp.sum(jnp.where(here, told, 0.0), axis=1, keepdims=True), c_ref.shape[1:]
        )

    @pl.when(inner)
    def _():
        if LATE:
            add_on(2, every)
        add_on(3, every)

    def to_token(p, k):
        dd = lax.rem(d + k, nd)
        return remote(
            fin.at[p, dd], o_ref.at[:, pl.ds(pl.multiple_of(d * cols + p * pc, pc), pc)],
            osend.at[p, k], orecv.at[p, d], dd, e,
        )

    for p in range(np_):
        cs = pl.ds(p * pc, pc)
        from_pair(z, p)
        keep[z, :, cs] = keep[z, :, cs] + recvy[z, p].astype(f32)
        for there, place in ((z > 0, z), (z < nz - 1, nz)):
            @pl.when(there)
            def _():
                remote(
                    sendz.at[0, p], recvz.at[place, p], zsend.at[0, p], zrecv.at[place, p], d, e
                ).wait_recv()
                keep[z, :, cs] = keep[z, :, cs] + recvz[place, p].astype(f32)
        fin[p] = keep[z, :, cs].astype(bf).reshape(nd, tokens, pc)
        for k in range(1, nd):
            to_token(p, k).start()
        o_ref[:, pl.ds(pl.multiple_of(d * cols + p * pc, pc), pc)] = fin[p, d]

    for p in range(np_):
        for k in range(1, nd):
            dd = lax.rem(d + k, nd)
            remote(
                fin.at[p, dd], o_ref.at[:, pl.ds(pl.multiple_of(dd * cols + p * pc, pc), pc)],
                osend.at[p, k], orecv.at[p, dd], d, e,
            ).wait_recv()

    def drain(k, carry):
        @pl.when(k != e)
        def _():
            for copy in first_leg(k):
                copy.wait_send()

        for copies in (to_x(k), to_core(0, k), to_core(1, k)):
            for copy in copies:
                copy.wait_send()
        return carry

    lax.fori_loop(0, ne, drain, 0)

    def drain_z(k, carry):
        for p in range(np_):
            to_pair(k, p).wait_send()

            @pl.when(k != z)
            def _():
                remote(
                    sendz.at[k, p], recvz.at[k, p], zsend.at[k, p], zrecv.at[k, p], d, e
                ).wait_send()

        return carry

    lax.fori_loop(0, nz, drain_z, 0)
    for k in range(nz - 1):
        for copy in second_leg(k):
            copy.wait_send()
    for p in range(np_):
        for k in range(1, nd):
            to_token(p, k).wait_send()


def finish_kernel(steps, c_ref, out_ref, gram_ref, out_done, gram_done, work, osem, gsem):
    copy = pltpu.make_async_copy(out_ref, out_done, osem)
    copy.start()
    po, block, _ = gram_ref.shape
    size = block // steps
    scale = [1.0 / c_ref[q, 0:1, 0:1] for q in range(po)]
    sent = []
    for i in range(steps):
        span = pl.ds(i * size, size)
        for q in range(po):
            work[q, span] = gram_ref[q, span] * scale[q]
        sent.append(pltpu.make_async_copy(work.at[:, span], gram_done.at[:, span], gsem.at[i]))
        sent[i].start()
    copy.wait()
    for one in sent:
        one.wait()


def finish(out, gram, count):
    steps = 6
    any_space = pl.BlockSpec(memory_space=pl.ANY)
    vmem = pl.BlockSpec(memory_space=pltpu.VMEM)
    dma = pltpu.SemaphoreType.DMA
    return pl.pallas_call(
        functools.partial(finish_kernel, steps),
        out_shape=(
            jax.ShapeDtypeStruct(out.shape, out.dtype),
            jax.ShapeDtypeStruct(gram.shape, gram.dtype),
        ),
        in_specs=[vmem, vmem, vmem],
        out_specs=(any_space, any_space),
        scratch_shapes=[pltpu.VMEM(gram.shape, gram.dtype), dma, dma((steps,))],
        compiler_params=pltpu.CompilerParams(vmem_limit_bytes=40 * 2**20),
    )(count, out, gram)


def fused(hidden, routes, gate_scores, down_weight):
    tokens, top, width = hidden.shape
    ne, nd = lax.axis_size("expert"), lax.axis_size("dp")
    po, _, cols = down_weight.shape
    pairs = tokens * top
    cap = 3 * pairs // (2 * ne * po)
    nz, group = ne // 2, nd * tokens
    pc = cols // PIECES
    bf, f32 = jnp.bfloat16, jnp.float32
    dma = pltpu.SemaphoreType.DMA
    any_space = pl.BlockSpec(memory_space=pl.ANY)
    vmem = pl.BlockSpec(memory_space=pltpu.VMEM)
    out, gram, count = pl.pallas_call(
        functools.partial(fused_kernel, nd, ne, top, cap, PIECES),
        out_shape=(
            pltpu.VMEM((tokens, nd * cols), bf),
            pltpu.VMEM((po, width // nd, width), f32),
            pltpu.VMEM((po, 8, 128), f32),
        ),
        in_specs=[any_space, vmem, vmem, any_space],
        out_specs=(vmem, vmem, vmem),
        scratch_shapes=[
            pltpu.VMEM((pairs, width), bf),
            pltpu.VMEM((po, ne * nd * cap, width), bf),
            pltpu.VMEM((ne * nd, 16, META), bf),
            pltpu.VMEM((ne * po, cap, width), bf),
            pltpu.VMEM((ne, 16, META), bf),
            pltpu.VMEM((nz - 1, po, cap, width), bf),
            pltpu.VMEM((nz - 1, 16, META), bf),
            pltpu.VMEM((8, pairs), jnp.int32),
            pltpu.VMEM((16, pairs), bf),
            pltpu.VMEM((po, width, cols), bf),
            pltpu.VMEM((nz, PIECES, group, pc), bf),
            pltpu.VMEM((nz, PIECES, group, pc), bf),
            pltpu.VMEM((nz, group, cols), f32),
            pltpu.VMEM((nz, PIECES, group, pc), bf),
            pltpu.VMEM((nz + 1, PIECES, group, pc), bf),
            pltpu.VMEM((PIECES, nd, tokens, pc), bf),
            dma, dma, dma, dma,
            dma((ne,)), dma((ne,)), dma((nz - 1,)), dma((nz - 1,)), dma((nz - 1,)), dma((nz - 1,)),
            dma((ne,)), dma((ne,)), dma((2, ne)), dma((2, ne)),
            dma((ne * nd,)), dma((ne * nd,)),
            dma((nz, PIECES)), dma((nz, PIECES)), dma((nz, PIECES)), dma((nz + 1, PIECES)),
            dma((PIECES, nd)), dma((PIECES, nd)),
        ],
        compiler_params=pltpu.CompilerParams(
            collective_id=0, has_side_effects=True, vmem_limit_bytes=VMEM_LIMIT
        ),
    )(
        hidden.reshape(pairs, width), routes.T, gate_scores.T, down_weight,
    )
    return finish(out, gram, count)


def earlier(onehot):
    pairs = jnp.arange(onehot.shape[0], dtype=jnp.int32)
    above = (pairs[None, :] < pairs[:, None]).astype(jnp.bfloat16)
    return jnp.dot(
        above, onehot.astype(jnp.bfloat16), preferred_element_type=jnp.float32
    ).astype(jnp.int32)


def plain(hidden, routes, gate_scores, down_weight):
    tokens = hidden.shape[0]
    top_count = hidden.shape[1]
    hidden_width = hidden.shape[2]
    n_owner = lax.axis_size("expert")
    n_group = lax.axis_size("dp")
    per_owner = down_weight.shape[0]
    experts = n_owner * per_owner
    pair_total = tokens * top_count
    capacity = 3 * tokens * top_count // (2 * experts)
    flat_routes = routes.reshape(pair_total)
    onehot = (flat_routes[:, None] == jnp.arange(experts, dtype=jnp.int32)[None, :]).astype(
        jnp.int32
    )
    before = earlier(onehot)
    position = jnp.sum(before * onehot, axis=1)
    slot_index = flat_routes * capacity + position
    local_counts = jnp.sum(onehot, axis=0).astype(jnp.float32)
    totals = lax.psum(local_counts, ("dp", "expert"))
    pair_rows = hidden.reshape(pair_total, hidden_width)
    outgoing = (
        jnp.zeros((experts * capacity, hidden_width), jnp.bfloat16).at[slot_index].set(pair_rows)
    )
    outgoing = outgoing.reshape(n_owner, per_owner, capacity, hidden_width)
    arrived = lax.all_to_all(outgoing, "expert", split_axis=0, concat_axis=0, tiled=True)
    everyone = lax.all_gather(arrived, "dp", axis=0, tiled=True)
    own_counts = lax.dynamic_slice_in_dim(
        totals, lax.axis_index("expert") * per_owner, per_owner, 0
    )
    block_width = hidden_width // n_group
    my_columns = lax.dynamic_slice_in_dim(
        everyone, lax.axis_index("dp") * block_width, block_width, 3
    )
    gram_rows = jnp.einsum(
        "sxcf,sxcg->xfg", my_columns, everyone, preferred_element_type=jnp.float32
    )
    results = jnp.einsum(
        "sxcf,xfd->sxcd", everyone, down_weight, preferred_element_type=jnp.float32
    ).astype(jnp.bfloat16)
    returned = lax.all_to_all(
        lax.all_to_all(results, "dp", split_axis=0, concat_axis=3, tiled=True),
        "expert",
        split_axis=0,
        concat_axis=0,
        tiled=True,
    )
    gram = gram_rows / own_counts[:, None, None]
    model_width = returned.shape[3]
    pair_results = returned.reshape(experts * capacity, model_width)[slot_index]
    scores = gate_scores.astype(jnp.float32)
    weight = scores / jnp.sum(scores, axis=1, keepdims=True)
    combined = jnp.sum(
        pair_results.reshape(tokens, top_count, model_width).astype(jnp.float32)
        * weight[:, :, None],
        axis=1,
    )
    return (combined.astype(jnp.bfloat16), gram)


def fits(hidden, down_weight, nd, ne):
    tokens, top, width = hidden.shape
    po, _, cols = down_weight.shape
    pairs = tokens * top
    cap = 3 * pairs // (2 * ne * po)
    nz, group = ne // 2, nd * tokens
    if nd != 4 or ne != 8 or cap % 16 or po * cap > META or tokens % 16 or tokens > 256:
        return False
    if top & (top - 1) or cols % (PIECES * 128) or width % 256 or (width // nd) % 384 or top != 8:
        return False
    need = (
        2 * po * ne * cap * (nd + 1) * width
        + 2 * po * width * cols
        + nz * group * cols * 12
        + 2 * group * cols * 2
        + 4 * po * (width // nd) * width
        + 6 * pairs * width
        + 8 * group * cols
    )
    return need <= VMEM_BUDGET


def local(hidden, routes, gate_scores, down_weight):
    if fits(hidden, down_weight, lax.axis_size("dp"), lax.axis_size("expert")):
        return fused(hidden, routes, gate_scores, down_weight)
    return plain(hidden, routes, gate_scores, down_weight)


def solution(mesh):
    placed = (
        P(("dp", "expert"), None, None),
        P(("dp", "expert"), None),
        P(("dp", "expert"), None),
        P("expert", None, "dp"),
    )
    return jax.shard_map(
        local,
        mesh=mesh,
        in_specs=placed,
        out_specs=(P(("dp", "expert"), None), P("expert", "dp", None)),
        check_vma=False,
    )
```

```python
import functools

import jax
import jax.numpy as jnp
from jax import lax
from jax.experimental import pallas as pl
from jax.experimental.pallas import tpu as pltpu
from jax.sharding import PartitionSpec as P

MESH = pl.DeviceIdType.MESH
META = 128
PIECES = 4
GATE = 2
SWAP = 4
AT = (4, 6, 5, 6)
SPLIT = (0, 0, 2, 4, 4, 4, 5, 6, 6)
VMEM_BUDGET = 46 * 2**20
VMEM_LIMIT = 52 * 2**20


def fused_kernel(
    nd, ne, top, cap, np_,
    hid_hbm, rt, gt, w_hbm, o_ref, g, c_ref,
    hid, buf, mbuf, og, mog, held, mheld, slot, meta, w, sendy, recvy, keep, sendz, recvz, fin,
    hsem, wsem, lsem, mlsem, asend, msend, fsend, mfsend, hsend, mhsend, hrecv, mhrecv, xsend, mxsend, csend, mcsend, recv, mrecv,
    ysend, yrecv, zsend, zrecv, osend, orecv,
):
    f32, bf = jnp.float32, jnp.bfloat16
    po, width, cols = w.shape
    pairs = hid.shape[0]
    tokens = pairs // top
    nz = ne // 2
    rows = nd * cap
    chunk = po * cap
    group = nd * tokens
    pc = cols // np_
    experts = ne * po
    d = lax.axis_index("dp")
    e = lax.axis_index("expert")
    x, c = lax.div(d, 2), lax.rem(d, 2)
    z, y = lax.div(e, 2), lax.rem(e, 2)
    other = d + 1 - 2 * c
    across = lax.rem(d + 2, nd)
    pair = e + 1 - 2 * y
    inner = jnp.logical_and(z > 0, z < nz - 1)
    outer = jnp.logical_not(inner)

    load_h = pltpu.make_async_copy(hid_hbm, hid, hsem)
    load_h.start()
    load_w = pltpu.make_async_copy(w_hbm, w, wsem)
    load_w.start()

    barrier = pltpu.get_barrier_semaphore()
    for k in range(1, nz):
        pl.semaphore_signal(
            barrier, inc=1, device_id=(d, lax.rem(e + 2 * k, ne)), device_id_type=MESH
        )
    pl.semaphore_signal(barrier, inc=1, device_id=(d, pair), device_id_type=MESH)
    for k in range(1, nd):
        pl.semaphore_signal(
            barrier, inc=1, device_id=(lax.rem(d + k, nd), e), device_id_type=MESH
        )

    def remote(src, dst, ss, rs, dd, ee):
        return pltpu.make_async_remote_copy(
            src_ref=src, dst_ref=dst, send_sem=ss, recv_sem=rs,
            device_id=(dd, ee), device_id_type=MESH,
        )

    def slot_of(dd, ee):
        return buf.at[:, pl.ds(pl.multiple_of((ee * nd + dd) * cap, cap), cap), :]

    def part_of(q, dd, ee):
        return buf.at[q, pl.ds(pl.multiple_of((ee * nd + dd) * cap, cap), cap), :]

    def meta_of(dd, ee):
        return mbuf.at[ee * nd + dd]

    shift = top.bit_length() - 1
    told = jnp.concatenate([rt[...], gt[...]], axis=0).astype(f32).astype(bf)
    spread = jnp.dot(
        told,
        jnp.where(
            lax.broadcasted_iota(jnp.int32, (tokens, pairs), 0)
            == jnp.right_shift(lax.broadcasted_iota(jnp.int32, (tokens, pairs), 1), shift),
            1.0, 0.0,
        ).astype(bf),
        preferred_element_type=f32,
    )
    choice = lax.broadcasted_iota(jnp.int32, (top, pairs), 0) == jnp.bitwise_and(
        lax.broadcasted_iota(jnp.int32, (top, pairs), 1), top - 1
    )
    route = jnp.sum(jnp.where(choice, spread[:top], 0.0), axis=0, keepdims=True).astype(jnp.int32)
    score = jnp.sum(jnp.where(choice, spread[top:], 0.0), axis=0, keepdims=True)
    weight = score / jnp.sum(spread[top:], axis=0, keepdims=True)
    high = weight.astype(bf).astype(f32)
    set_ = jnp.where(
        lax.broadcasted_iota(jnp.int32, (experts, pairs), 0) == route, 1.0, 0.0
    )
    before = jnp.dot(
        set_.astype(bf),
        jnp.where(
            lax.broadcasted_iota(jnp.int32, (pairs, pairs), 0)
            < lax.broadcasted_iota(jnp.int32, (pairs, pairs), 1),
            1.0, 0.0,
        ).astype(bf),
        preferred_element_type=f32,
    )
    position = jnp.sum(before * set_, axis=0, keepdims=True).astype(jnp.int32)
    slot[...] = jnp.broadcast_to(route * cap + position, slot.shape)
    kind = lax.broadcasted_iota(jnp.int32, (16, pairs), 0)
    token = jnp.right_shift(lax.broadcasted_iota(jnp.int32, (16, pairs), 1), shift)
    meta[...] = jnp.where(
        kind == 0, token.astype(f32),
        jnp.where(kind == 1, high, jnp.where(kind == 2, weight - high, jnp.where(kind == 3, 1.0, 0.0))),
    ).astype(bf)
    load_h.wait()

    def pack(zt):
        first = zt * 2 * chunk
        pick = jnp.where(
            lax.broadcasted_iota(jnp.int32, (2 * chunk, pairs), 0) + first == slot[0:1], 1.0, 0.0
        ).astype(bf)
        block = jnp.dot(pick, hid[...], preferred_element_type=f32).astype(bf)
        og[pl.ds(zt * 2 * po, 2 * po)] = block.reshape(2 * po, cap, width)
        for k in range(2):
            pick = jnp.where(
                lax.broadcasted_iota(jnp.int32, (META, pairs), 0) + (first + k * chunk)
                == slot[0:1],
                1.0, 0.0,
            ).astype(bf)
            mog[zt * 2 + k] = lax.dot_general(
                meta[...], pick, (((1,), (1,)), ((), ())), preferred_element_type=f32
            ).astype(bf)

    whole = tuple(range(po + 1))

    def legs(rows_from, meta_from, rows_sem, meta_sem, dd, ee, to_d, to_e, which=whole):
        at = ee * nd + dd
        return tuple(
            remote(rows_from(q), part_of(q, dd, ee), rows_sem(q), recv.at[q, at], to_d, to_e)
            if q < po
            else remote(meta_from, meta_of(dd, ee), meta_sem, mrecv.at[at], to_d, to_e)
            for q in which
        )

    def first_leg(there):
        return legs(
            lambda q: og.at[there * po + q], mog.at[there],
            lambda q: asend.at[q, there], msend.at[there], d, e, d, there,
        )

    def to_x(ee, which=whole):
        return legs(
            lambda q: part_of(q, d, ee), meta_of(d, ee),
            lambda q: xsend.at[q, ee], mxsend.at[ee], d, ee, across, e, which,
        )

    def to_core(j, ee, which=whole):
        dd = d if j == 0 else across
        return legs(
            lambda q: part_of(q, dd, ee), meta_of(dd, ee),
            lambda q: csend.at[j, q, ee], mcsend.at[j, ee], dd, ee, other, e, which,
        )

    def start(copies):
        for copy in copies:
            copy.start()

    def came(q, dd, ee):
        here = part_of(q, dd, ee)
        remote(here, here, asend.at[0, 0], recv.at[q, ee * nd + dd], d, e).wait_recv()

    def meta_came(dd, ee):
        there = meta_of(dd, ee)
        remote(there, there, msend.at[0], mrecv.at[ee * nd + dd], d, e).wait_recv()

    def arrived(dd, ee):
        for q in range(po):
            came(q, dd, ee)
        meta_came(dd, ee)

    def near(k):
        start(first_leg(target[k] * 2 + y))

    def across_y(k):
        there = target[k] * 2 + 1 - y
        return (
            remote(og.at[pl.ds(there * po, po)], held.at[k], fsend.at[k], hrecv.at[k], d, pair),
            remote(mog.at[there], mheld.at[k], mfsend.at[k], mhrecv.at[k], d, pair),
        )

    def far(k):
        start(across_y(k))

    def second_leg(k):
        return legs(
            lambda q: held.at[k, q], mheld.at[k],
            lambda q: hsend.at[q, k], mhsend.at[k], d, pair, d, target[k] * 2 + y,
        )

    def relay(k):
        remote(held.at[k], held.at[k], fsend.at[k], hrecv.at[k], d, e).wait_recv()
        remote(mheld.at[k], mheld.at[k], mhsend.at[k], mhrecv.at[k], d, e).wait_recv()
        start(second_leg(k))

    target = ((nz - 1) * (1 - lax.rem(z, 2)), lax.rem(z + 2, nz), 1 + lax.rem(z, 2))

    def source(s):
        return jnp.where(
            s == 0, z,
            jnp.where(
                s == 1, (nz - 1) * (1 - lax.div(z, 2)),
                jnp.where(s == 2, z + 1 - 2 * lax.rem(z, 2), 2 - lax.div(z, 2)),
            ),
        )

    pack(target[0])
    pl.semaphore_wait(barrier, nz + nd - 1)
    far(0)

    @pl.when(outer)
    def _():
        near(0)

    pack(z)
    own = pltpu.make_async_copy(og.at[pl.ds(e * po, po)], slot_of(d, e), lsem)
    own_meta = pltpu.make_async_copy(mog.at[e], meta_of(d, e), mlsem)
    own.start()
    own_meta.start()
    start(first_leg(pair))
    own.wait()
    own_meta.wait()
    start(to_x(e))
    start(to_core(0, e))
    pack(target[1])
    far(1)
    pack(target[2])
    far(2)

    @pl.when(outer)
    def _():
        relay(0)
        near(1)

    load_w.wait()

    def to_pair(zi, p):
        return remote(
            sendy.at[zi, p], recvy.at[zi, p], ysend.at[zi, p], yrecv.at[zi, p], d, pair
        )

    def from_pair(zi, p):
        remote(
            sendy.at[zi, p], recvy.at[zi, p], ysend.at[zi, p], yrecv.at[zi, p], d, e
        ).wait_recv()

    def partial_sums(ee):
        span = pl.ds(pl.multiple_of(ee * rows, rows), rows)
        told = [mbuf[ee * nd + k].astype(f32).T for k in range(nd)]
        row = lax.broadcasted_iota(jnp.int32, (rows, 1), 0)
        base = jnp.zeros((rows, 1), jnp.int32)
        for k in range(1, nd):
            base = base + jnp.where(row >= k * cap, tokens, 0)
        col = lax.broadcasted_iota(jnp.int32, (rows, group), 1)
        acc = jnp.zeros((group, cols), f32)
        for q in range(po):
            mine = jnp.concatenate([m[q * cap:(q + 1) * cap] for m in told], axis=0)
            hit = col == mine[:, 0:1].astype(jnp.int32) + base
            h = jnp.dot(buf[q, span, :], w[q], preferred_element_type=f32).astype(bf)
            for k in (1, 2):
                acc = acc + lax.dot_general(
                    jnp.where(hit, mine[:, k:k + 1], 0.0).astype(bf), h,
                    (((0,), (0,)), ((), ())), preferred_element_type=f32,
                )
        return acc

    def add_on(s, pieces):
        zs = source(s)
        up = zs > z
        follow = jnp.where(up, z + 1, z - 1)
        place = jnp.where(jnp.logical_and(jnp.logical_not(up), follow == zs), nz, zs)
        beyond = jnp.where(up, z > 0, z < nz - 1)
        for p in pieces:
            cs = pl.ds(p * pc, pc)
            from_pair(zs, p)

            @pl.when(beyond)
            def _():
                remote(
                    sendz.at[zs, p], recvz.at[zs, p], zsend.at[zs, p], zrecv.at[zs, p], d, e
                ).wait_recv()
                sendz[zs, p] = (
                    keep[zs, :, cs] + recvy[zs, p].astype(f32) + recvz[zs, p].astype(f32)
                ).astype(bf)

            @pl.when(jnp.logical_not(beyond))
            def _():
                sendz[zs, p] = (keep[zs, :, cs] + recvy[zs, p].astype(f32)).astype(bf)

            remote(
                sendz.at[zs, p], recvz.at[place, p], zsend.at[zs, p], zrecv.at[place, p],
                d, follow * 2 + y,
            ).start()

    every = tuple(range(np_))

    def owner(n):
        turn = jnp.where(inner, n, jnp.where(n == 0, 0, jnp.where(n == ne - 1, 1, n + 1)))
        ys = jnp.where(
            turn == 0, y, jnp.where(
                turn == 1, 1 - y, jnp.where(
                    lax.rem(turn + jnp.where(turn < SWAP, 1, 0), 2) == 0, 1 - y, y
                ),
            ),
        )
        return source(lax.div(turn, 2)), ys

    def took(part, ee):
        for q in whole[:1] if part == 0 else whole[1:]:
            if q < po:
                came(q, d, ee)
            else:
                meta_came(d, ee)
            start(to_x(ee, (q,)))
            start(to_core(0, ee, (q,)))

    def step(n, carry):
        @pl.when(n < ne)
        def _():
            zs, ys = owner(n)
            took(0, zs * 2 + ys)

        @pl.when(jnp.logical_and(inner, n == 1))
        def _():
            relay(0)
            near(0)

        @pl.when(jnp.logical_and(inner, n == 4))
        def _():
            relay(2)
            near(2)

        @pl.when(jnp.logical_and(outer, n == 3))
        def _():
            relay(1)

        @pl.when(jnp.logical_and(outer, n == 4))
        def _():
            relay(2)
            near(2)

        zs, ys = owner(n - 1)
        ee = zs * 2 + ys
        arrived(across, ee)
        start(to_core(1, ee))

        @pl.when(n < ne)
        def _():
            zn, yn = owner(n)
            took(1, zn * 2 + yn)

        arrived(other, ee)
        arrived(other + across - d, ee)
        acc = partial_sums(ee)

        @pl.when(ys == y)
        def _():
            keep[zs] = acc

        @pl.when(ys != y)
        def _():
            for p in range(np_):
                sendy[zs, p] = acc[:, p * pc:(p + 1) * pc].astype(bf)
                to_pair(zs, p).start()

        @pl.when(jnp.logical_and(inner, n == GATE))
        def _():
            relay(1)
            near(1)

        done = n - 1

        @pl.when(jnp.logical_and(outer, done == AT[0]))
        def _():
            add_on(1, every)

        @pl.when(jnp.logical_and(outer, done == AT[1]))
        def _():
            add_on(2, every)

        @pl.when(jnp.logical_and(inner, done == AT[2]))
        def _():
            add_on(1, every[:np_ // 2])

        @pl.when(jnp.logical_and(inner, done == AT[3]))
        def _():
            add_on(1, every[np_ // 2:])

        return carry

    lax.fori_loop(1, ne + 1, step, 0)

    block = width // nd
    wide = width // 3

    def gram_tiles(low, high):
        @pl.loop(low, high)
        def _(i):
            q = lax.div(i, 3)
            cs = pl.ds(pl.multiple_of(lax.rem(i, 3) * wide, wide), wide)
            g[q, :, cs] = lax.dot_general(
                buf[q, :, pl.ds(pl.multiple_of(d * block, block), block)],
                buf[q, :, cs],
                (((0,), (0,)), ((), ())),
                preferred_element_type=f32,
            )

    @pl.when(outer)
    def _():
        add_on(3, every)

    @pl.when(inner)
    def _():
        add_on(2, every)

    for p in range(np_):
        @pl.when(inner)
        def _():
            add_on(3, (p,))

        gram_tiles(SPLIT[p], SPLIT[p + 1])

    told = jnp.sum(mbuf[...].astype(f32), axis=0)[3:4]
    lane = lax.broadcasted_iota(jnp.int32, (1, META), 1)
    for q in range(po):
        here = jnp.logical_and(lane >= q * cap, lane < (q + 1) * cap)
        c_ref[q] = jnp.broadcast_to(
            jnp.sum(jnp.where(here, told, 0.0), axis=1, keepdims=True), c_ref.shape[1:]
        )

    def to_token(p, k):
        dd = lax.rem(d + k, nd)
        return remote(
            fin.at[p, dd], o_ref.at[:, pl.ds(pl.multiple_of(d * cols + p * pc, pc), pc)],
            osend.at[p, k], orecv.at[p, d], dd, e,
        )

    for p in range(np_):
        gram_tiles(SPLIT[np_ + p], SPLIT[np_ + p + 1])
        cs = pl.ds(p * pc, pc)
        from_pair(z, p)
        keep[z, :, cs] = keep[z, :, cs] + recvy[z, p].astype(f32)
        for there, place in ((z > 0, z), (z < nz - 1, nz)):
            @pl.when(there)
            def _():
                remote(
                    sendz.at[0, p], recvz.at[place, p], zsend.at[0, p], zrecv.at[place, p], d, e
                ).wait_recv()
                keep[z, :, cs] = keep[z, :, cs] + recvz[place, p].astype(f32)
        fin[p] = keep[z, :, cs].astype(bf).reshape(nd, tokens, pc)
        for k in range(1, nd):
            to_token(p, k).start()
        o_ref[:, pl.ds(pl.multiple_of(d * cols + p * pc, pc), pc)] = fin[p, d]

    for p in range(np_):
        for k in range(1, nd):
            dd = lax.rem(d + k, nd)
            remote(
                fin.at[p, dd], o_ref.at[:, pl.ds(pl.multiple_of(dd * cols + p * pc, pc), pc)],
                osend.at[p, k], orecv.at[p, dd], d, e,
            ).wait_recv()

    def drain(k, carry):
        for copies in (to_x(k), to_core(0, k), to_core(1, k)):
            for copy in copies:
                copy.wait_send()
        return carry

    lax.fori_loop(0, ne, drain, 0)

    def drain_z(k, carry):
        for p in range(np_):
            to_pair(k, p).wait_send()

            @pl.when(k != z)
            def _():
                remote(
                    sendz.at[k, p], recvz.at[k, p], zsend.at[k, p], zrecv.at[k, p], d, e
                ).wait_send()

        return carry

    lax.fori_loop(0, nz, drain_z, 0)
    for copy in first_leg(pair):
        copy.wait_send()
    for k in range(nz - 1):
        for copies in (first_leg(target[k] * 2 + y), across_y(k), second_leg(k)):
            for copy in copies:
                copy.wait_send()
    for p in range(np_):
        for k in range(1, nd):
            to_token(p, k).wait_send()


def finish_kernel(steps, c_ref, out_ref, gram_ref, out_done, gram_done, work, osem, gsem):
    copy = pltpu.make_async_copy(out_ref, out_done, osem)
    copy.start()
    po, block, _ = gram_ref.shape
    size = block // steps
    scale = [1.0 / c_ref[q, 0:1, 0:1] for q in range(po)]
    sent = []
    for i in range(steps):
        span = pl.ds(i * size, size)
        for q in range(po):
            work[q, span] = gram_ref[q, span] * scale[q]
        sent.append(pltpu.make_async_copy(work.at[:, span], gram_done.at[:, span], gsem.at[i]))
        sent[i].start()
    copy.wait()
    for one in sent:
        one.wait()


def finish(out, gram, count):
    steps = 6
    any_space = pl.BlockSpec(memory_space=pl.ANY)
    vmem = pl.BlockSpec(memory_space=pltpu.VMEM)
    dma = pltpu.SemaphoreType.DMA
    return pl.pallas_call(
        functools.partial(finish_kernel, steps),
        out_shape=(
            jax.ShapeDtypeStruct(out.shape, out.dtype),
            jax.ShapeDtypeStruct(gram.shape, gram.dtype),
        ),
        in_specs=[vmem, vmem, vmem],
        out_specs=(any_space, any_space),
        scratch_shapes=[pltpu.VMEM(gram.shape, gram.dtype), dma, dma((steps,))],
        compiler_params=pltpu.CompilerParams(vmem_limit_bytes=40 * 2**20),
    )(count, out, gram)


def fused(hidden, routes, gate_scores, down_weight):
    tokens, top, width = hidden.shape
    ne, nd = lax.axis_size("expert"), lax.axis_size("dp")
    po, _, cols = down_weight.shape
    pairs = tokens * top
    cap = 3 * pairs // (2 * ne * po)
    nz, group = ne // 2, nd * tokens
    pc = cols // PIECES
    bf, f32 = jnp.bfloat16, jnp.float32
    dma = pltpu.SemaphoreType.DMA
    any_space = pl.BlockSpec(memory_space=pl.ANY)
    vmem = pl.BlockSpec(memory_space=pltpu.VMEM)
    out, gram, count = pl.pallas_call(
        functools.partial(fused_kernel, nd, ne, top, cap, PIECES),
        out_shape=(
            pltpu.VMEM((tokens, nd * cols), bf),
            pltpu.VMEM((po, width // nd, width), f32),
            pltpu.VMEM((po, 8, 128), f32),
        ),
        in_specs=[any_space, vmem, vmem, any_space],
        out_specs=(vmem, vmem, vmem),
        scratch_shapes=[
            pltpu.VMEM((pairs, width), bf),
            pltpu.VMEM((po, ne * nd * cap, width), bf),
            pltpu.VMEM((ne * nd, 16, META), bf),
            pltpu.VMEM((ne * po, cap, width), bf),
            pltpu.VMEM((ne, 16, META), bf),
            pltpu.VMEM((nz - 1, po, cap, width), bf),
            pltpu.VMEM((nz - 1, 16, META), bf),
            pltpu.VMEM((8, pairs), jnp.int32),
            pltpu.VMEM((16, pairs), bf),
            pltpu.VMEM((po, width, cols), bf),
            pltpu.VMEM((nz, PIECES, group, pc), bf),
            pltpu.VMEM((nz, PIECES, group, pc), bf),
            pltpu.VMEM((nz, group, cols), f32),
            pltpu.VMEM((nz, PIECES, group, pc), bf),
            pltpu.VMEM((nz + 1, PIECES, group, pc), bf),
            pltpu.VMEM((PIECES, nd, tokens, pc), bf),
            dma, dma, dma, dma,
            dma((po, ne)), dma((ne,)), dma((nz - 1,)), dma((nz - 1,)),
            dma((po, nz - 1)), dma((nz - 1,)), dma((nz - 1,)), dma((nz - 1,)),
            dma((po, ne)), dma((ne,)), dma((2, po, ne)), dma((2, ne)),
            dma((po, ne * nd)), dma((ne * nd,)),
            dma((nz, PIECES)), dma((nz, PIECES)), dma((nz, PIECES)), dma((nz + 1, PIECES)),
            dma((PIECES, nd)), dma((PIECES, nd)),
        ],
        compiler_params=pltpu.CompilerParams(
            collective_id=0, has_side_effects=True, vmem_limit_bytes=VMEM_LIMIT
        ),
    )(
        hidden.reshape(pairs, width), routes.T, gate_scores.T, down_weight,
    )
    return finish(out, gram, count)


def earlier(onehot):
    pairs = jnp.arange(onehot.shape[0], dtype=jnp.int32)
    above = (pairs[None, :] < pairs[:, None]).astype(jnp.bfloat16)
    return jnp.dot(
        above, onehot.astype(jnp.bfloat16), preferred_element_type=jnp.float32
    ).astype(jnp.int32)


def plain(hidden, routes, gate_scores, down_weight):
    tokens = hidden.shape[0]
    top_count = hidden.shape[1]
    hidden_width = hidden.shape[2]
    n_owner = lax.axis_size("expert")
    n_group = lax.axis_size("dp")
    per_owner = down_weight.shape[0]
    experts = n_owner * per_owner
    pair_total = tokens * top_count
    capacity = 3 * tokens * top_count // (2 * experts)
    flat_routes = routes.reshape(pair_total)
    onehot = (flat_routes[:, None] == jnp.arange(experts, dtype=jnp.int32)[None, :]).astype(
        jnp.int32
    )
    before = earlier(onehot)
    position = jnp.sum(before * onehot, axis=1)
    slot_index = flat_routes * capacity + position
    local_counts = jnp.sum(onehot, axis=0).astype(jnp.float32)
    totals = lax.psum(local_counts, ("dp", "expert"))
    pair_rows = hidden.reshape(pair_total, hidden_width)
    outgoing = (
        jnp.zeros((experts * capacity, hidden_width), jnp.bfloat16).at[slot_index].set(pair_rows)
    )
    outgoing = outgoing.reshape(n_owner, per_owner, capacity, hidden_width)
    arrived = lax.all_to_all(outgoing, "expert", split_axis=0, concat_axis=0, tiled=True)
    everyone = lax.all_gather(arrived, "dp", axis=0, tiled=True)
    own_counts = lax.dynamic_slice_in_dim(
        totals, lax.axis_index("expert") * per_owner, per_owner, 0
    )
    block_width = hidden_width // n_group
    my_columns = lax.dynamic_slice_in_dim(
        everyone, lax.axis_index("dp") * block_width, block_width, 3
    )
    gram_rows = jnp.einsum(
        "sxcf,sxcg->xfg", my_columns, everyone, preferred_element_type=jnp.float32
    )
    results = jnp.einsum(
        "sxcf,xfd->sxcd", everyone, down_weight, preferred_element_type=jnp.float32
    ).astype(jnp.bfloat16)
    returned = lax.all_to_all(
        lax.all_to_all(results, "dp", split_axis=0, concat_axis=3, tiled=True),
        "expert",
        split_axis=0,
        concat_axis=0,
        tiled=True,
    )
    gram = gram_rows / own_counts[:, None, None]
    model_width = returned.shape[3]
    pair_results = returned.reshape(experts * capacity, model_width)[slot_index]
    scores = gate_scores.astype(jnp.float32)
    weight = scores / jnp.sum(scores, axis=1, keepdims=True)
    combined = jnp.sum(
        pair_results.reshape(tokens, top_count, model_width).astype(jnp.float32)
        * weight[:, :, None],
        axis=1,
    )
    return (combined.astype(jnp.bfloat16), gram)


def fits(hidden, down_weight, nd, ne):
    tokens, top, width = hidden.shape
    po, _, cols = down_weight.shape
    pairs = tokens * top
    cap = 3 * pairs // (2 * ne * po)
    nz, group = ne // 2, nd * tokens
    if nd != 4 or ne != 8 or cap % 16 or po * cap > META or tokens % 16 or tokens > 256:
        return False
    if top & (top - 1) or cols % (PIECES * 128) or width % 768 or po != 2 or (width // nd) % 384 or top != 8:
        return False
    need = (
        2 * po * ne * cap * (nd + 1) * width
        + 2 * po * width * cols
        + nz * group * cols * 12
        + 2 * group * cols * 2
        + 4 * po * (width // nd) * width
        + 6 * pairs * width
        + 8 * group * cols
    )
    return need <= VMEM_BUDGET


def local(hidden, routes, gate_scores, down_weight):
    if fits(hidden, down_weight, lax.axis_size("dp"), lax.axis_size("expert")):
        return fused(hidden, routes, gate_scores, down_weight)
    return plain(hidden, routes, gate_scores, down_weight)


def solution(mesh):
    placed = (
        P(("dp", "expert"), None, None),
        P(("dp", "expert"), None),
        P(("dp", "expert"), None),
        P("expert", None, "dp"),
    )
    return jax.shard_map(
        local,
        mesh=mesh,
        in_specs=placed,
        out_specs=(P(("dp", "expert"), None), P("expert", "dp", None)),
        check_vma=False,
    )
```

```python
import functools

import jax
import jax.numpy as jnp
from jax import lax
from jax.experimental import pallas as pl
from jax.experimental.pallas import tpu as pltpu
from jax.sharding import PartitionSpec as P

MESH = pl.DeviceIdType.MESH
META = 128
PIECES = 4
GATE = 2
SWAP = 4
AT = (4, 6, 5, 6)
SPLIT = (0, 0, 2, 4, 4, 4, 5, 6, 6)
VMEM_BUDGET = 46 * 2**20
VMEM_LIMIT = 52 * 2**20


def fused_kernel(
    nd, ne, top, cap, np_,
    hid_hbm, rt, gt, w_hbm, o_ref, g, c_ref,
    hid, buf, mbuf, og, mog, held, mheld, slot, meta, w, sendy, recvy, keep, sendz, recvz, fin,
    hsem, wsem, lsem, mlsem, asend, msend, fsend, mfsend, hsend, mhsend, hrecv, mhrecv, xsend, mxsend, csend, mcsend, recv, mrecv,
    ysend, yrecv, zsend, zrecv, osend, orecv,
):
    f32, bf = jnp.float32, jnp.bfloat16
    po, width, cols = w.shape
    pairs = hid.shape[0]
    tokens = pairs // top
    nz = ne // 2
    rows = nd * cap
    chunk = po * cap
    group = nd * tokens
    pc = cols // np_
    experts = ne * po
    d = lax.axis_index("dp")
    e = lax.axis_index("expert")
    x, c = lax.div(d, 2), lax.rem(d, 2)
    z, y = lax.div(e, 2), lax.rem(e, 2)
    other = d + 1 - 2 * c
    across = lax.rem(d + 2, nd)
    pair = e + 1 - 2 * y
    inner = jnp.logical_and(z > 0, z < nz - 1)
    outer = jnp.logical_not(inner)

    load_h = pltpu.make_async_copy(hid_hbm, hid, hsem)
    load_h.start()
    load_w = pltpu.make_async_copy(w_hbm, w, wsem)

    barrier = pltpu.get_barrier_semaphore()
    for k in range(1, nz):
        pl.semaphore_signal(
            barrier, inc=1, device_id=(d, lax.rem(e + 2 * k, ne)), device_id_type=MESH
        )
    pl.semaphore_signal(barrier, inc=1, device_id=(d, pair), device_id_type=MESH)
    for k in range(1, nd):
        pl.semaphore_signal(
            barrier, inc=1, device_id=(lax.rem(d + k, nd), e), device_id_type=MESH
        )

    def remote(src, dst, ss, rs, dd, ee):
        return pltpu.make_async_remote_copy(
            src_ref=src, dst_ref=dst, send_sem=ss, recv_sem=rs,
            device_id=(dd, ee), device_id_type=MESH,
        )

    def slot_of(dd, ee):
        return buf.at[:, pl.ds(pl.multiple_of((ee * nd + dd) * cap, cap), cap), :]

    def part_of(q, dd, ee):
        return buf.at[q, pl.ds(pl.multiple_of((ee * nd + dd) * cap, cap), cap), :]

    def meta_of(dd, ee):
        return mbuf.at[ee * nd + dd]

    shift = top.bit_length() - 1
    told = jnp.concatenate([rt[...], gt[...]], axis=0).astype(f32).astype(bf)
    spread = jnp.dot(
        told,
        jnp.where(
            lax.broadcasted_iota(jnp.int32, (tokens, pairs), 0)
            == jnp.right_shift(lax.broadcasted_iota(jnp.int32, (tokens, pairs), 1), shift),
            1.0, 0.0,
        ).astype(bf),
        preferred_element_type=f32,
    )
    choice = lax.broadcasted_iota(jnp.int32, (top, pairs), 0) == jnp.bitwise_and(
        lax.broadcasted_iota(jnp.int32, (top, pairs), 1), top - 1
    )
    route = jnp.sum(jnp.where(choice, spread[:top], 0.0), axis=0, keepdims=True).astype(jnp.int32)
    score = jnp.sum(jnp.where(choice, spread[top:], 0.0), axis=0, keepdims=True)
    weight = score / jnp.sum(spread[top:], axis=0, keepdims=True)
    high = weight.astype(bf).astype(f32)
    set_ = jnp.where(
        lax.broadcasted_iota(jnp.int32, (experts, pairs), 0) == route, 1.0, 0.0
    )
    before = jnp.dot(
        set_.astype(bf),
        jnp.where(
            lax.broadcasted_iota(jnp.int32, (pairs, pairs), 0)
            < lax.broadcasted_iota(jnp.int32, (pairs, pairs), 1),
            1.0, 0.0,
        ).astype(bf),
        preferred_element_type=f32,
    )
    position = jnp.sum(before * set_, axis=0, keepdims=True).astype(jnp.int32)
    slot[...] = jnp.broadcast_to(route * cap + position, slot.shape)
    kind = lax.broadcasted_iota(jnp.int32, (16, pairs), 0)
    token = jnp.right_shift(lax.broadcasted_iota(jnp.int32, (16, pairs), 1), shift)
    meta[...] = jnp.where(
        kind == 0, token.astype(f32),
        jnp.where(kind == 1, high, jnp.where(kind == 2, weight - high, jnp.where(kind == 3, 1.0, 0.0))),
    ).astype(bf)
    load_h.wait()
    load_w.start()

    def pack(zt):
        first = zt * 2 * chunk
        pick = jnp.where(
            lax.broadcasted_iota(jnp.int32, (2 * chunk, pairs), 0) + first == slot[0:1], 1.0, 0.0
        ).astype(bf)
        block = jnp.dot(pick, hid[...], preferred_element_type=f32).astype(bf)
        og[pl.ds(zt * 2 * po, 2 * po)] = block.reshape(2 * po, cap, width)
        for k in range(2):
            pick = jnp.where(
                lax.broadcasted_iota(jnp.int32, (META, pairs), 0) + (first + k * chunk)
                == slot[0:1],
                1.0, 0.0,
            ).astype(bf)
            mog[zt * 2 + k] = lax.dot_general(
                meta[...], pick, (((1,), (1,)), ((), ())), preferred_element_type=f32
            ).astype(bf)

    whole = tuple(range(po + 1))

    def legs(rows_from, meta_from, rows_sem, meta_sem, dd, ee, to_d, to_e, which=whole):
        at = ee * nd + dd
        return tuple(
            remote(rows_from(q), part_of(q, dd, ee), rows_sem(q), recv.at[q, at], to_d, to_e)
            if q < po
            else remote(meta_from, meta_of(dd, ee), meta_sem, mrecv.at[at], to_d, to_e)
            for q in which
        )

    def first_leg(there):
        return legs(
            lambda q: og.at[there * po + q], mog.at[there],
            lambda q: asend.at[q, there], msend.at[there], d, e, d, there,
        )

    def to_x(ee, which=whole):
        return legs(
            lambda q: part_of(q, d, ee), meta_of(d, ee),
            lambda q: xsend.at[q, ee], mxsend.at[ee], d, ee, across, e, which,
        )

    def to_core(j, ee, which=whole):
        dd = d if j == 0 else across
        return legs(
            lambda q: part_of(q, dd, ee), meta_of(dd, ee),
            lambda q: csend.at[j, q, ee], mcsend.at[j, ee], dd, ee, other, e, which,
        )

    def start(copies):
        for copy in copies:
            copy.start()

    def came(q, dd, ee):
        here = part_of(q, dd, ee)
        remote(here, here, asend.at[0, 0], recv.at[q, ee * nd + dd], d, e).wait_recv()

    def meta_came(dd, ee):
        there = meta_of(dd, ee)
        remote(there, there, msend.at[0], mrecv.at[ee * nd + dd], d, e).wait_recv()

    def arrived(dd, ee):
        for q in range(po):
            came(q, dd, ee)
        meta_came(dd, ee)

    def near(k):
        start(first_leg(target[k] * 2 + y))

    def across_y(k):
        there = target[k] * 2 + 1 - y
        return (
            *(
                remote(og.at[there * po + q], held.at[k, q], fsend.at[q, k], hrecv.at[q, k], d, pair)
                for q in range(po)
            ),
            remote(mog.at[there], mheld.at[k], mfsend.at[k], mhrecv.at[k], d, pair),
        )

    def far(k):
        start(across_y(k))

    def second_leg(k, which=whole):
        return legs(
            lambda q: held.at[k, q], mheld.at[k],
            lambda q: hsend.at[q, k], mhsend.at[k], d, pair, d, target[k] * 2 + y, which,
        )

    def relay(k):
        for q in range(po):
            here = held.at[k, q]
            remote(here, here, fsend.at[q, k], hrecv.at[q, k], d, e).wait_recv()
            start(second_leg(k, (q,)))
        remote(mheld.at[k], mheld.at[k], mhsend.at[k], mhrecv.at[k], d, e).wait_recv()
        start(second_leg(k, (po,)))

    target = ((nz - 1) * (1 - lax.rem(z, 2)), lax.rem(z + 2, nz), 1 + lax.rem(z, 2))

    def source(s):
        return jnp.where(
            s == 0, z,
            jnp.where(
                s == 1, (nz - 1) * (1 - lax.div(z, 2)),
                jnp.where(s == 2, z + 1 - 2 * lax.rem(z, 2), 2 - lax.div(z, 2)),
            ),
        )

    pack(target[0])
    pl.semaphore_wait(barrier, nz + nd - 1)
    far(0)

    @pl.when(outer)
    def _():
        near(0)

    pack(z)
    own = pltpu.make_async_copy(og.at[pl.ds(e * po, po)], slot_of(d, e), lsem)
    own_meta = pltpu.make_async_copy(mog.at[e], meta_of(d, e), mlsem)
    own.start()
    own_meta.start()
    start(first_leg(pair))
    own.wait()
    own_meta.wait()
    start(to_x(e))
    start(to_core(0, e))
    pack(target[1])
    far(1)
    pack(target[2])
    far(2)

    @pl.when(outer)
    def _():
        relay(0)
        near(1)

    load_w.wait()

    def to_pair(zi, p):
        return remote(
            sendy.at[zi, p], recvy.at[zi, p], ysend.at[zi, p], yrecv.at[zi, p], d, pair
        )

    def from_pair(zi, p):
        remote(
            sendy.at[zi, p], recvy.at[zi, p], ysend.at[zi, p], yrecv.at[zi, p], d, e
        ).wait_recv()

    def partial_sums(ee):
        span = pl.ds(pl.multiple_of(ee * rows, rows), rows)
        told = [mbuf[ee * nd + k].astype(f32).T for k in range(nd)]
        row = lax.broadcasted_iota(jnp.int32, (rows, 1), 0)
        base = jnp.zeros((rows, 1), jnp.int32)
        for k in range(1, nd):
            base = base + jnp.where(row >= k * cap, tokens, 0)
        col = lax.broadcasted_iota(jnp.int32, (rows, group), 1)
        acc = jnp.zeros((group, cols), f32)
        for q in range(po):
            mine = jnp.concatenate([m[q * cap:(q + 1) * cap] for m in told], axis=0)
            hit = col == mine[:, 0:1].astype(jnp.int32) + base
            h = jnp.dot(buf[q, span, :], w[q], preferred_element_type=f32).astype(bf)
            share = jnp.concatenate(
                [jnp.where(hit, mine[:, k:k + 1], 0.0).astype(bf) for k in (1, 2)], axis=1
            )
            both = lax.dot_general(
                share, h, (((0,), (0,)), ((), ())), preferred_element_type=f32
            )
            acc = acc + (both[:group] + both[group:])
        return acc

    def add_on(s, pieces):
        zs = source(s)
        up = zs > z
        follow = jnp.where(up, z + 1, z - 1)
        place = jnp.where(jnp.logical_and(jnp.logical_not(up), follow == zs), nz, zs)
        beyond = jnp.where(up, z > 0, z < nz - 1)
        for p in pieces:
            cs = pl.ds(p * pc, pc)
            from_pair(zs, p)

            @pl.when(beyond)
            def _():
                remote(
                    sendz.at[zs, p], recvz.at[zs, p], zsend.at[zs, p], zrecv.at[zs, p], d, e
                ).wait_recv()
                sendz[zs, p] = (
                    keep[zs, :, cs] + recvy[zs, p].astype(f32) + recvz[zs, p].astype(f32)
                ).astype(bf)

            @pl.when(jnp.logical_not(beyond))
            def _():
                sendz[zs, p] = (keep[zs, :, cs] + recvy[zs, p].astype(f32)).astype(bf)

            remote(
                sendz.at[zs, p], recvz.at[place, p], zsend.at[zs, p], zrecv.at[place, p],
                d, follow * 2 + y,
            ).start()

    every = tuple(range(np_))

    def owner(n):
        turn = jnp.where(inner, n, jnp.where(n == 0, 0, jnp.where(n == ne - 1, 1, n + 1)))
        ys = jnp.where(
            turn == 0, y, jnp.where(
                turn == 1, 1 - y, jnp.where(
                    lax.rem(turn + jnp.where(turn < SWAP, 1, 0), 2) == 0, 1 - y, y
                ),
            ),
        )
        return source(lax.div(turn, 2)), ys

    def took(part, ee):
        for q in whole[:1] if part == 0 else whole[1:]:
            if q < po:
                came(q, d, ee)
            else:
                meta_came(d, ee)
            start(to_x(ee, (q,)))
            start(to_core(0, ee, (q,)))

    def step(n, carry):
        @pl.when(n < ne)
        def _():
            zs, ys = owner(n)
            took(0, zs * 2 + ys)

        @pl.when(jnp.logical_and(inner, n == 1))
        def _():
            relay(0)
            near(0)

        @pl.when(jnp.logical_and(inner, n == 4))
        def _():
            relay(2)
            near(2)

        @pl.when(jnp.logical_and(outer, n == 3))
        def _():
            relay(1)

        @pl.when(jnp.logical_and(outer, n == 4))
        def _():
            relay(2)
            near(2)

        zs, ys = owner(n - 1)
        ee = zs * 2 + ys
        arrived(across, ee)
        start(to_core(1, ee))

        @pl.when(n < ne)
        def _():
            zn, yn = owner(n)
            took(1, zn * 2 + yn)

        arrived(other, ee)
        arrived(other + across - d, ee)
        acc = partial_sums(ee)

        @pl.when(ys == y)
        def _():
            keep[zs] = acc

        @pl.when(ys != y)
        def _():
            for p in range(np_):
                sendy[zs, p] = acc[:, p * pc:(p + 1) * pc].astype(bf)
                to_pair(zs, p).start()

        @pl.when(jnp.logical_and(inner, n == GATE))
        def _():
            relay(1)
            near(1)

        done = n - 1

        @pl.when(jnp.logical_and(outer, done == AT[0]))
        def _():
            add_on(1, every)

        @pl.when(jnp.logical_and(outer, done == AT[1]))
        def _():
            add_on(2, every)

        @pl.when(jnp.logical_and(inner, done == AT[2]))
        def _():
            add_on(1, every[:np_ // 2])

        @pl.when(jnp.logical_and(inner, done == AT[3]))
        def _():
            add_on(1, every[np_ // 2:])

        return carry

    lax.fori_loop(1, ne + 1, step, 0)

    block = width // nd
    wide = width // 3

    def gram_tiles(low, high):
        @pl.loop(low, high)
        def _(i):
            q = lax.div(i, 3)
            cs = pl.ds(pl.multiple_of(lax.rem(i, 3) * wide, wide), wide)
            g[q, :, cs] = lax.dot_general(
                buf[q, :, pl.ds(pl.multiple_of(d * block, block), block)],
                buf[q, :, cs],
                (((0,), (0,)), ((), ())),
                preferred_element_type=f32,
            )

    @pl.when(outer)
    def _():
        add_on(3, every)

    @pl.when(inner)
    def _():
        add_on(2, every)

    for p in range(np_):
        @pl.when(inner)
        def _():
            add_on(3, (p,))

        gram_tiles(SPLIT[p], SPLIT[p + 1])

    def drain(k, carry):
        for copies in (to_x(k), to_core(0, k), to_core(1, k)):
            for copy in copies:
                copy.wait_send()
        return carry

    lax.fori_loop(0, ne, drain, 0)

    for copy in first_leg(pair):
        copy.wait_send()
    for k in range(nz - 1):
        for copies in (first_leg(target[k] * 2 + y), across_y(k), second_leg(k)):
            for copy in copies:
                copy.wait_send()
    told = jnp.sum(mbuf[...].astype(f32), axis=0)[3:4]
    lane = lax.broadcasted_iota(jnp.int32, (1, META), 1)
    for q in range(po):
        here = jnp.logical_and(lane >= q * cap, lane < (q + 1) * cap)
        c_ref[q] = jnp.broadcast_to(
            jnp.sum(jnp.where(here, told, 0.0), axis=1, keepdims=True), c_ref.shape[1:]
        )

    def to_token(p, k):
        dd = lax.rem(d + (2, 3, 1)[k - 1], nd)
        return remote(
            fin.at[p, dd], o_ref.at[:, pl.ds(pl.multiple_of(d * cols + p * pc, pc), pc)],
            osend.at[p, k], orecv.at[p, d], dd, e,
        )

    for p in range(np_):
        gram_tiles(SPLIT[np_ + p], SPLIT[np_ + p + 1])
        cs = pl.ds(p * pc, pc)
        from_pair(z, p)
        keep[z, :, cs] = keep[z, :, cs] + recvy[z, p].astype(f32)
        for there, place in ((z > 0, z), (z < nz - 1, nz)):
            @pl.when(there)
            def _():
                remote(
                    sendz.at[0, p], recvz.at[place, p], zsend.at[0, p], zrecv.at[place, p], d, e
                ).wait_recv()
                keep[z, :, cs] = keep[z, :, cs] + recvz[place, p].astype(f32)
        fin[p] = keep[z, :, cs].astype(bf).reshape(nd, tokens, pc)
        for k in range(1, nd):
            to_token(p, k).start()
        o_ref[:, pl.ds(pl.multiple_of(d * cols + p * pc, pc), pc)] = fin[p, d]

    for p in range(np_):
        for k in range(1, nd):
            dd = lax.rem(d + (2, 3, 1)[k - 1], nd)
            remote(
                fin.at[p, dd], o_ref.at[:, pl.ds(pl.multiple_of(dd * cols + p * pc, pc), pc)],
                osend.at[p, k], orecv.at[p, dd], d, e,
            ).wait_recv()

    def drain_z(k, carry):
        for p in range(np_):
            to_pair(k, p).wait_send()

            @pl.when(k != z)
            def _():
                remote(
                    sendz.at[k, p], recvz.at[k, p], zsend.at[k, p], zrecv.at[k, p], d, e
                ).wait_send()

        return carry

    lax.fori_loop(0, nz, drain_z, 0)
    for p in range(np_):
        for k in range(1, nd):
            to_token(p, k).wait_send()


def finish_kernel(steps, c_ref, out_ref, gram_ref, out_done, gram_done, work, osem, gsem):
    copy = pltpu.make_async_copy(out_ref, out_done, osem)
    copy.start()
    po, block, _ = gram_ref.shape
    size = block // steps
    scale = [1.0 / c_ref[q, 0:1, 0:1] for q in range(po)]
    sent = []
    for i in range(steps):
        span = pl.ds(i * size, size)
        for q in range(po):
            work[q, span] = gram_ref[q, span] * scale[q]
        sent.append(pltpu.make_async_copy(work.at[:, span], gram_done.at[:, span], gsem.at[i]))
        sent[i].start()
    copy.wait()
    for one in sent:
        one.wait()


def finish(out, gram, count):
    steps = 6
    any_space = pl.BlockSpec(memory_space=pl.ANY)
    vmem = pl.BlockSpec(memory_space=pltpu.VMEM)
    dma = pltpu.SemaphoreType.DMA
    return pl.pallas_call(
        functools.partial(finish_kernel, steps),
        out_shape=(
            jax.ShapeDtypeStruct(out.shape, out.dtype),
            jax.ShapeDtypeStruct(gram.shape, gram.dtype),
        ),
        in_specs=[vmem, vmem, vmem],
        out_specs=(any_space, any_space),
        scratch_shapes=[pltpu.VMEM(gram.shape, gram.dtype), dma, dma((steps,))],
        compiler_params=pltpu.CompilerParams(vmem_limit_bytes=40 * 2**20),
    )(count, out, gram)


def fused(hidden, routes, gate_scores, down_weight):
    tokens, top, width = hidden.shape
    ne, nd = lax.axis_size("expert"), lax.axis_size("dp")
    po, _, cols = down_weight.shape
    pairs = tokens * top
    cap = 3 * pairs // (2 * ne * po)
    nz, group = ne // 2, nd * tokens
    pc = cols // PIECES
    bf, f32 = jnp.bfloat16, jnp.float32
    dma = pltpu.SemaphoreType.DMA
    any_space = pl.BlockSpec(memory_space=pl.ANY)
    vmem = pl.BlockSpec(memory_space=pltpu.VMEM)
    out, gram, count = pl.pallas_call(
        functools.partial(fused_kernel, nd, ne, top, cap, PIECES),
        out_shape=(
            pltpu.VMEM((tokens, nd * cols), bf),
            pltpu.VMEM((po, width // nd, width), f32),
            pltpu.VMEM((po, 8, 128), f32),
        ),
        in_specs=[any_space, vmem, vmem, any_space],
        out_specs=(vmem, vmem, vmem),
        scratch_shapes=[
            pltpu.VMEM((pairs, width), bf),
            pltpu.VMEM((po, ne * nd * cap, width), bf),
            pltpu.VMEM((ne * nd, 16, META), bf),
            pltpu.VMEM((ne * po, cap, width), bf),
            pltpu.VMEM((ne, 16, META), bf),
            pltpu.VMEM((nz - 1, po, cap, width), bf),
            pltpu.VMEM((nz - 1, 16, META), bf),
            pltpu.VMEM((8, pairs), jnp.int32),
            pltpu.VMEM((16, pairs), bf),
            pltpu.VMEM((po, width, cols), bf),
            pltpu.VMEM((nz, PIECES, group, pc), bf),
            pltpu.VMEM((nz, PIECES, group, pc), bf),
            pltpu.VMEM((nz, group, cols), f32),
            pltpu.VMEM((nz, PIECES, group, pc), bf),
            pltpu.VMEM((nz + 1, PIECES, group, pc), bf),
            pltpu.VMEM((PIECES, nd, tokens, pc), bf),
            dma, dma, dma, dma,
            dma((po, ne)), dma((ne,)), dma((po, nz - 1)), dma((nz - 1,)),
            dma((po, nz - 1)), dma((nz - 1,)), dma((po, nz - 1)), dma((nz - 1,)),
            dma((po, ne)), dma((ne,)), dma((2, po, ne)), dma((2, ne)),
            dma((po, ne * nd)), dma((ne * nd,)),
            dma((nz, PIECES)), dma((nz, PIECES)), dma((nz, PIECES)), dma((nz + 1, PIECES)),
            dma((PIECES, nd)), dma((PIECES, nd)),
        ],
        compiler_params=pltpu.CompilerParams(
            collective_id=0, has_side_effects=True, vmem_limit_bytes=VMEM_LIMIT
        ),
    )(
        hidden.reshape(pairs, width), routes.T, gate_scores.T, down_weight,
    )
    return finish(out, gram, count)


def earlier(onehot):
    pairs = jnp.arange(onehot.shape[0], dtype=jnp.int32)
    above = (pairs[None, :] < pairs[:, None]).astype(jnp.bfloat16)
    return jnp.dot(
        above, onehot.astype(jnp.bfloat16), preferred_element_type=jnp.float32
    ).astype(jnp.int32)


def plain(hidden, routes, gate_scores, down_weight):
    tokens = hidden.shape[0]
    top_count = hidden.shape[1]
    hidden_width = hidden.shape[2]
    n_owner = lax.axis_size("expert")
    n_group = lax.axis_size("dp")
    per_owner = down_weight.shape[0]
    experts = n_owner * per_owner
    pair_total = tokens * top_count
    capacity = 3 * tokens * top_count // (2 * experts)
    flat_routes = routes.reshape(pair_total)
    onehot = (flat_routes[:, None] == jnp.arange(experts, dtype=jnp.int32)[None, :]).astype(
        jnp.int32
    )
    before = earlier(onehot)
    position = jnp.sum(before * onehot, axis=1)
    slot_index = flat_routes * capacity + position
    local_counts = jnp.sum(onehot, axis=0).astype(jnp.float32)
    totals = lax.psum(local_counts, ("dp", "expert"))
    pair_rows = hidden.reshape(pair_total, hidden_width)
    outgoing = (
        jnp.zeros((experts * capacity, hidden_width), jnp.bfloat16).at[slot_index].set(pair_rows)
    )
    outgoing = outgoing.reshape(n_owner, per_owner, capacity, hidden_width)
    arrived = lax.all_to_all(outgoing, "expert", split_axis=0, concat_axis=0, tiled=True)
    everyone = lax.all_gather(arrived, "dp", axis=0, tiled=True)
    own_counts = lax.dynamic_slice_in_dim(
        totals, lax.axis_index("expert") * per_owner, per_owner, 0
    )
    block_width = hidden_width // n_group
    my_columns = lax.dynamic_slice_in_dim(
        everyone, lax.axis_index("dp") * block_width, block_width, 3
    )
    gram_rows = jnp.einsum(
        "sxcf,sxcg->xfg", my_columns, everyone, preferred_element_type=jnp.float32
    )
    results = jnp.einsum(
        "sxcf,xfd->sxcd", everyone, down_weight, preferred_element_type=jnp.float32
    ).astype(jnp.bfloat16)
    returned = lax.all_to_all(
        lax.all_to_all(results, "dp", split_axis=0, concat_axis=3, tiled=True),
        "expert",
        split_axis=0,
        concat_axis=0,
        tiled=True,
    )
    gram = gram_rows / own_counts[:, None, None]
    model_width = returned.shape[3]
    pair_results = returned.reshape(experts * capacity, model_width)[slot_index]
    scores = gate_scores.astype(jnp.float32)
    weight = scores / jnp.sum(scores, axis=1, keepdims=True)
    combined = jnp.sum(
        pair_results.reshape(tokens, top_count, model_width).astype(jnp.float32)
        * weight[:, :, None],
        axis=1,
    )
    return (combined.astype(jnp.bfloat16), gram)


def fits(hidden, down_weight, nd, ne):
    tokens, top, width = hidden.shape
    po, _, cols = down_weight.shape
    pairs = tokens * top
    cap = 3 * pairs // (2 * ne * po)
    nz, group = ne // 2, nd * tokens
    if nd != 4 or ne != 8 or cap % 16 or po * cap > META or tokens % 16 or tokens > 256:
        return False
    if top & (top - 1) or cols % (PIECES * 128) or width % 768 or po != 2 or (width // nd) % 384 or top != 8:
        return False
    need = (
        2 * po * ne * cap * (nd + 1) * width
        + 2 * po * width * cols
        + nz * group * cols * 12
        + 2 * group * cols * 2
        + 4 * po * (width // nd) * width
        + 6 * pairs * width
        + 8 * group * cols
    )
    return need <= VMEM_BUDGET


def local(hidden, routes, gate_scores, down_weight):
    if fits(hidden, down_weight, lax.axis_size("dp"), lax.axis_size("expert")):
        return fused(hidden, routes, gate_scores, down_weight)
    return plain(hidden, routes, gate_scores, down_weight)


def solution(mesh):
    placed = (
        P(("dp", "expert"), None, None),
        P(("dp", "expert"), None),
        P(("dp", "expert"), None),
        P("expert", None, "dp"),
    )
    return jax.shard_map(
        local,
        mesh=mesh,
        in_specs=placed,
        out_specs=(P(("dp", "expert"), None), P("expert", "dp", None)),
        check_vma=False,
    )
```

```python
import functools

import jax
import jax.numpy as jnp
from jax import lax
from jax.experimental import pallas as pl
from jax.experimental.pallas import tpu as pltpu
from jax.sharding import PartitionSpec as P

MESH = pl.DeviceIdType.MESH
META = 128
PIECES = 4
GATE = 2
SWAP = 4
AT = (4, 6, 5, 6)
SPLIT = (0, 0, 2, 4, 4, 4, 5, 6, 6)
VMEM_BUDGET = 46 * 2**20
VMEM_LIMIT = 52 * 2**20


def fused_kernel(
    nd, ne, top, cap, np_,
    hid_hbm, rt, gt, w_hbm, o_ref, g, c_ref,
    hid, buf, mbuf, og, mog, held, mheld, slot, meta, w, sendy, recvy, keep, sendz, recvz, fin,
    hsem, wsem, lsem, mlsem, asend, msend, fsend, mfsend, hsend, mhsend, hrecv, mhrecv, xsend, mxsend, csend, mcsend, recv, mrecv,
    ysend, yrecv, zsend, zrecv, osend, orecv,
):
    f32, bf = jnp.float32, jnp.bfloat16
    po, width, cols = w.shape
    pairs = hid.shape[0]
    tokens = pairs // top
    nz = ne // 2
    rows = nd * cap
    chunk = po * cap
    group = nd * tokens
    pc = cols // np_
    experts = ne * po
    d = lax.axis_index("dp")
    e = lax.axis_index("expert")
    x, c = lax.div(d, 2), lax.rem(d, 2)
    z, y = lax.div(e, 2), lax.rem(e, 2)
    other = d + 1 - 2 * c
    across = lax.rem(d + 2, nd)
    pair = e + 1 - 2 * y
    inner = jnp.logical_and(z > 0, z < nz - 1)
    outer = jnp.logical_not(inner)

    load_h = pltpu.make_async_copy(hid_hbm, hid, hsem)
    load_h.start()
    load_w = pltpu.make_async_copy(w_hbm, w, wsem)

    barrier = pltpu.get_barrier_semaphore()
    for k in range(1, nz):
        pl.semaphore_signal(
            barrier, inc=1, device_id=(d, lax.rem(e + 2 * k, ne)), device_id_type=MESH
        )
    pl.semaphore_signal(barrier, inc=1, device_id=(d, pair), device_id_type=MESH)
    for k in range(1, nd):
        pl.semaphore_signal(
            barrier, inc=1, device_id=(lax.rem(d + k, nd), e), device_id_type=MESH
        )

    def remote(src, dst, ss, rs, dd, ee):
        return pltpu.make_async_remote_copy(
            src_ref=src, dst_ref=dst, send_sem=ss, recv_sem=rs,
            device_id=(dd, ee), device_id_type=MESH,
        )

    def slot_of(dd, ee):
        return buf.at[:, pl.ds(pl.multiple_of((ee * nd + dd) * cap, cap), cap), :]

    def part_of(q, dd, ee):
        return buf.at[q, pl.ds(pl.multiple_of((ee * nd + dd) * cap, cap), cap), :]

    def meta_of(dd, ee):
        return mbuf.at[ee * nd + dd]

    shift = top.bit_length() - 1
    told = jnp.concatenate([rt[...], gt[...]], axis=0).astype(f32).astype(bf)
    spread = jnp.dot(
        told,
        jnp.where(
            lax.broadcasted_iota(jnp.int32, (tokens, pairs), 0)
            == jnp.right_shift(lax.broadcasted_iota(jnp.int32, (tokens, pairs), 1), shift),
            1.0, 0.0,
        ).astype(bf),
        preferred_element_type=f32,
    )
    choice = lax.broadcasted_iota(jnp.int32, (top, pairs), 0) == jnp.bitwise_and(
        lax.broadcasted_iota(jnp.int32, (top, pairs), 1), top - 1
    )
    route = jnp.sum(jnp.where(choice, spread[:top], 0.0), axis=0, keepdims=True).astype(jnp.int32)
    score = jnp.sum(jnp.where(choice, spread[top:], 0.0), axis=0, keepdims=True)
    weight = score / jnp.sum(spread[top:], axis=0, keepdims=True)
    high = weight.astype(bf).astype(f32)
    set_ = jnp.where(
        lax.broadcasted_iota(jnp.int32, (experts, pairs), 0) == route, 1.0, 0.0
    )
    before = jnp.dot(
        set_.astype(bf),
        jnp.where(
            lax.broadcasted_iota(jnp.int32, (pairs, pairs), 0)
            < lax.broadcasted_iota(jnp.int32, (pairs, pairs), 1),
            1.0, 0.0,
        ).astype(bf),
        preferred_element_type=f32,
    )
    position = jnp.sum(before * set_, axis=0, keepdims=True).astype(jnp.int32)
    slot[...] = jnp.broadcast_to(route * cap + position, slot.shape)
    kind = lax.broadcasted_iota(jnp.int32, (16, pairs), 0)
    token = jnp.right_shift(lax.broadcasted_iota(jnp.int32, (16, pairs), 1), shift)
    meta[...] = jnp.where(
        kind == 0, token.astype(f32),
        jnp.where(kind == 1, high, jnp.where(kind == 2, weight - high, jnp.where(kind == 3, 1.0, 0.0))),
    ).astype(bf)
    load_h.wait()
    load_w.start()

    def pack(zt):
        first = zt * 2 * chunk
        pick = jnp.where(
            lax.broadcasted_iota(jnp.int32, (2 * chunk, pairs), 0) + first == slot[0:1], 1.0, 0.0
        ).astype(bf)
        block = jnp.dot(pick, hid[...], preferred_element_type=f32).astype(bf)
        og[pl.ds(zt * 2 * po, 2 * po)] = block.reshape(2 * po, cap, width)
        for k in range(2):
            pick = jnp.where(
                lax.broadcasted_iota(jnp.int32, (META, pairs), 0) + (first + k * chunk)
                == slot[0:1],
                1.0, 0.0,
            ).astype(bf)
            mog[zt * 2 + k] = lax.dot_general(
                meta[...], pick, (((1,), (1,)), ((), ())), preferred_element_type=f32
            ).astype(bf)

    whole = tuple(range(po + 1))

    def legs(rows_from, meta_from, rows_sem, meta_sem, dd, ee, to_d, to_e, which=whole):
        at = ee * nd + dd
        return tuple(
            remote(rows_from(q), part_of(q, dd, ee), rows_sem(q), recv.at[q, at], to_d, to_e)
            if q < po
            else remote(meta_from, meta_of(dd, ee), meta_sem, mrecv.at[at], to_d, to_e)
            for q in which
        )

    def first_leg(there):
        return legs(
            lambda q: og.at[there * po + q], mog.at[there],
            lambda q: asend.at[q, there], msend.at[there], d, e, d, there,
        )

    def to_x(ee, which=whole):
        return legs(
            lambda q: part_of(q, d, ee), meta_of(d, ee),
            lambda q: xsend.at[q, ee], mxsend.at[ee], d, ee, across, e, which,
        )

    def to_core(j, ee, which=whole):
        dd = d if j == 0 else across
        return legs(
            lambda q: part_of(q, dd, ee), meta_of(dd, ee),
            lambda q: csend.at[j, q, ee], mcsend.at[j, ee], dd, ee, other, e, which,
        )

    def start(copies):
        for copy in copies:
            copy.start()

    def came(q, dd, ee):
        here = part_of(q, dd, ee)
        remote(here, here, asend.at[0, 0], recv.at[q, ee * nd + dd], d, e).wait_recv()

    def meta_came(dd, ee):
        there = meta_of(dd, ee)
        remote(there, there, msend.at[0], mrecv.at[ee * nd + dd], d, e).wait_recv()

    def arrived(dd, ee):
        for q in range(po):
            came(q, dd, ee)
        meta_came(dd, ee)

    def near(k):
        start(first_leg(target[k] * 2 + y))

    def across_y(k):
        there = target[k] * 2 + 1 - y
        return (
            *(
                remote(og.at[there * po + q], held.at[k, q], fsend.at[q, k], hrecv.at[q, k], d, pair)
                for q in range(po)
            ),
            remote(mog.at[there], mheld.at[k], mfsend.at[k], mhrecv.at[k], d, pair),
        )

    def far(k):
        start(across_y(k))

    def second_leg(k, which=whole):
        return legs(
            lambda q: held.at[k, q], mheld.at[k],
            lambda q: hsend.at[q, k], mhsend.at[k], d, pair, d, target[k] * 2 + y, which,
        )

    def relay(k):
        for q in range(po):
            here = held.at[k, q]
            remote(here, here, fsend.at[q, k], hrecv.at[q, k], d, e).wait_recv()
            start(second_leg(k, (q,)))
        remote(mheld.at[k], mheld.at[k], mhsend.at[k], mhrecv.at[k], d, e).wait_recv()
        start(second_leg(k, (po,)))

    target = ((nz - 1) * (1 - lax.rem(z, 2)), lax.rem(z + 2, nz), 1 + lax.rem(z, 2))

    def source(s):
        return jnp.where(
            s == 0, z,
            jnp.where(
                s == 1, (nz - 1) * (1 - lax.div(z, 2)),
                jnp.where(s == 2, z + 1 - 2 * lax.rem(z, 2), 2 - lax.div(z, 2)),
            ),
        )

    pack(target[0])
    pl.semaphore_wait(barrier, nz + nd - 1)
    far(0)

    @pl.when(outer)
    def _():
        near(0)

    pack(z)
    own = pltpu.make_async_copy(og.at[pl.ds(e * po, po)], slot_of(d, e), lsem)
    own_meta = pltpu.make_async_copy(mog.at[e], meta_of(d, e), mlsem)
    own.start()
    own_meta.start()

    @pl.when(inner)
    def _():
        start(first_leg(pair))

    own.wait()
    own_meta.wait()
    start(to_x(e))
    start(to_core(0, e))
    pack(target[1])
    far(1)
    pack(target[2])
    far(2)

    @pl.when(outer)
    def _():
        start(first_leg(pair))
        relay(0)
        near(1)

    load_w.wait()

    def to_pair(zi, p):
        return remote(
            sendy.at[zi, p], recvy.at[zi, p], ysend.at[zi, p], yrecv.at[zi, p], d, pair
        )

    def from_pair(zi, p):
        remote(
            sendy.at[zi, p], recvy.at[zi, p], ysend.at[zi, p], yrecv.at[zi, p], d, e
        ).wait_recv()

    def partial_sums(ee):
        span = pl.ds(pl.multiple_of(ee * rows, rows), rows)
        told = [mbuf[ee * nd + k].astype(f32).T for k in range(nd)]
        row = lax.broadcasted_iota(jnp.int32, (rows, 1), 0)
        base = jnp.zeros((rows, 1), jnp.int32)
        for k in range(1, nd):
            base = base + jnp.where(row >= k * cap, tokens, 0)
        col = lax.broadcasted_iota(jnp.int32, (rows, group), 1)
        acc = jnp.zeros((group, cols), f32)
        for q in range(po):
            mine = jnp.concatenate([m[q * cap:(q + 1) * cap] for m in told], axis=0)
            hit = col == mine[:, 0:1].astype(jnp.int32) + base
            h = jnp.dot(buf[q, span, :], w[q], preferred_element_type=f32).astype(bf)
            share = jnp.concatenate(
                [jnp.where(hit, mine[:, k:k + 1], 0.0).astype(bf) for k in (1, 2)], axis=1
            )
            both = lax.dot_general(
                share, h, (((0,), (0,)), ((), ())), preferred_element_type=f32
            )
            acc = acc + (both[:group] + both[group:])
        return acc

    def add_on(s, pieces):
        zs = source(s)
        up = zs > z
        follow = jnp.where(up, z + 1, z - 1)
        place = jnp.where(jnp.logical_and(jnp.logical_not(up), follow == zs), nz, zs)
        beyond = jnp.where(up, z > 0, z < nz - 1)
        for p in pieces:
            cs = pl.ds(p * pc, pc)
            from_pair(zs, p)

            @pl.when(beyond)
            def _():
                remote(
                    sendz.at[zs, p], recvz.at[zs, p], zsend.at[zs, p], zrecv.at[zs, p], d, e
                ).wait_recv()
                sendz[zs, p] = (
                    keep[zs, :, cs] + recvy[zs, p].astype(f32) + recvz[zs, p].astype(f32)
                ).astype(bf)

            @pl.when(jnp.logical_not(beyond))
            def _():
                sendz[zs, p] = (keep[zs, :, cs] + recvy[zs, p].astype(f32)).astype(bf)

            remote(
                sendz.at[zs, p], recvz.at[place, p], zsend.at[zs, p], zrecv.at[place, p],
                d, follow * 2 + y,
            ).start()

    every = tuple(range(np_))

    def owner(n):
        turn = jnp.where(inner, n, jnp.where(n == 0, 0, jnp.where(n == ne - 1, 1, n + 1)))
        ys = jnp.where(
            turn == 0, y, jnp.where(
                turn == 1, 1 - y, jnp.where(
                    lax.rem(turn + jnp.where(turn < SWAP, 1, 0), 2) == 0, 1 - y, y
                ),
            ),
        )
        return source(lax.div(turn, 2)), ys

    def took(part, ee):
        for q in whole[:1] if part == 0 else whole[1:]:
            if q < po:
                came(q, d, ee)
            else:
                meta_came(d, ee)
            start(to_x(ee, (q,)))
            start(to_core(0, ee, (q,)))

    def step(n, carry):
        @pl.when(n < ne)
        def _():
            zs, ys = owner(n)
            took(0, zs * 2 + ys)

        @pl.when(jnp.logical_and(inner, n == 1))
        def _():
            relay(0)
            near(0)

        @pl.when(jnp.logical_and(inner, n == 4))
        def _():
            relay(2)
            near(2)

        @pl.when(jnp.logical_and(outer, n == 3))
        def _():
            relay(1)

        @pl.when(jnp.logical_and(outer, n == 4))
        def _():
            relay(2)
            near(2)

        zs, ys = owner(n - 1)
        ee = zs * 2 + ys
        arrived(across, ee)
        start(to_core(1, ee))

        @pl.when(n < ne)
        def _():
            zn, yn = owner(n)
            took(1, zn * 2 + yn)

        arrived(other, ee)
        arrived(other + across - d, ee)
        acc = partial_sums(ee)

        @pl.when(ys == y)
        def _():
            keep[zs] = acc

        @pl.when(ys != y)
        def _():
            for p in range(np_):
                sendy[zs, p] = acc[:, p * pc:(p + 1) * pc].astype(bf)
                to_pair(zs, p).start()

        @pl.when(jnp.logical_and(inner, n == GATE))
        def _():
            relay(1)
            near(1)

        done = n - 1

        @pl.when(jnp.logical_and(outer, done == AT[0]))
        def _():
            add_on(1, every)

        @pl.when(jnp.logical_and(outer, done == AT[1]))
        def _():
            add_on(2, every)

        @pl.when(jnp.logical_and(inner, done == AT[2]))
        def _():
            add_on(1, every[:np_ // 2])

        @pl.when(jnp.logical_and(inner, done == AT[3]))
        def _():
            add_on(1, every[np_ // 2:])

        return carry

    lax.fori_loop(1, ne + 1, step, 0)

    block = width // nd
    wide = width // 3

    def gram_tiles(low, high):
        @pl.loop(low, high)
        def _(i):
            q = lax.div(i, 3)
            cs = pl.ds(pl.multiple_of(lax.rem(i, 3) * wide, wide), wide)
            g[q, :, cs] = lax.dot_general(
                buf[q, :, pl.ds(pl.multiple_of(d * block, block), block)],
                buf[q, :, cs],
                (((0,), (0,)), ((), ())),
                preferred_element_type=f32,
            )

    @pl.when(outer)
    def _():
        add_on(3, every)

    @pl.when(inner)
    def _():
        add_on(2, every)

    for p in range(np_):
        @pl.when(inner)
        def _():
            add_on(3, (p,))

        gram_tiles(SPLIT[p], SPLIT[p + 1])

    def drain(k, carry):
        for copies in (to_x(k), to_core(0, k), to_core(1, k)):
            for copy in copies:
                copy.wait_send()
        return carry

    lax.fori_loop(0, ne, drain, 0)

    for copy in first_leg(pair):
        copy.wait_send()
    for k in range(nz - 1):
        for copies in (first_leg(target[k] * 2 + y), across_y(k), second_leg(k)):
            for copy in copies:
                copy.wait_send()
    told = jnp.sum(mbuf[...].astype(f32), axis=0)[3:4]
    lane = lax.broadcasted_iota(jnp.int32, (1, META), 1)
    for q in range(po):
        here = jnp.logical_and(lane >= q * cap, lane < (q + 1) * cap)
        c_ref[q] = jnp.broadcast_to(
            jnp.sum(jnp.where(here, told, 0.0), axis=1, keepdims=True), c_ref.shape[1:]
        )

    def to_token(p, k):
        dd = lax.rem(d + (2, 3, 1)[k - 1], nd)
        return remote(
            fin.at[p, dd], o_ref.at[:, pl.ds(pl.multiple_of(d * cols + p * pc, pc), pc)],
            osend.at[p, k], orecv.at[p, d], dd, e,
        )

    for p in range(np_):
        gram_tiles(SPLIT[np_ + p], SPLIT[np_ + p + 1])
        cs = pl.ds(p * pc, pc)
        from_pair(z, p)
        keep[z, :, cs] = keep[z, :, cs] + recvy[z, p].astype(f32)
        for there, place in ((z > 0, z), (z < nz - 1, nz)):
            @pl.when(there)
            def _():
                remote(
                    sendz.at[0, p], recvz.at[place, p], zsend.at[0, p], zrecv.at[place, p], d, e
                ).wait_recv()
                keep[z, :, cs] = keep[z, :, cs] + recvz[place, p].astype(f32)
        fin[p] = keep[z, :, cs].astype(bf).reshape(nd, tokens, pc)
        for k in range(1, nd):
            to_token(p, k).start()
        o_ref[:, pl.ds(pl.multiple_of(d * cols + p * pc, pc), pc)] = fin[p, d]

    for p in range(np_):
        for k in range(1, nd):
            dd = lax.rem(d + (2, 3, 1)[k - 1], nd)
            remote(
                fin.at[p, dd], o_ref.at[:, pl.ds(pl.multiple_of(dd * cols + p * pc, pc), pc)],
                osend.at[p, k], orecv.at[p, dd], d, e,
            ).wait_recv()

    def drain_z(k, carry):
        for p in range(np_):
            to_pair(k, p).wait_send()

            @pl.when(k != z)
            def _():
                remote(
                    sendz.at[k, p], recvz.at[k, p], zsend.at[k, p], zrecv.at[k, p], d, e
                ).wait_send()

        return carry

    lax.fori_loop(0, nz, drain_z, 0)
    for p in range(np_):
        for k in range(1, nd):
            to_token(p, k).wait_send()


def finish_kernel(steps, c_ref, out_ref, gram_ref, out_done, gram_done, work, osem, gsem):
    copy = pltpu.make_async_copy(out_ref, out_done, osem)
    copy.start()
    po, block, _ = gram_ref.shape
    size = block // steps
    scale = [1.0 / c_ref[q, 0:1, 0:1] for q in range(po)]
    sent = []
    for i in range(steps):
        span = pl.ds(i * size, size)
        for q in range(po):
            work[q, span] = gram_ref[q, span] * scale[q]
        sent.append(pltpu.make_async_copy(work.at[:, span], gram_done.at[:, span], gsem.at[i]))
        sent[i].start()
    copy.wait()
    for one in sent:
        one.wait()


def finish(out, gram, count):
    steps = 6
    any_space = pl.BlockSpec(memory_space=pl.ANY)
    vmem = pl.BlockSpec(memory_space=pltpu.VMEM)
    dma = pltpu.SemaphoreType.DMA
    return pl.pallas_call(
        functools.partial(finish_kernel, steps),
        out_shape=(
            jax.ShapeDtypeStruct(out.shape, out.dtype),
            jax.ShapeDtypeStruct(gram.shape, gram.dtype),
        ),
        in_specs=[vmem, vmem, vmem],
        out_specs=(any_space, any_space),
        scratch_shapes=[pltpu.VMEM(gram.shape, gram.dtype), dma, dma((steps,))],
        compiler_params=pltpu.CompilerParams(vmem_limit_bytes=40 * 2**20),
    )(count, out, gram)


def fused(hidden, routes, gate_scores, down_weight):
    tokens, top, width = hidden.shape
    ne, nd = lax.axis_size("expert"), lax.axis_size("dp")
    po, _, cols = down_weight.shape
    pairs = tokens * top
    cap = 3 * pairs // (2 * ne * po)
    nz, group = ne // 2, nd * tokens
    pc = cols // PIECES
    bf, f32 = jnp.bfloat16, jnp.float32
    dma = pltpu.SemaphoreType.DMA
    any_space = pl.BlockSpec(memory_space=pl.ANY)
    vmem = pl.BlockSpec(memory_space=pltpu.VMEM)
    out, gram, count = pl.pallas_call(
        functools.partial(fused_kernel, nd, ne, top, cap, PIECES),
        out_shape=(
            pltpu.VMEM((tokens, nd * cols), bf),
            pltpu.VMEM((po, width // nd, width), f32),
            pltpu.VMEM((po, 8, 128), f32),
        ),
        in_specs=[any_space, vmem, vmem, any_space],
        out_specs=(vmem, vmem, vmem),
        scratch_shapes=[
            pltpu.VMEM((pairs, width), bf),
            pltpu.VMEM((po, ne * nd * cap, width), bf),
            pltpu.VMEM((ne * nd, 16, META), bf),
            pltpu.VMEM((ne * po, cap, width), bf),
            pltpu.VMEM((ne, 16, META), bf),
            pltpu.VMEM((nz - 1, po, cap, width), bf),
            pltpu.VMEM((nz - 1, 16, META), bf),
            pltpu.VMEM((8, pairs), jnp.int32),
            pltpu.VMEM((16, pairs), bf),
            pltpu.VMEM((po, width, cols), bf),
            pltpu.VMEM((nz, PIECES, group, pc), bf),
            pltpu.VMEM((nz, PIECES, group, pc), bf),
            pltpu.VMEM((nz, group, cols), f32),
            pltpu.VMEM((nz, PIECES, group, pc), bf),
            pltpu.VMEM((nz + 1, PIECES, group, pc), bf),
            pltpu.VMEM((PIECES, nd, tokens, pc), bf),
            dma, dma, dma, dma,
            dma((po, ne)), dma((ne,)), dma((po, nz - 1)), dma((nz - 1,)),
            dma((po, nz - 1)), dma((nz - 1,)), dma((po, nz - 1)), dma((nz - 1,)),
            dma((po, ne)), dma((ne,)), dma((2, po, ne)), dma((2, ne)),
            dma((po, ne * nd)), dma((ne * nd,)),
            dma((nz, PIECES)), dma((nz, PIECES)), dma((nz, PIECES)), dma((nz + 1, PIECES)),
            dma((PIECES, nd)), dma((PIECES, nd)),
        ],
        compiler_params=pltpu.CompilerParams(
            collective_id=0, has_side_effects=True, vmem_limit_bytes=VMEM_LIMIT
        ),
    )(
        hidden.reshape(pairs, width), routes.T, gate_scores.T, down_weight,
    )
    return finish(out, gram, count)


def earlier(onehot):
    pairs = jnp.arange(onehot.shape[0], dtype=jnp.int32)
    above = (pairs[None, :] < pairs[:, None]).astype(jnp.bfloat16)
    return jnp.dot(
        above, onehot.astype(jnp.bfloat16), preferred_element_type=jnp.float32
    ).astype(jnp.int32)


def plain(hidden, routes, gate_scores, down_weight):
    tokens = hidden.shape[0]
    top_count = hidden.shape[1]
    hidden_width = hidden.shape[2]
    n_owner = lax.axis_size("expert")
    n_group = lax.axis_size("dp")
    per_owner = down_weight.shape[0]
    experts = n_owner * per_owner
    pair_total = tokens * top_count
    capacity = 3 * tokens * top_count // (2 * experts)
    flat_routes = routes.reshape(pair_total)
    onehot = (flat_routes[:, None] == jnp.arange(experts, dtype=jnp.int32)[None, :]).astype(
        jnp.int32
    )
    before = earlier(onehot)
    position = jnp.sum(before * onehot, axis=1)
    slot_index = flat_routes * capacity + position
    local_counts = jnp.sum(onehot, axis=0).astype(jnp.float32)
    totals = lax.psum(local_counts, ("dp", "expert"))
    pair_rows = hidden.reshape(pair_total, hidden_width)
    outgoing = (
        jnp.zeros((experts * capacity, hidden_width), jnp.bfloat16).at[slot_index].set(pair_rows)
    )
    outgoing = outgoing.reshape(n_owner, per_owner, capacity, hidden_width)
    arrived = lax.all_to_all(outgoing, "expert", split_axis=0, concat_axis=0, tiled=True)
    everyone = lax.all_gather(arrived, "dp", axis=0, tiled=True)
    own_counts = lax.dynamic_slice_in_dim(
        totals, lax.axis_index("expert") * per_owner, per_owner, 0
    )
    block_width = hidden_width // n_group
    my_columns = lax.dynamic_slice_in_dim(
        everyone, lax.axis_index("dp") * block_width, block_width, 3
    )
    gram_rows = jnp.einsum(
        "sxcf,sxcg->xfg", my_columns, everyone, preferred_element_type=jnp.float32
    )
    results = jnp.einsum(
        "sxcf,xfd->sxcd", everyone, down_weight, preferred_element_type=jnp.float32
    ).astype(jnp.bfloat16)
    returned = lax.all_to_all(
        lax.all_to_all(results, "dp", split_axis=0, concat_axis=3, tiled=True),
        "expert",
        split_axis=0,
        concat_axis=0,
        tiled=True,
    )
    gram = gram_rows / own_counts[:, None, None]
    model_width = returned.shape[3]
    pair_results = returned.reshape(experts * capacity, model_width)[slot_index]
    scores = gate_scores.astype(jnp.float32)
    weight = scores / jnp.sum(scores, axis=1, keepdims=True)
    combined = jnp.sum(
        pair_results.reshape(tokens, top_count, model_width).astype(jnp.float32)
        * weight[:, :, None],
        axis=1,
    )
    return (combined.astype(jnp.bfloat16), gram)


def fits(hidden, down_weight, nd, ne):
    tokens, top, width = hidden.shape
    po, _, cols = down_weight.shape
    pairs = tokens * top
    cap = 3 * pairs // (2 * ne * po)
    nz, group = ne // 2, nd * tokens
    if nd != 4 or ne != 8 or cap % 16 or po * cap > META or tokens % 16 or tokens > 256:
        return False
    if top & (top - 1) or cols % (PIECES * 128) or width % 768 or po != 2 or (width // nd) % 384 or top != 8:
        return False
    need = (
        2 * po * ne * cap * (nd + 1) * width
        + 2 * po * width * cols
        + nz * group * cols * 12
        + 2 * group * cols * 2
        + 4 * po * (width // nd) * width
        + 6 * pairs * width
        + 8 * group * cols
    )
    return need <= VMEM_BUDGET


def local(hidden, routes, gate_scores, down_weight):
    if fits(hidden, down_weight, lax.axis_size("dp"), lax.axis_size("expert")):
        return fused(hidden, routes, gate_scores, down_weight)
    return plain(hidden, routes, gate_scores, down_weight)


def solution(mesh):
    placed = (
        P(("dp", "expert"), None, None),
        P(("dp", "expert"), None),
        P(("dp", "expert"), None),
        P("expert", None, "dp"),
    )
    return jax.shard_map(
        local,
        mesh=mesh,
        in_specs=placed,
        out_specs=(P(("dp", "expert"), None), P("expert", "dp", None)),
        check_vma=False,
    )
```

```python
import functools

import jax
import jax.numpy as jnp
from jax import lax
from jax.experimental import pallas as pl
from jax.experimental.pallas import tpu as pltpu
from jax.sharding import PartitionSpec as P

MESH = pl.DeviceIdType.MESH
META = 128
PIECES = 4
GATE = 2
SWAP = 4
AT = (4, 6, 5, 6)
SPLIT = (0, 0, 2, 4, 4, 4, 5, 6, 6)
VMEM_BUDGET = 46 * 2**20
VMEM_LIMIT = 52 * 2**20


def fused_kernel(
    nd, ne, top, cap, np_,
    hid_hbm, rt, gt, w_hbm, o_ref, g, c_ref,
    hid, buf, mbuf, og, mog, held, mheld, slot, meta, w, sendy, recvy, keep, sendz, recvz, fin,
    hsem, wsem, lsem, mlsem, asend, msend, fsend, mfsend, hsend, mhsend, hrecv, mhrecv, xsend, mxsend, csend, mcsend, recv, mrecv,
    ysend, yrecv, zsend, zrecv, osend, orecv,
):
    f32, bf = jnp.float32, jnp.bfloat16
    po, width, cols = w.shape
    pairs = hid.shape[0]
    tokens = pairs // top
    nz = ne // 2
    rows = nd * cap
    chunk = po * cap
    group = nd * tokens
    pc = cols // np_
    experts = ne * po
    d = lax.axis_index("dp")
    e = lax.axis_index("expert")
    x, c = lax.div(d, 2), lax.rem(d, 2)
    z, y = lax.div(e, 2), lax.rem(e, 2)
    other = d + 1 - 2 * c
    across = lax.rem(d + 2, nd)
    pair = e + 1 - 2 * y
    inner = jnp.logical_and(z > 0, z < nz - 1)
    outer = jnp.logical_not(inner)

    load_h = pltpu.make_async_copy(hid_hbm, hid, hsem)
    load_h.start()
    load_w = pltpu.make_async_copy(w_hbm, w, wsem)

    barrier = pltpu.get_barrier_semaphore()
    for k in range(1, nz):
        pl.semaphore_signal(
            barrier, inc=1, device_id=(d, lax.rem(e + 2 * k, ne)), device_id_type=MESH
        )
    pl.semaphore_signal(barrier, inc=1, device_id=(d, pair), device_id_type=MESH)
    for k in range(1, nd):
        pl.semaphore_signal(
            barrier, inc=1, device_id=(lax.rem(d + k, nd), e), device_id_type=MESH
        )

    def remote(src, dst, ss, rs, dd, ee):
        return pltpu.make_async_remote_copy(
            src_ref=src, dst_ref=dst, send_sem=ss, recv_sem=rs,
            device_id=(dd, ee), device_id_type=MESH,
        )

    def slot_of(dd, ee):
        return buf.at[:, pl.ds(pl.multiple_of((ee * nd + dd) * cap, cap), cap), :]

    def part_of(q, dd, ee):
        return buf.at[q, pl.ds(pl.multiple_of((ee * nd + dd) * cap, cap), cap), :]

    def meta_of(dd, ee):
        return mbuf.at[ee * nd + dd]

    shift = top.bit_length() - 1
    told = jnp.concatenate([rt[...], gt[...]], axis=0).astype(f32).astype(bf)
    spread = jnp.dot(
        told,
        jnp.where(
            lax.broadcasted_iota(jnp.int32, (tokens, pairs), 0)
            == jnp.right_shift(lax.broadcasted_iota(jnp.int32, (tokens, pairs), 1), shift),
            1.0, 0.0,
        ).astype(bf),
        preferred_element_type=f32,
    )
    choice = lax.broadcasted_iota(jnp.int32, (top, pairs), 0) == jnp.bitwise_and(
        lax.broadcasted_iota(jnp.int32, (top, pairs), 1), top - 1
    )
    route = jnp.sum(jnp.where(choice, spread[:top], 0.0), axis=0, keepdims=True).astype(jnp.int32)
    score = jnp.sum(jnp.where(choice, spread[top:], 0.0), axis=0, keepdims=True)
    weight = score / jnp.sum(spread[top:], axis=0, keepdims=True)
    high = weight.astype(bf).astype(f32)
    set_ = jnp.where(
        lax.broadcasted_iota(jnp.int32, (experts, pairs), 0) == route, 1.0, 0.0
    )
    before = jnp.dot(
        set_.astype(bf),
        jnp.where(
            lax.broadcasted_iota(jnp.int32, (pairs, pairs), 0)
            < lax.broadcasted_iota(jnp.int32, (pairs, pairs), 1),
            1.0, 0.0,
        ).astype(bf),
        preferred_element_type=f32,
    )
    position = jnp.sum(before * set_, axis=0, keepdims=True).astype(jnp.int32)
    slot[...] = jnp.broadcast_to(route * cap + position, slot.shape)
    kind = lax.broadcasted_iota(jnp.int32, (16, pairs), 0)
    token = jnp.right_shift(lax.broadcasted_iota(jnp.int32, (16, pairs), 1), shift)
    meta[...] = jnp.where(
        kind == 0, token.astype(f32),
        jnp.where(kind == 1, high, jnp.where(kind == 2, weight - high, jnp.where(kind == 3, 1.0, 0.0))),
    ).astype(bf)
    load_h.wait()
    load_w.start()

    def pack(zt):
        first = zt * 2 * chunk
        pick = jnp.where(
            lax.broadcasted_iota(jnp.int32, (2 * chunk, pairs), 0) + first == slot[0:1], 1.0, 0.0
        ).astype(bf)
        block = jnp.dot(pick, hid[...], preferred_element_type=f32).astype(bf)
        og[pl.ds(zt * 2 * po, 2 * po)] = block.reshape(2 * po, cap, width)
        for k in range(2):
            pick = jnp.where(
                lax.broadcasted_iota(jnp.int32, (META, pairs), 0) + (first + k * chunk)
                == slot[0:1],
                1.0, 0.0,
            ).astype(bf)
            mog[zt * 2 + k] = lax.dot_general(
                meta[...], pick, (((1,), (1,)), ((), ())), preferred_element_type=f32
            ).astype(bf)

    whole = tuple(range(po + 1))

    def legs(rows_from, meta_from, rows_sem, meta_sem, dd, ee, to_d, to_e, which=whole):
        at = ee * nd + dd
        return tuple(
            remote(rows_from(q), part_of(q, dd, ee), rows_sem(q), recv.at[q, at], to_d, to_e)
            if q < po
            else remote(meta_from, meta_of(dd, ee), meta_sem, mrecv.at[at], to_d, to_e)
            for q in which
        )

    def first_leg(there):
        return legs(
            lambda q: og.at[there * po + q], mog.at[there],
            lambda q: asend.at[q, there], msend.at[there], d, e, d, there,
        )

    def to_x(ee, which=whole):
        return legs(
            lambda q: part_of(q, d, ee), meta_of(d, ee),
            lambda q: xsend.at[q, ee], mxsend.at[ee], d, ee, across, e, which,
        )

    def to_core(j, ee, which=whole):
        dd = d if j == 0 else across
        return legs(
            lambda q: part_of(q, dd, ee), meta_of(dd, ee),
            lambda q: csend.at[j, q, ee], mcsend.at[j, ee], dd, ee, other, e, which,
        )

    def start(copies):
        for copy in copies:
            copy.start()

    def came(q, dd, ee):
        here = part_of(q, dd, ee)
        remote(here, here, asend.at[0, 0], recv.at[q, ee * nd + dd], d, e).wait_recv()

    def meta_came(dd, ee):
        there = meta_of(dd, ee)
        remote(there, there, msend.at[0], mrecv.at[ee * nd + dd], d, e).wait_recv()

    def arrived(dd, ee):
        for q in range(po):
            came(q, dd, ee)
        meta_came(dd, ee)

    def near(k):
        start(first_leg(target[k] * 2 + y))

    def across_y(k):
        there = target[k] * 2 + 1 - y
        return (
            *(
                remote(og.at[there * po + q], held.at[k, q], fsend.at[q, k], hrecv.at[q, k], d, pair)
                for q in range(po)
            ),
            remote(mog.at[there], mheld.at[k], mfsend.at[k], mhrecv.at[k], d, pair),
        )

    def far(k):
        start(across_y(k))

    def second_leg(k, which=whole):
        return legs(
            lambda q: held.at[k, q], mheld.at[k],
            lambda q: hsend.at[q, k], mhsend.at[k], d, pair, d, target[k] * 2 + y, which,
        )

    def relay(k):
        for q in range(po):
            here = held.at[k, q]
            remote(here, here, fsend.at[q, k], hrecv.at[q, k], d, e).wait_recv()
            start(second_leg(k, (q,)))
        remote(mheld.at[k], mheld.at[k], mhsend.at[k], mhrecv.at[k], d, e).wait_recv()
        start(second_leg(k, (po,)))

    target = ((nz - 1) * (1 - lax.rem(z, 2)), lax.rem(z + 2, nz), 1 + lax.rem(z, 2))

    def source(s):
        return jnp.where(
            s == 0, z,
            jnp.where(
                s == 1, (nz - 1) * (1 - lax.div(z, 2)),
                jnp.where(s == 2, z + 1 - 2 * lax.rem(z, 2), 2 - lax.div(z, 2)),
            ),
        )

    pack(target[0])
    pl.semaphore_wait(barrier, nz + nd - 1)
    far(0)

    @pl.when(outer)
    def _():
        near(0)

    pack(z)
    own = pltpu.make_async_copy(og.at[pl.ds(e * po, po)], slot_of(d, e), lsem)
    own_meta = pltpu.make_async_copy(mog.at[e], meta_of(d, e), mlsem)
    own.start()
    own_meta.start()
    start(first_leg(pair))
    own.wait()
    own_meta.wait()
    start(to_x(e))
    start(to_core(0, e))
    pack(target[1])
    far(1)
    pack(target[2])
    far(2)

    @pl.when(outer)
    def _():
        relay(0)
        near(1)

    load_w.wait()

    def to_pair(zi, p):
        return remote(
            sendy.at[zi, p], recvy.at[zi, p], ysend.at[zi, p], yrecv.at[zi, p], d, pair
        )

    def from_pair(zi, p):
        remote(
            sendy.at[zi, p], recvy.at[zi, p], ysend.at[zi, p], yrecv.at[zi, p], d, e
        ).wait_recv()

    def partial_sums(ee):
        span = pl.ds(pl.multiple_of(ee * rows, rows), rows)
        told = [mbuf[ee * nd + k].astype(f32).T for k in range(nd)]
        row = lax.broadcasted_iota(jnp.int32, (rows, 1), 0)
        base = jnp.zeros((rows, 1), jnp.int32)
        for k in range(1, nd):
            base = base + jnp.where(row >= k * cap, tokens, 0)
        col = lax.broadcasted_iota(jnp.int32, (rows, group), 1)
        acc = jnp.zeros((group, cols), f32)
        for q in range(po):
            mine = jnp.concatenate([m[q * cap:(q + 1) * cap] for m in told], axis=0)
            hit = col == mine[:, 0:1].astype(jnp.int32) + base
            h = jnp.dot(buf[q, span, :], w[q], preferred_element_type=f32).astype(bf)
            share = jnp.concatenate(
                [jnp.where(hit, mine[:, k:k + 1], 0.0).astype(bf) for k in (1, 2)], axis=1
            )
            both = lax.dot_general(
                share, h, (((0,), (0,)), ((), ())), preferred_element_type=f32
            )
            acc = acc + (both[:group] + both[group:])
        return acc

    def add_on(s, pieces):
        zs = source(s)
        up = zs > z
        follow = jnp.where(up, z + 1, z - 1)
        place = jnp.where(jnp.logical_and(jnp.logical_not(up), follow == zs), nz, zs)
        beyond = jnp.where(up, z > 0, z < nz - 1)
        for p in pieces:
            cs = pl.ds(p * pc, pc)
            from_pair(zs, p)

            @pl.when(beyond)
            def _():
                remote(
                    sendz.at[zs, p], recvz.at[zs, p], zsend.at[zs, p], zrecv.at[zs, p], d, e
                ).wait_recv()
                sendz[zs, p] = (
                    keep[zs, :, cs] + recvy[zs, p].astype(f32) + recvz[zs, p].astype(f32)
                ).astype(bf)

            @pl.when(jnp.logical_not(beyond))
            def _():
                sendz[zs, p] = (keep[zs, :, cs] + recvy[zs, p].astype(f32)).astype(bf)

            remote(
                sendz.at[zs, p], recvz.at[place, p], zsend.at[zs, p], zrecv.at[place, p],
                d, follow * 2 + y,
            ).start()

    every = tuple(range(np_))

    def owner(n):
        turn = jnp.where(inner, n, jnp.where(n == 0, 0, jnp.where(n == ne - 1, 1, n + 1)))
        ys = jnp.where(
            turn == 0, y, jnp.where(
                turn == 1, 1 - y, jnp.where(
                    lax.rem(turn + jnp.where(turn < SWAP, 1, 0), 2) == 0, 1 - y, y
                ),
            ),
        )
        return source(lax.div(turn, 2)), ys

    def took(part, ee):
        for q in whole[:1] if part == 0 else whole[1:]:
            if q < po:
                came(q, d, ee)
            else:
                meta_came(d, ee)
            start(to_x(ee, (q,)))
            start(to_core(0, ee, (q,)))

    def step(n, carry):
        @pl.when(n < ne)
        def _():
            zs, ys = owner(n)
            took(0, zs * 2 + ys)

        @pl.when(jnp.logical_and(inner, n == 1))
        def _():
            relay(0)
            near(0)

        @pl.when(jnp.logical_and(inner, n == 4))
        def _():
            relay(2)
            near(2)

        @pl.when(jnp.logical_and(outer, n == 3))
        def _():
            relay(1)

        @pl.when(jnp.logical_and(outer, n == 4))
        def _():
            relay(2)
            near(2)

        zs, ys = owner(n - 1)
        ee = zs * 2 + ys
        arrived(across, ee)
        start(to_core(1, ee))

        @pl.when(n < ne)
        def _():
            zn, yn = owner(n)
            took(1, zn * 2 + yn)

        arrived(other, ee)
        arrived(other + across - d, ee)
        acc = partial_sums(ee)

        @pl.when(ys == y)
        def _():
            keep[zs] = acc

        @pl.when(ys != y)
        def _():
            for p in range(np_):
                sendy[zs, p] = acc[:, p * pc:(p + 1) * pc].astype(bf)
                to_pair(zs, p).start()

        @pl.when(jnp.logical_and(inner, n == GATE))
        def _():
            relay(1)
            near(1)

        done = n - 1

        @pl.when(jnp.logical_and(outer, done == AT[0]))
        def _():
            add_on(1, every)

        @pl.when(jnp.logical_and(outer, done == AT[1]))
        def _():
            add_on(2, every)

        @pl.when(jnp.logical_and(inner, done == AT[2]))
        def _():
            add_on(1, every[:3 * np_ // 4])

        @pl.when(jnp.logical_and(inner, done == AT[3]))
        def _():
            add_on(1, every[3 * np_ // 4:])

        return carry

    lax.fori_loop(1, ne + 1, step, 0)

    block = width // nd
    wide = width // 3

    def gram_tiles(low, high):
        @pl.loop(low, high)
        def _(i):
            q = lax.div(i, 3)
            cs = pl.ds(pl.multiple_of(lax.rem(i, 3) * wide, wide), wide)
            g[q, :, cs] = lax.dot_general(
                buf[q, :, pl.ds(pl.multiple_of(d * block, block), block)],
                buf[q, :, cs],
                (((0,), (0,)), ((), ())),
                preferred_element_type=f32,
            )

    @pl.when(outer)
    def _():
        add_on(3, every)

    @pl.when(inner)
    def _():
        add_on(2, every)

    for p in range(np_):
        @pl.when(inner)
        def _():
            add_on(3, (p,))

        gram_tiles(SPLIT[p], SPLIT[p + 1])

    def drain(k, carry):
        for copies in (to_x(k), to_core(0, k), to_core(1, k)):
            for copy in copies:
                copy.wait_send()
        return carry

    lax.fori_loop(0, ne, drain, 0)

    for copy in first_leg(pair):
        copy.wait_send()
    for k in range(nz - 1):
        for copies in (first_leg(target[k] * 2 + y), across_y(k), second_leg(k)):
            for copy in copies:
                copy.wait_send()
    told = jnp.sum(mbuf[...].astype(f32), axis=0)[3:4]
    lane = lax.broadcasted_iota(jnp.int32, (1, META), 1)
    for q in range(po):
        here = jnp.logical_and(lane >= q * cap, lane < (q + 1) * cap)
        c_ref[q] = jnp.broadcast_to(
            jnp.sum(jnp.where(here, told, 0.0), axis=1, keepdims=True), c_ref.shape[1:]
        )

    def to_token(p, k):
        dd = lax.rem(d + (2, 3, 1)[k - 1], nd)
        return remote(
            fin.at[p, dd], o_ref.at[:, pl.ds(pl.multiple_of(d * cols + p * pc, pc), pc)],
            osend.at[p, k], orecv.at[p, d], dd, e,
        )

    for p in range(np_):
        gram_tiles(SPLIT[np_ + p], SPLIT[np_ + p + 1])
        cs = pl.ds(p * pc, pc)
        from_pair(z, p)
        keep[z, :, cs] = keep[z, :, cs] + recvy[z, p].astype(f32)
        for there, place in ((z > 0, z), (z < nz - 1, nz)):
            @pl.when(there)
            def _():
                remote(
                    sendz.at[0, p], recvz.at[place, p], zsend.at[0, p], zrecv.at[place, p], d, e
                ).wait_recv()
                keep[z, :, cs] = keep[z, :, cs] + recvz[place, p].astype(f32)
        fin[p] = keep[z, :, cs].astype(bf).reshape(nd, tokens, pc)
        for k in range(1, nd):
            to_token(p, k).start()
        o_ref[:, pl.ds(pl.multiple_of(d * cols + p * pc, pc), pc)] = fin[p, d]

    for p in range(np_):
        for k in range(1, nd):
            dd = lax.rem(d + (2, 3, 1)[k - 1], nd)
            remote(
                fin.at[p, dd], o_ref.at[:, pl.ds(pl.multiple_of(dd * cols + p * pc, pc), pc)],
                osend.at[p, k], orecv.at[p, dd], d, e,
            ).wait_recv()

    def drain_z(k, carry):
        for p in range(np_):
            to_pair(k, p).wait_send()

            @pl.when(k != z)
            def _():
                remote(
                    sendz.at[k, p], recvz.at[k, p], zsend.at[k, p], zrecv.at[k, p], d, e
                ).wait_send()

        return carry

    lax.fori_loop(0, nz, drain_z, 0)
    for p in range(np_):
        for k in range(1, nd):
            to_token(p, k).wait_send()


def finish_kernel(steps, c_ref, out_ref, gram_ref, out_done, gram_done, work, osem, gsem):
    copy = pltpu.make_async_copy(out_ref, out_done, osem)
    copy.start()
    po, block, _ = gram_ref.shape
    size = block // steps
    scale = [1.0 / c_ref[q, 0:1, 0:1] for q in range(po)]
    sent = []
    for i in range(steps):
        span = pl.ds(i * size, size)
        for q in range(po):
            work[q, span] = gram_ref[q, span] * scale[q]
        sent.append(pltpu.make_async_copy(work.at[:, span], gram_done.at[:, span], gsem.at[i]))
        sent[i].start()
    copy.wait()
    for one in sent:
        one.wait()


def finish(out, gram, count):
    steps = 6
    any_space = pl.BlockSpec(memory_space=pl.ANY)
    vmem = pl.BlockSpec(memory_space=pltpu.VMEM)
    dma = pltpu.SemaphoreType.DMA
    return pl.pallas_call(
        functools.partial(finish_kernel, steps),
        out_shape=(
            jax.ShapeDtypeStruct(out.shape, out.dtype),
            jax.ShapeDtypeStruct(gram.shape, gram.dtype),
        ),
        in_specs=[vmem, vmem, vmem],
        out_specs=(any_space, any_space),
        scratch_shapes=[pltpu.VMEM(gram.shape, gram.dtype), dma, dma((steps,))],
        compiler_params=pltpu.CompilerParams(vmem_limit_bytes=40 * 2**20),
    )(count, out, gram)


def fused(hidden, routes, gate_scores, down_weight):
    tokens, top, width = hidden.shape
    ne, nd = lax.axis_size("expert"), lax.axis_size("dp")
    po, _, cols = down_weight.shape
    pairs = tokens * top
    cap = 3 * pairs // (2 * ne * po)
    nz, group = ne // 2, nd * tokens
    pc = cols // PIECES
    bf, f32 = jnp.bfloat16, jnp.float32
    dma = pltpu.SemaphoreType.DMA
    any_space = pl.BlockSpec(memory_space=pl.ANY)
    vmem = pl.BlockSpec(memory_space=pltpu.VMEM)
    out, gram, count = pl.pallas_call(
        functools.partial(fused_kernel, nd, ne, top, cap, PIECES),
        out_shape=(
            pltpu.VMEM((tokens, nd * cols), bf),
            pltpu.VMEM((po, width // nd, width), f32),
            pltpu.VMEM((po, 8, 128), f32),
        ),
        in_specs=[any_space, vmem, vmem, any_space],
        out_specs=(vmem, vmem, vmem),
        scratch_shapes=[
            pltpu.VMEM((pairs, width), bf),
            pltpu.VMEM((po, ne * nd * cap, width), bf),
            pltpu.VMEM((ne * nd, 16, META), bf),
            pltpu.VMEM((ne * po, cap, width), bf),
            pltpu.VMEM((ne, 16, META), bf),
            pltpu.VMEM((nz - 1, po, cap, width), bf),
            pltpu.VMEM((nz - 1, 16, META), bf),
            pltpu.VMEM((8, pairs), jnp.int32),
            pltpu.VMEM((16, pairs), bf),
            pltpu.VMEM((po, width, cols), bf),
            pltpu.VMEM((nz, PIECES, group, pc), bf),
            pltpu.VMEM((nz, PIECES, group, pc), bf),
            pltpu.VMEM((nz, group, cols), f32),
            pltpu.VMEM((nz, PIECES, group, pc), bf),
            pltpu.VMEM((nz + 1, PIECES, group, pc), bf),
            pltpu.VMEM((PIECES, nd, tokens, pc), bf),
            dma, dma, dma, dma,
            dma((po, ne)), dma((ne,)), dma((po, nz - 1)), dma((nz - 1,)),
            dma((po, nz - 1)), dma((nz - 1,)), dma((po, nz - 1)), dma((nz - 1,)),
            dma((po, ne)), dma((ne,)), dma((2, po, ne)), dma((2, ne)),
            dma((po, ne * nd)), dma((ne * nd,)),
            dma((nz, PIECES)), dma((nz, PIECES)), dma((nz, PIECES)), dma((nz + 1, PIECES)),
            dma((PIECES, nd)), dma((PIECES, nd)),
        ],
        compiler_params=pltpu.CompilerParams(
            collective_id=0, has_side_effects=True, vmem_limit_bytes=VMEM_LIMIT
        ),
    )(
        hidden.reshape(pairs, width), routes.T, gate_scores.T, down_weight,
    )
    return finish(out, gram, count)


def earlier(onehot):
    pairs = jnp.arange(onehot.shape[0], dtype=jnp.int32)
    above = (pairs[None, :] < pairs[:, None]).astype(jnp.bfloat16)
    return jnp.dot(
        above, onehot.astype(jnp.bfloat16), preferred_element_type=jnp.float32
    ).astype(jnp.int32)


def plain(hidden, routes, gate_scores, down_weight):
    tokens = hidden.shape[0]
    top_count = hidden.shape[1]
    hidden_width = hidden.shape[2]
    n_owner = lax.axis_size("expert")
    n_group = lax.axis_size("dp")
    per_owner = down_weight.shape[0]
    experts = n_owner * per_owner
    pair_total = tokens * top_count
    capacity = 3 * tokens * top_count // (2 * experts)
    flat_routes = routes.reshape(pair_total)
    onehot = (flat_routes[:, None] == jnp.arange(experts, dtype=jnp.int32)[None, :]).astype(
        jnp.int32
    )
    before = earlier(onehot)
    position = jnp.sum(before * onehot, axis=1)
    slot_index = flat_routes * capacity + position
    local_counts = jnp.sum(onehot, axis=0).astype(jnp.float32)
    totals = lax.psum(local_counts, ("dp", "expert"))
    pair_rows = hidden.reshape(pair_total, hidden_width)
    outgoing = (
        jnp.zeros((experts * capacity, hidden_width), jnp.bfloat16).at[slot_index].set(pair_rows)
    )
    outgoing = outgoing.reshape(n_owner, per_owner, capacity, hidden_width)
    arrived = lax.all_to_all(outgoing, "expert", split_axis=0, concat_axis=0, tiled=True)
    everyone = lax.all_gather(arrived, "dp", axis=0, tiled=True)
    own_counts = lax.dynamic_slice_in_dim(
        totals, lax.axis_index("expert") * per_owner, per_owner, 0
    )
    block_width = hidden_width // n_group
    my_columns = lax.dynamic_slice_in_dim(
        everyone, lax.axis_index("dp") * block_width, block_width, 3
    )
    gram_rows = jnp.einsum(
        "sxcf,sxcg->xfg", my_columns, everyone, preferred_element_type=jnp.float32
    )
    results = jnp.einsum(
        "sxcf,xfd->sxcd", everyone, down_weight, preferred_element_type=jnp.float32
    ).astype(jnp.bfloat16)
    returned = lax.all_to_all(
        lax.all_to_all(results, "dp", split_axis=0, concat_axis=3, tiled=True),
        "expert",
        split_axis=0,
        concat_axis=0,
        tiled=True,
    )
    gram = gram_rows / own_counts[:, None, None]
    model_width = returned.shape[3]
    pair_results = returned.reshape(experts * capacity, model_width)[slot_index]
    scores = gate_scores.astype(jnp.float32)
    weight = scores / jnp.sum(scores, axis=1, keepdims=True)
    combined = jnp.sum(
        pair_results.reshape(tokens, top_count, model_width).astype(jnp.float32)
        * weight[:, :, None],
        axis=1,
    )
    return (combined.astype(jnp.bfloat16), gram)


def fits(hidden, down_weight, nd, ne):
    tokens, top, width = hidden.shape
    po, _, cols = down_weight.shape
    pairs = tokens * top
    cap = 3 * pairs // (2 * ne * po)
    nz, group = ne // 2, nd * tokens
    if nd != 4 or ne != 8 or cap % 16 or po * cap > META or tokens % 16 or tokens > 256:
        return False
    if top & (top - 1) or cols % (PIECES * 128) or width % 768 or po != 2 or (width // nd) % 384 or top != 8:
        return False
    need = (
        2 * po * ne * cap * (nd + 1) * width
        + 2 * po * width * cols
        + nz * group * cols * 12
        + 2 * group * cols * 2
        + 4 * po * (width // nd) * width
        + 6 * pairs * width
        + 8 * group * cols
    )
    return need <= VMEM_BUDGET


def local(hidden, routes, gate_scores, down_weight):
    if fits(hidden, down_weight, lax.axis_size("dp"), lax.axis_size("expert")):
        return fused(hidden, routes, gate_scores, down_weight)
    return plain(hidden, routes, gate_scores, down_weight)


def solution(mesh):
    placed = (
        P(("dp", "expert"), None, None),
        P(("dp", "expert"), None),
        P(("dp", "expert"), None),
        P("expert", None, "dp"),
    )
    return jax.shard_map(
        local,
        mesh=mesh,
        in_specs=placed,
        out_specs=(P(("dp", "expert"), None), P("expert", "dp", None)),
        check_vma=False,
    )
```
